32 devices in a mesh: wide: 4 (over y, x), narrow: 8 (over z, core).
Axes of the slice: x: 2, y: 2, z: 4, core: 2. Of those that a mesh axis runs over, the one named last changes fastest.
Arguments:
- images: bfloat16 [64, 256, 1024], P('wide', 'narrow'), may hold values from -6 to 6
- cotangent: bfloat16 [64, 256, 1024], P('wide', 'narrow'), may hold values from -12 to 12
- test_images: bfloat16 [4, 256, 1024], P('wide', 'narrow'), may hold values from -6 to 6
- test_cotangent: bfloat16 [4, 256, 1024], P('wide', 'narrow'), may hold values from -6 to 6
- pair_index: int32 [32, 2], P('wide'), may hold values from 0 to 63, as said below
- example_count: int32 [4], P('wide'), may hold values from 1 to 16, as said below
- aug_count: int32 [64], P('wide'), may hold values from 8 to 16, as said below
- conv_weight: float32 [2, 3, 3, 256, 256], P(None, None, None, None, 'narrow'), may hold values from -0.125 to 0.125
- gn_params: float32 [4, 256], P(None, 'narrow'), may hold values from -0.5 to 1.4, as said below
- conv_moment1: float32 [2, 3, 3, 256, 256], P(None, None, None, None, 'narrow'), may hold values from -2.5 to 2.5
- conv_moment2: float32 [2, 3, 3, 256, 256], P(None, None, None, None, 'narrow'), may hold values from 0.0265625 to 0.10625
- gn_moment1: float32 [4, 256], P(None, 'narrow'), may hold values from -3.5 to 3.5
- gn_moment2: float32 [4, 256], P(None, 'narrow'), may hold values from 0.05625 to 0.225
- noise_conv: float32 [2, 3, 3, 256, 256], P(None, None, None, None, 'narrow'), may hold values from -6 to 6
- noise_gn: float32 [4, 256], P(None, 'narrow'), may hold values from -6 to 6
- step_count: int32 [1], replicated, may hold values from 2 to 20
Outputs:
- block_out: bfloat16 [64, 256, 1024], P('wide', 'narrow')
- input_grad: float32 [64, 256, 1024], P('wide', 'narrow')
- example_norm: float32 [64], P('wide')
- influence: float32 [64], P('wide')
- conv_new: float32 [2, 3, 3, 256, 256], P(None, None, None, None, 'narrow')
- conv_low: bfloat16 [2, 3, 3, 256, 256], P(None, None, None, None, 'narrow')
- conv_first: float32 [2, 3, 3, 256, 256], P(None, None, None, None, 'narrow')
- conv_second: float32 [2, 3, 3, 256, 256], P(None, None, None, None, 'narrow')
- gn_new: float32 [4, 256], P(None, 'narrow')
- gn_first: float32 [4, 256], P(None, 'narrow')
- gn_second: float32 [4, 256], P(None, 'narrow')
The draws below stay inside these ranges and needn't reach their ends.
Inputs may be any that keep to these rules, and one draw needn't show every extreme that they name: `pair_index`: pair p uses two different test images of the block of 16 test images 16 * (p div (8)) and on; every test image is in exactly one pair. `example_count`: some index of wide has all 16 examples live and some has one. `aug_count`: some example has all 16 augmentations live and some has 8. `gn_params`: rows 0 and 2 are gains, rows 1 and 3 biases.
All inputs are finite; a program needn't handle non-finite values.
Results may differ from the reference program's by a relative error of at most 0.0068.
Values may be sent and summed in bfloat16 or wider, within the bound.
A program may use at most 320 MiB of HBM per device.

```python
import math
import jax
import jax.numpy as jnp
from jax import lax

C = 256
MAP = 8
GROUPS = 16
AUG = 16
EX_DEV = 16
EXAMPLES = 64
TESTS = 64
PAIRS = 32
PARAMS = 1180672
N_WIDE = 4


def draw_cotangent(key, part):
    scale_key, value_key = jax.random.split(key)
    scales = jnp.exp(jax.random.uniform(scale_key, (EXAMPLES, 1, 1), jnp.float32, math.log(0.3), math.log(3.0)))
    values = jnp.clip(jax.random.normal(value_key, (EXAMPLES, C, AUG * MAP * MAP), jnp.float32), -4.0, 4.0)
    return (values * scales).astype(jnp.bfloat16)


def draw_pair_index(key, part):
    blocks = jnp.arange(N_WIDE, dtype=jnp.int32)

    def shuffle(block_id):
        order = jax.random.permutation(jax.random.fold_in(key, block_id), AUG).astype(jnp.int32)
        return order.reshape(AUG // 2, 2) + block_id * AUG
    return jax.vmap(shuffle)(blocks).reshape(PAIRS, 2)


def draw_example_count(key, part):
    first_key, second_key = jax.random.split(key)
    counts = jax.random.randint(first_key, (N_WIDE,), 1, EX_DEV + 1, dtype=jnp.int32)
    order = jax.random.permutation(second_key, N_WIDE)
    counts = counts.at[order[0]].set(EX_DEV)
    counts = counts.at[order[1]].set(1)
    return counts


def draw_aug_count(key, part):
    first_key, second_key = jax.random.split(key)
    counts = jax.random.randint(first_key, (EXAMPLES,), AUG // 2, AUG + 1, dtype=jnp.int32)
    order = jax.random.permutation(second_key, EXAMPLES)
    counts = counts.at[order[0]].set(AUG)
    counts = counts.at[order[1]].set(AUG // 2)
    return counts


def draw_gn_params(key, part):
    gain_key, bias_key = jax.random.split(key)
    gains = jax.random.uniform(gain_key, (2, C), jnp.float32, 0.6, 1.4)
    biases = jax.random.uniform(bias_key, (2, C), jnp.float32, -0.5, 0.5)
    return jnp.stack([gains[0], biases[0], gains[1], biases[1]], 0)


def levels(own_key, extent, cuts, low, high):
    factor_of = 1.0
    for position, shards_of in cuts:
        draws = jax.random.uniform(jax.random.fold_in(jax.random.fold_in(own_key, 6), position), (shards_of,), jnp.float32, low / len(cuts), high / len(cuts))
        factor_of = factor_of * jnp.repeat(jnp.exp(draws), extent[position] // shards_of).reshape((-1,) + (1,) * (len(extent) - 1 - position))
    return factor_of


def noise(stream_key, extent, scale, limit, cuts=(), held_as=jnp.bfloat16):
    drawn = jax.random.normal(stream_key, extent, jnp.float32) * scale
    if len(cuts) > 0:
        drawn = levels(stream_key, extent, cuts, -0.22, 0.18) * drawn
    return jnp.clip(drawn, min=-limit, max=limit).astype(held_as)


def setup_inputs(seed: int = 0) -> dict:
    keys = jax.random.split(jax.random.key(seed), 17)
    return {
        "images": noise(keys[0], (EXAMPLES, C, AUG * MAP * MAP), 1.0, 6.0, ((0, 4), (1, 8))),
        "cotangent": draw_cotangent(jax.random.fold_in(keys[16], 71), 0),
        "test_images": noise(keys[2], (TESTS // AUG, C, AUG * MAP * MAP), 1.0, 6.0, ((0, 4), (1, 8))),
        "test_cotangent": noise(keys[3], (TESTS // AUG, C, AUG * MAP * MAP), 1.0, 6.0, ((0, 4), (1, 8))),
        "pair_index": draw_pair_index(jax.random.fold_in(keys[16], 71), 0),
        "example_count": draw_example_count(jax.random.fold_in(keys[16], 71), 0),
        "aug_count": draw_aug_count(jax.random.fold_in(keys[16], 71), 0),
        "conv_weight": noise(keys[7], (2, 3, 3, C, C), (9 * C) ** -0.5, 0.125, ((4, 8),), jnp.float32),
        "gn_params": draw_gn_params(jax.random.fold_in(keys[16], 71), 0),
        "conv_moment1": noise(keys[9], (2, 3, 3, C, C), (1.3 / (EX_DEV * N_WIDE) ** 0.5), 2.5, ((4, 8),), jnp.float32),
        "conv_moment2": jnp.clip(jnp.exp(math.log(0.10625) - 1.3862944 * jax.random.uniform(keys[10], (2, 3, 3, C, C), jnp.float32) ** levels(keys[10], (2, 3, 3, C, C), ((4, 8),), -0.2, 0.2)), 0.0265625, 0.10625),
        "gn_moment1": noise(keys[11], (4, C), (1.9 / (EX_DEV * N_WIDE) ** 0.5), 3.5, ((1, 8),), jnp.float32),
        "gn_moment2": jnp.clip(jnp.exp(math.log(0.225) - 1.3862944 * jax.random.uniform(keys[12], (4, C), jnp.float32) ** levels(keys[12], (4, C), ((1, 8),), -0.2, 0.2)), 0.05625, 0.225),
        "noise_conv": noise(keys[13], (2, 3, 3, C, C), 1.0, 6.0, ((4, 8),), jnp.float32),
        "noise_gn": noise(keys[14], (4, C), 1.0, 6.0, ((1, 8),), jnp.float32),
        "step_count": jax.random.randint(keys[15], (1,), 2, 21).astype(jnp.int32),
    }


@jax.custom_vjp
def low(v):
    return lax.optimization_barrier(v.astype(jnp.bfloat16)).astype(jnp.float32)

@jax.custom_vjp
def low_back(v):
    return v

def low_keep(v):
    return (low(v), None)

def low_pass(kept, grad):
    return (grad,)

def back_keep(v):
    return (v, None)

def back_low(kept, grad):
    return (low(grad),)
low.defvjp(low_keep, low_pass)
low_back.defvjp(back_keep, back_low)
precise = lax.Precision.HIGHEST

def standardize(weight):
    fan_in = weight.shape[-4] * weight.shape[-3] * weight.shape[-2]
    centre = weight - lax.optimization_barrier(jnp.mean(weight, axis=(-4, -3, -2), keepdims=True))
    spread = lax.optimization_barrier(jnp.mean(centre * centre, axis=(-4, -3, -2), keepdims=True))
    return centre * lax.rsqrt(fan_in * spread + 1e-06)

def norm_act(values, gains, biases, group_size):
    count, height, width, chans = values.shape
    grouped = values.reshape(count, height * width, chans // group_size, group_size)
    centre = grouped - lax.optimization_barrier(jnp.mean(grouped, axis=(1, 3), keepdims=True))
    spread = lax.optimization_barrier(jnp.mean(centre * centre, axis=(1, 3), keepdims=True))
    normed = (centre * lax.rsqrt(spread + 1e-05)).reshape(values.shape)
    scaled = normed * gains[:, None, None, :] + biases[:, None, None, :]
    return scaled * jax.nn.sigmoid(scaled)

def convolve(inputs, kernel):
    return lax.conv_general_dilated(inputs, kernel, (1, 1), 'SAME', dimension_numbers=('NHWC', 'HWIO', 'NHWC'), precision=precise)

def block(pictures, conv_pair, gn_rows, group_size):
    hidden = low(norm_act(pictures, gn_rows[0][None], gn_rows[1][None], group_size))
    middle = low_back(convolve(hidden, low(standardize(conv_pair[0]))))
    second = low(norm_act(middle, gn_rows[2][None], gn_rows[3][None], group_size))
    branch = low_back(convolve(second, low(standardize(conv_pair[1]))))
    return pictures + branch

def adamw(weight, first, second, grad, correction, rate, decay):
    first_new = 0.5 * first + 0.5 * grad
    second_new = 0.5 * second + 0.5 * grad * grad
    update = first_new / correction / (jnp.sqrt(second_new / correction) + 1e-08)
    return (weight - rate * (update + decay * weight), first_new, second_new)

def to_pixels(values):
    lead = values.shape[0]
    return values.reshape(lead, C, AUG, MAP, MAP).transpose(0, 2, 3, 4, 1)

def from_pixels(values):
    lead = values.shape[0]
    return values.transpose(0, 4, 1, 2, 3).reshape(lead, C, AUG * MAP * MAP)

def reference(images, cotangent, test_images, test_cotangent, pair_index, example_count, aug_count, conv_weight, gn_params, conv_moment1, conv_moment2, gn_moment1, gn_moment2, noise_conv, noise_gn, step_count):
    group_size = C // GROUPS
    clip = 6.0 * C
    image_px = to_pixels(images)
    cot_px = to_pixels(cotangent)
    test_px = to_pixels(test_images).reshape(TESTS, MAP, MAP, C)
    test_cot_px = to_pixels(test_cotangent).reshape(TESTS, MAP, MAP, C)
    example_ids = jnp.arange(EXAMPLES, dtype=jnp.int32)
    live = example_ids % EX_DEV < example_count[example_ids // EX_DEV]
    slots = jnp.arange(AUG, dtype=jnp.int32)
    counts = aug_count.astype(jnp.float32)
    weights = jnp.where(live[:, None] & (slots[None, :] < aug_count[:, None]), 1.0 / counts[:, None], jnp.float32(0.0))
    test_ids = jnp.arange(TESTS, dtype=jnp.int32)
    signs = lax.optimization_barrier(jnp.sum((pair_index[:, 0:1] == test_ids[None, :]).astype(jnp.float32), 0)) - lax.optimization_barrier(jnp.sum((pair_index[:, 1:2] == test_ids[None, :]).astype(jnp.float32), 0))
    params = (conv_weight, gn_params)

    def test_loss(values):
        outputs = block(test_px.astype(jnp.float32), values[0], values[1], group_size)
        return jnp.sum(outputs * test_cot_px.astype(jnp.float32) * signs[:, None, None, None])
    test_value, test_pull = jax.vjp(test_loss, params)
    dir_conv, dir_norm = test_pull(jnp.ones_like(test_value))[0]
    dir_sq = jnp.sum(dir_conv * dir_conv) + jnp.sum(dir_norm * dir_norm)

    def visit(carry, item):
        pics, cots, row_weights = item

        def loss(values, pictures):
            outputs = block(pictures, values[0], values[1], group_size)
            return (jnp.sum(outputs * cots.astype(jnp.float32) * row_weights[:, None, None, None]), outputs)
        value, pull, outputs = jax.vjp(loss, params, pics.astype(jnp.float32), has_aux=True)
        grads, pic_grad = pull(jnp.ones_like(value))
        conv_grad, norm_grad = grads
        square = jnp.sum(conv_grad * conv_grad) + jnp.sum(norm_grad * norm_grad)
        inner = jnp.sum(conv_grad * dir_conv) + jnp.sum(norm_grad * dir_norm)
        length = jnp.sqrt(square)
        factor = clip / jnp.maximum(length, clip)
        carry = (carry[0] + factor * conv_grad, carry[1] + factor * norm_grad)
        return (carry, (outputs.astype(jnp.bfloat16), pic_grad, length, factor * inner))
    start = (jnp.zeros_like(conv_weight), jnp.zeros_like(gn_params))
    (sum_conv, sum_norm), (block_px, grad_px, example_norm, inner) = lax.scan(visit, start, (image_px, cot_px, weights))
    block_out = from_pixels(block_px)
    input_grad = from_pixels(grad_px)
    influence = inner * math.sqrt(PARAMS) / (clip * jnp.sqrt(dir_sq + 1e-06))
    noisy_conv = (sum_conv + math.sqrt(EXAMPLES) * noise_conv) / EXAMPLES
    noisy_norm = (sum_norm + math.sqrt(EXAMPLES) * noise_gn) / EXAMPLES
    correction = 1.0 - jnp.power(jnp.float32(0.5), step_count[0].astype(jnp.float32))
    conv_new, conv_first, conv_second = adamw(conv_weight, conv_moment1, conv_moment2, noisy_conv, correction, 1.0 / math.sqrt(9 * C), 0.1)
    gn_new, gn_first, gn_second = adamw(gn_params, gn_moment1, gn_moment2, noisy_norm, correction, 0.1, 0.0)
    return (block_out, input_grad, example_norm, influence, conv_new, conv_new.astype(jnp.bfloat16), conv_first, conv_second, gn_new, gn_first, gn_second)
```

```python
import functools
import math

import jax
import jax.numpy as jnp
from jax import lax
from jax.experimental import pallas as pl
from jax.experimental.pallas import tpu as pltpu
from jax.sharding import PartitionSpec as P

C = 256
MAP = 8
GROUPS = 16
AUG = 16
PIX = MAP * MAP
FAN = 9 * C
LANES = 128
CLIP = 6.0 * C
MESH = pl.DeviceIdType.MESH
f32 = jnp.float32
bf16 = jnp.bfloat16
KCOLS = 2 * FAN


def lane_tile(index):
    return pl.ds(pl.multiple_of(index * LANES, LANES), LANES)


def group_sum(tile):
    return tile.reshape(GROUPS, C // GROUPS, LANES).sum(1)


def spread_group(rows):
    return jnp.broadcast_to(rows[:, None, :], (GROUPS, C // GROUPS, LANES)).reshape(C, LANES)


def image_sum(rows, ones):
    return lax.dot_general(
        rows,
        ones,
        (((1,), (0,)), ((), ())),
        precision=lax.Precision.HIGHEST,
        preferred_element_type=f32,
    )


def sigmoid(z):
    return 0.5 * jnp.tanh(0.5 * z) + 0.5


def tap_masks():
    lane = lax.broadcasted_iota(jnp.int32, (1, LANES), 1)
    row = (lane // MAP) % MAP
    col = lane % MAP
    masks = []
    for r in (-1, 0, 1):
        for c in (-1, 0, 1):
            ok = (row + r >= 0) & (row + r < MAP) & (col + c >= 0) & (col + c < MAP)
            masks.append(jnp.where(ok, 1.0, 0.0).astype(f32).astype(bf16))
    return masks


def store_taps(value, col_ref, t, masks, flip):
    for tap in range(9):
        shift = (tap // 3 - 1) * MAP + (tap % 3 - 1)
        if shift == 0:
            moved = value
        else:
            moved = pltpu.roll(value, (-shift) % LANES, 1) * masks[tap]
        place = 8 - tap if flip else tap
        col_ref[place * C : (place + 1) * C, lane_tile(t)] = moved


def product(a, b):
    return jnp.dot(a, b, preferred_element_type=f32)


def product_nt(a, b):
    return lax.dot_general(a, b, (((1,), (1,)), ((), ())), preferred_element_type=f32)


class Work:
    pass


def norm_forward(wk, load, tiles, which, hat, rstd, hidden, col):
    stat = wk.stat

    @pl.loop(0, tiles)
    def _(t):
        stat[pl.ds(pl.multiple_of(t * GROUPS, GROUPS), GROUPS), :] = group_sum(load(t))

    rows = tiles * GROUPS
    stat[:rows, :] = image_sum(stat[:rows, :], wk.ones[...]) * (1.0 / (PIX * C // GROUPS))

    @pl.loop(0, tiles)
    def _(t):
        at = pl.ds(pl.multiple_of(t * GROUPS, GROUPS), GROUPS)
        centre = load(t) - spread_group(stat[at, :])
        hat[:, lane_tile(t)] = centre
        stat[at, :] = group_sum(centre * centre)

    spread = image_sum(stat[:rows, :], wk.ones[...]) * (1.0 / (PIX * C // GROUPS))
    rstd[:rows, :] = lax.rsqrt(spread + 1e-05)

    @pl.loop(0, tiles)
    def _(t):
        at = pl.ds(pl.multiple_of(t * GROUPS, GROUPS), GROUPS)
        normed = hat[:, lane_tile(t)] * spread_group(rstd[at, :])
        hat[:, lane_tile(t)] = normed
        scaled = normed * wk.gn[2 * which] + wk.gn[2 * which + 1]
        act = (scaled * sigmoid(scaled)).astype(bf16)
        hidden[:, lane_tile(t)] = act
        if col is not None:
            store_taps(act, col, t, wk.masks, False)


def norm_backward(wk, grad, tiles, which, hat, rstd, emit, acc):
    stat, stat2 = wk.stat, wk.stat2
    acc[0] = jnp.zeros((C, LANES), f32)
    acc[1] = jnp.zeros((C, LANES), f32)

    @pl.loop(0, tiles)
    def _(t):
        at = pl.ds(pl.multiple_of(t * GROUPS, GROUPS), GROUPS)
        normed = hat[:, lane_tile(t)]
        scaled = normed * wk.gn[2 * which] + wk.gn[2 * which + 1]
        gate = sigmoid(scaled)
        inner = grad[:, lane_tile(t)] * gate * (1.0 + scaled * (1.0 - gate))
        acc[0] += inner * normed
        acc[1] += inner
        inner = inner * wk.gn[2 * which]
        grad[:, lane_tile(t)] = inner
        stat[at, :] = group_sum(inner)
        stat2[at, :] = group_sum(inner * normed)

    if emit is not None:
        rows = tiles * GROUPS
        scale = 1.0 / (PIX * C // GROUPS)
        stat[:rows, :] = image_sum(stat[:rows, :], wk.ones[...]) * scale
        stat2[:rows, :] = image_sum(stat2[:rows, :], wk.ones[...]) * scale

        @pl.loop(0, tiles)
        def _(t):
            at = pl.ds(pl.multiple_of(t * GROUPS, GROUPS), GROUPS)
            value = grad[:, lane_tile(t)] - spread_group(stat[at, :])
            value = value - hat[:, lane_tile(t)] * spread_group(stat2[at, :])
            emit(t, value * spread_group(rstd[at, :]))


def matmul_cols(out, left, right, width):
    step = min(width, 256)
    for j in range(0, width, step):
        out[:, j : j + step] = product(left, right[:, j : j + step])


def fill_work(wk):
    half_a = lax.broadcasted_iota(jnp.int32, (LANES, LANES), 0) // PIX
    half_b = lax.broadcasted_iota(jnp.int32, (LANES, LANES), 1) // PIX
    wk.ones[...] = jnp.where(half_a == half_b, 1.0, 0.0).astype(f32)
    wk.masks = tap_masks()


def unpack_params(wk):
    tail = wk.ktp[:, KCOLS : KCOLS + LANES].astype(f32)
    for k in range(6):
        value = tail[:, k : k + 1] + tail[:, 8 + k : 9 + k] + tail[:, 16 + k : 17 + k]
        value = jnp.broadcast_to(value, (C, LANES))
        if k < 4:
            wk.gn[k] = value
        else:
            wk.rs[k - 4] = value


def turn_kernels(wk):
    for k in range(18):
        at = (k // 9) * FAN + (k % 9) * C
        wk.kb[k // 9, :, (k % 9) * C : (k % 9 + 1) * C] = wk.ktp[:, at : at + C].T


def unit(wk, x_load, cot_load, weight_load, tiles, grads, gn_out, block_store, part_store):
    width = tiles * LANES
    col = wk.col

    def cols(ref):
        return ref if width == ref.shape[1] else ref.at[:, :width]

    norm_forward(wk, x_load, tiles, 0, wk.hat1, wk.rstd1, wk.hid1, col)
    matmul_cols(wk.mid, wk.ktp[:, :FAN], cols(col), width)
    norm_forward(
        wk,
        lambda t: wk.mid[:, lane_tile(t)],
        tiles,
        1,
        wk.hat2,
        wk.rstd2,
        wk.hid2,
        col if block_store is not None else None,
    )
    if block_store is not None:
        matmul_cols(wk.mid, wk.ktp[:, FAN : 2 * FAN], cols(col), width)

    @pl.loop(0, tiles)
    def _(t):
        if block_store is not None:
            block_store(t, x_load(t) + wk.mid[:, lane_tile(t)])
        store_taps((cot_load(t) * weight_load(t)).astype(bf16), col, t, wk.masks, True)

    matmul_cols(wk.mid, wk.kb[1], cols(col), width)
    for tap in range(9):
        grads[9 + tap] = product_nt(col[tap * C : (tap + 1) * C, :width], wk.hid2[:, :width])

    def emit_middle(t, value):
        store_taps(value.astype(bf16), col, t, wk.masks, True)

    norm_backward(wk, wk.mid, tiles, 1, wk.hat2, wk.rstd2, emit_middle, wk.acc.at[1])
    matmul_cols(wk.mid, wk.kb[0], cols(col), width)
    for tap in range(9):
        grads[tap] = product_nt(col[tap * C : (tap + 1) * C, :width], wk.hid1[:, :width])
    norm_backward(wk, wk.mid, tiles, 0, wk.hat1, wk.rstd1, part_store, wk.acc.at[0])

    lane = lax.broadcasted_iota(jnp.int32, (1, LANES), 1)
    total = jnp.zeros((C, LANES), f32)
    for k in range(4):
        one = jnp.sum(wk.acc[k // 2, k % 2], axis=1, keepdims=True)
        total = total + jnp.where(lane == k, one, 0.0)
    gn_out[...] = total


def raw_gradient(wk, grads, sq):
    rows = 32

    @pl.loop(0, C // rows)
    def _(j):
        at = pl.ds(pl.multiple_of(j * rows, rows), rows)
        for conv in range(2):
            first = jnp.zeros((rows, C), f32)
            second = jnp.zeros((rows, C), f32)
            for tap in range(9):
                g = grads[conv * 9 + tap, at, :]
                k = wk.ktp[at, conv * FAN + tap * C : conv * FAN + (tap + 1) * C].astype(f32)
                first = first + g
                second = second + g * k
            first = jnp.sum(first, axis=1, keepdims=True) * (1.0 / FAN)
            second = jnp.sum(second, axis=1, keepdims=True)
            rs = wk.rs[conv, at, 0:1]
            squares = jnp.zeros((rows, C), f32)
            for tap in range(9):
                g = grads[conv * 9 + tap, at, :]
                k = wk.ktp[at, conv * FAN + tap * C : conv * FAN + (tap + 1) * C].astype(f32)
                value = (g - first - k * second) * rs
                grads[conv * 9 + tap, at, :] = value
                squares = squares + value * value
            fold = squares[:, :LANES] + squares[:, LANES:]
            sq[...] += fold.reshape(rows // 8, 8, LANES).sum(0)


def whole_sum(tile):
    return jnp.sum(jnp.sum(tile, axis=1, keepdims=True), axis=0, keepdims=True)


WORK_SCRATCH = [
    pltpu.VMEM((2, C, FAN), bf16),
    pltpu.VMEM((FAN, AUG * PIX), bf16),
    pltpu.VMEM((C, AUG * PIX), f32),
    pltpu.VMEM((C, AUG * PIX), f32),
    pltpu.VMEM((C, AUG * PIX), f32),
    pltpu.VMEM((C, AUG * PIX), bf16),
    pltpu.VMEM((C, AUG * PIX), bf16),
    pltpu.VMEM((LANES, LANES), f32),
    pltpu.VMEM((LANES, LANES), f32),
    pltpu.VMEM((LANES, LANES), f32),
    pltpu.VMEM((LANES, LANES), f32),
    pltpu.VMEM((LANES, LANES), f32),
    pltpu.VMEM((4, C, LANES), f32),
    pltpu.VMEM((2, C, LANES), f32),
    pltpu.VMEM((2, 2, C, LANES), f32),
]
WORK_NAMES = (
    "kb",
    "col",
    "mid",
    "hat1",
    "hat2",
    "hid1",
    "hid2",
    "stat",
    "stat2",
    "rstd1",
    "rstd2",
    "ones",
    "gn",
    "rs",
    "acc",
)


def make_work(ktp, refs):
    wk = Work()
    wk.ktp = ktp
    for name, ref in zip(WORK_NAMES, refs):
        setattr(wk, name, ref)
    return wk


def compute_kernel(
    x, cot, xt, ct, ktp, wl, sg, block, part, clipped, test, clipped_gn, test_gn, raw, raw_gn, length, *scratch
):
    examples = x.shape[0]
    wk = make_work(ktp, scratch[:-2])
    tgrad, sq = scratch[-2:]
    fill_work(wk)
    unpack_params(wk)
    turn_kernels(wk)
    gn_tmp = test_gn
    unit(
        wk,
        lambda t: xt[...].astype(f32),
        lambda t: ct[...].astype(f32),
        lambda t: sg[...],
        1,
        tgrad,
        gn_tmp,
        None,
        None,
    )
    raw_gradient(wk, tgrad, sq)

    @pl.loop(0, 18)
    def _(k):
        test[k] = tgrad[k].astype(bf16)

    sq[...] = jnp.zeros_like(sq)

    @pl.loop(0, examples)
    def _(e):
        def block_store(t, value):
            block[e, :, lane_tile(t)] = value.astype(bf16)

        def part_store(t, value):
            part[e, :, lane_tile(t)] = value.astype(bf16)

        unit(
            wk,
            lambda t: x[e, :, lane_tile(t)].astype(f32),
            lambda t: cot[e, :, lane_tile(t)].astype(f32),
            lambda t: wl[e, :, lane_tile(t)],
            8,
            raw.at[e],
            raw_gn.at[e],
            block_store,
            part_store,
        )
        sq[...] = jnp.zeros_like(sq)
        raw_gradient(wk, raw.at[e], sq)
        gn = raw_gn[e]
        square = whole_sum(sq[...]) + whole_sum(gn * gn)
        length[e] = jnp.broadcast_to(jnp.sqrt(square), (8, LANES))

    factors = [CLIP / jnp.maximum(length[e][0:1, 0:1], CLIP) for e in range(examples)]
    total = factors[0] * raw_gn[0]
    for e in range(1, examples):
        total = total + factors[e] * raw_gn[e]
    clipped_gn[...] = total

    @pl.loop(0, 18)
    def _(k):
        total = factors[0] * raw[0, k]
        for e in range(1, examples):
            total = total + factors[e] * raw[e, k]
        clipped[k] = total.astype(bf16)


def compute(x, cot, xt, ct, ktp, wl, sg):
    examples = x.shape[0]
    out = jax.ShapeDtypeStruct
    shapes = (
        out(x.shape, bf16),
        out(x.shape, bf16),
        out((18, C, C), bf16),
        out((18, C, C), bf16),
        out((C, LANES), f32),
        out((C, LANES), f32),
        out((examples, 18, C, C), f32),
        out((examples, C, LANES), f32),
        out((examples, 8, LANES), f32),
    )
    spec = pl.BlockSpec(memory_space=pltpu.VMEM)
    return pl.pallas_call(
        compute_kernel,
        out_shape=shapes,
        in_specs=[spec] * 7,
        out_specs=(spec,) * 9,
        scratch_shapes=WORK_SCRATCH + [pltpu.VMEM((18, C, C), f32), pltpu.VMEM((8, LANES), f32)],
        compiler_params=pltpu.CompilerParams(vmem_limit_bytes=58 << 20),
    )(x, cot, xt, ct, ktp, wl, sg)


def peer_copy(src, dst, send, recv, **where):
    return pltpu.make_async_remote_copy(
        src_ref=src, dst_ref=dst, send_sem=send, recv_sem=recv, device_id=where, device_id_type=MESH
    )


def greet(peers):
    barrier = pltpu.get_barrier_semaphore()
    for where in peers:
        pl.semaphore_signal(barrier, inc=1, device_id=where, device_id_type=MESH)
    pl.semaphore_wait(barrier, len(peers))


def gather_kernel(
    images, cots, timg, tcot, kshard, x, cot, xt, ct, ktp, s_a2a, r_a2a, s_own, r_up, r_dn, s_up, s_dn, s_core, r_core, s_loc
):
    n = 8
    me = lax.axis_index("narrow")
    z, c = me // 2, me % 2
    examples = x.shape[0]
    chans = images.shape[1]
    mine = pl.ds(pl.multiple_of(me * chans, chans), chans)
    greet([{"narrow": lax.rem(me + k, n)} for k in range(1, n)])

    def rows(zz):
        return pl.ds(pl.multiple_of((zz * 2 + c) * chans, chans), chans)

    sibling = me + 1 - 2 * c

    def up(step):
        src = kshard if step == 0 else ktp.at[rows(z - step)]
        return peer_copy(src, ktp.at[rows(z - step)], s_up.at[step], r_up.at[step], narrow=me + 2)

    def down(step):
        src = kshard if step == 0 else ktp.at[rows(z + step)]
        return peer_copy(src, ktp.at[rows(z + step)], s_dn.at[step], r_dn.at[step], narrow=me - 2)

    def across(slot, zz):
        src = kshard if slot == 0 else ktp.at[rows(zz)]
        return peer_copy(src, ktp.at[rows(zz)], s_core.at[slot], r_core.at[slot], narrow=sibling)

    @pl.when(z < 3)
    def _():
        up(0).start()

    @pl.when(z > 0)
    def _():
        down(0).start()

    across(0, z).start()
    pairs = ((timg, xt), (tcot, ct), (images, x), (cots, cot))
    local = [pltpu.make_async_copy(kshard, ktp.at[mine], s_loc.at[4])]
    sends = []
    for a, (src, dst) in enumerate(pairs):
        for k in range(n):
            to = lax.rem(me + k, n)
            if a < 2:
                piece = src.at[:, pl.ds(pl.multiple_of(to * LANES, LANES), LANES)]
                place = dst.at[mine]
            else:
                piece = src.at[pl.ds(to * examples, examples)]
                place = dst.at[:, mine]
            if k == 0:
                local.append(pltpu.make_async_copy(piece, place, s_loc.at[a]))
            else:
                sends.append(peer_copy(piece, place, s_a2a.at[a, k - 1], r_a2a.at[a, k - 1], narrow=to))
    for copy in local + sends:
        copy.start()
    for step in range(1, 4):

        @pl.when(z - step >= 0)
        def _():
            up(step - 1).wait_recv()
            across(step, z - step).start()
            if step < 3:

                @pl.when(z < 3)
                def _():
                    up(step).start()

        @pl.when(z + step <= 3)
        def _():
            down(step - 1).wait_recv()
            across(3 + step, z + step).start()
            if step < 3:

                @pl.when(z > 0)
                def _():
                    down(step).start()

    for step in range(3):

        @pl.when((z < 3) & (z - step >= 0))
        def _():
            up(step).wait_send()

        @pl.when((z > 0) & (z + step <= 3))
        def _():
            down(step).wait_send()

    across(0, z).wait()
    for step in range(1, 4):

        @pl.when(z - step >= 0)
        def _():
            across(step, z - step).wait()

        @pl.when(z + step <= 3)
        def _():
            across(3 + step, z + step).wait()

    for copy in local + sends:
        copy.wait()


def gather(images, cots, timg, tcot, kshard, examples):
    out = jax.ShapeDtypeStruct
    anyspace = pl.BlockSpec(memory_space=pl.ANY)
    dma = pltpu.SemaphoreType.DMA
    return pl.pallas_call(
        gather_kernel,
        out_shape=(
            out((examples, C, AUG * PIX), bf16),
            out((examples, C, AUG * PIX), bf16),
            out((C, LANES), bf16),
            out((C, LANES), bf16),
            out((C, KCOLS + LANES), bf16),
        ),
        in_specs=[anyspace] * 5,
        out_specs=(anyspace,) * 5,
        scratch_shapes=[
            dma((4, 7)),
            dma((4, 7)),
            dma,
            dma((3,)),
            dma((3,)),
            dma((3,)),
            dma((3,)),
            dma((7,)),
            dma((7,)),
            dma((5,)),
        ],
        compiler_params=pltpu.CompilerParams(collective_id=0, has_side_effects=True),
    )(images, cots, timg, tcot, kshard)


def reduce_kernel(
    block,
    part,
    clip_conv,
    test_conv,
    clip_gn,
    test_gn,
    raw,
    raw_gn,
    length,
    ob,
    op,
    red,
    figures,
    cb,
    cg,
    half,
    wb,
    quarter,
    zb,
    dt,
    s_back,
    r_back,
    s_core,
    r_core,
    s_wide,
    r_wide,
    s_z,
    r_z,
    s_f,
    r_f,
    s_fin,
    r_fin,
    s_fig,
    r_fig,
    s_loc,
):
    n = 8
    me = lax.axis_index("narrow")
    w = lax.axis_index("wide")
    z, c = me // 2, me % 2
    sibling = me + 1 - 2 * c
    examples = block.shape[0]
    chans = ob.shape[1]
    greet(
        [{"narrow": lax.rem(me + k, n)} for k in range(1, n)]
        + [{"wide": lax.rem(w + k, 4)} for k in range(1, 4)]
    )
    core = []
    for a, (conv, gn) in enumerate(((clip_conv, clip_gn), (test_conv, test_gn))):
        core.append(peer_copy(conv.at[:, :, 1 - c], cb.at[a], s_core.at[a, 0], r_core.at[a, 0], narrow=sibling))
        core.append(peer_copy(gn.at[:, 1 - c], cg.at[a], s_core.at[a, 1], r_core.at[a, 1], narrow=sibling))
    for copy in core:
        copy.start()
    back = []
    for a, (src, dst) in enumerate(((block, ob), (part, op))):
        for k in range(n):
            to = lax.rem(me + k, n)
            piece = src.at[:, pl.ds(pl.multiple_of(to * chans, chans), chans)]
            place = dst.at[pl.ds(me * examples, examples)]
            if k == 0:
                back.append(pltpu.make_async_copy(piece, place, s_loc.at[a]))
            else:
                back.append(peer_copy(piece, place, s_back.at[a, k - 1], r_back.at[a, k - 1], narrow=to))
    for copy in back:
        copy.start()
    for copy in core:
        copy.wait()
    for a, (conv, gn) in enumerate(((clip_conv, clip_gn), (test_conv, test_gn))):
        for k in range(2):

            @pl.loop(0, 9)
            def _(tap):
                total = conv[k * 9 + tap, :, c].astype(f32) + cb[a, k * 9 + tap].astype(f32)
                half[a, k * 2, tap] = total[:, :, :LANES].astype(bf16)
                half[a, k * 2 + 1, tap] = total[:, :, LANES:].astype(bf16)

        half[a, 0, 9] = (gn[:, c].astype(f32) + cg[a].astype(f32)).astype(bf16)
        for q in range(1, 4):
            half[a, q, 9] = jnp.zeros_like(half[a, q, 9])
    wide = []
    for k in range(1, 4):
        to = lax.rem(w + k, 4)
        wide.append(peer_copy(half.at[:, to], wb.at[k - 1], s_wide.at[k - 1], r_wide.at[k - 1], wide=to))
    for copy in wide:
        copy.start()
    for copy in wide:
        copy.wait()
    for a in range(2):

        @pl.loop(0, 10)
        def _(tap):
            total = half[a, w, tap].astype(f32)
            for k in range(3):
                total = total + wb[k, a, tap].astype(f32)
            quarter[a, tap] = total.astype(bf16)

    line = []
    for k in range(1, 4):
        to = lax.rem(z + k, 4)
        line.append(
            peer_copy(quarter.at[:, :, to], zb.at[k - 1], s_z.at[k - 1], r_z.at[k - 1], narrow=to * 2 + c)
        )
    for copy in line:
        copy.start()
    for copy in line:
        copy.wait()

    def final(a, tap):
        total = quarter[a, tap, z].astype(f32)
        for k in range(3):
            total = total + zb[k, a, tap].astype(f32)
        return total.astype(bf16)

    @pl.loop(0, 10)
    def _(tap):
        red[w, tap] = final(0, tap)
        dt[c, w, z, tap] = final(1, tap)

    finals = []
    for k in range(1, 4):
        to = lax.rem(w + k, 4)
        finals.append(peer_copy(red.at[w], red.at[w], s_f.at[0, k - 1], r_f.at[0, k - 1], wide=to))
    spread = []
    for k in range(1, 4):
        to = lax.rem(z + k, 4)
        own = dt.at[c, w, z]
        spread.append(peer_copy(own, own, s_f.at[1, k - 1], r_f.at[1, k - 1], narrow=to * 2 + c))
    for copy in spread + finals:
        copy.start()
    for copy in spread:
        copy.wait()
    fin = []
    for k in range(1, 4):
        to = lax.rem(w + k, 4)
        fin.append(peer_copy(dt.at[c, w], dt.at[c, w], s_fin.at[k - 1], r_fin.at[k - 1], wide=to))
    for copy in fin:
        copy.start()
    for copy in fin:
        copy.wait()
    last = peer_copy(dt.at[c], dt.at[c], s_fin.at[3], r_fin.at[3], narrow=sibling)
    last.start()
    last.wait()

    own_rows = lax.broadcasted_iota(jnp.int32, (8, LANES), 0)
    zero = jnp.zeros((chans, LANES), f32)

    def visit(index, carry):
        q, rest = index // 8, index % 8
        zz, cc = rest // 2, rest % 2
        at = pl.ds(pl.multiple_of(rest * chans, chans), chans)
        square = carry[0]
        sums = list(carry[1:])
        for tap in range(9):
            d = dt[cc, q, zz, tap].astype(f32)
            square = square + d * d
            for e in range(examples):
                sums[e] = sums[e] + d * raw[e, (q // 2) * 9 + tap, at, pl.ds(pl.multiple_of((q % 2) * LANES, LANES), LANES)]
        return (square, *sums)

    totals = lax.fori_loop(0, 32, visit, (zero,) * (examples + 1))

    def visit_gn(rest, carry):
        at = pl.ds(pl.multiple_of(rest * chans, chans), chans)
        d = dt[rest % 2, 0, rest // 2, 9].astype(f32)
        return (carry[0] + d * d,) + tuple(carry[1 + e] + d * raw_gn[e, at, :] for e in range(examples))

    totals = lax.fori_loop(0, 8, visit_gn, totals)
    dir_sq = whole_sum(totals[0])
    params = 18 * C * C + 4 * C
    for e in range(examples):
        size = length[e]
        factor = CLIP / jnp.maximum(size, CLIP)
        influence = factor * whole_sum(totals[1 + e]) * math.sqrt(params) / (CLIP * jnp.sqrt(dir_sq + 1e-06))
        figures[me, e] = jnp.where(own_rows == 0, size, influence)
    figs = []
    for k in range(1, n):
        figs.append(
            peer_copy(figures.at[me], figures.at[me], s_fig.at[k - 1], r_fig.at[k - 1], narrow=lax.rem(me + k, n))
        )
    for copy in figs:
        copy.start()
    for copy in figs + finals + back:
        copy.wait()


def reduce_all(block, part, clip_conv, test_conv, clip_gn, test_gn, raw, raw_gn, length, chans):
    examples = block.shape[0]
    out = jax.ShapeDtypeStruct
    anyspace = pl.BlockSpec(memory_space=pl.ANY)
    vmem = pl.BlockSpec(memory_space=pltpu.VMEM)
    dma = pltpu.SemaphoreType.DMA
    whole = (18, 4, 2, chans, C)
    return pl.pallas_call(
        reduce_kernel,
        out_shape=(
            out((8 * examples, chans, AUG * PIX), bf16),
            out((8 * examples, chans, AUG * PIX), bf16),
            out((4, 10, chans, LANES), bf16),
            out((8, examples, 8, LANES), f32),
        ),
        in_specs=[anyspace, anyspace] + [vmem] * 7,
        out_specs=(anyspace, anyspace, vmem, vmem),
        scratch_shapes=[
            pltpu.VMEM((2, 18, 4, chans, C), bf16),
            pltpu.VMEM((2, 4, chans, LANES), bf16),
            pltpu.VMEM((2, 4, 10, 4, chans, LANES), bf16),
            pltpu.VMEM((3, 2, 10, 4, chans, LANES), bf16),
            pltpu.VMEM((2, 10, 4, chans, LANES), bf16),
            pltpu.VMEM((3, 2, 10, chans, LANES), bf16),
            pltpu.VMEM((2, 4, 4, 10, chans, LANES), bf16),
            dma((2, 7)),
            dma((2, 7)),
            dma((2, 2)),
            dma((2, 2)),
            dma((3,)),
            dma((3,)),
            dma((3,)),
            dma((3,)),
            dma((2, 3)),
            dma((2, 3)),
            dma((4,)),
            dma((4,)),
            dma((7,)),
            dma((7,)),
            dma((2,)),
        ],
        compiler_params=pltpu.CompilerParams(collective_id=1, has_side_effects=True, vmem_limit_bytes=58 << 20),
    )(
        block,
        part,
        clip_conv.reshape(whole),
        test_conv.reshape(whole),
        clip_gn.astype(bf16).reshape(4, 2, chans, LANES),
        test_gn.astype(bf16).reshape(4, 2, chans, LANES),
        raw,
        raw_gn,
        length,
    )


def pieces(v):
    high = lax.reduce_precision(v, 8, 7)
    rest = v - high
    mid = lax.reduce_precision(rest, 8, 7)
    low = rest - mid
    return high.astype(bf16), mid.astype(bf16), low.astype(bf16)


def kernel_rows(conv_weight, gn_params):
    chans = conv_weight.shape[4]
    centre = conv_weight - jnp.mean(conv_weight, axis=(1, 2, 3), keepdims=True)
    spread = jnp.mean(centre * centre, axis=(1, 2, 3), keepdims=True)
    scale = lax.rsqrt(FAN * spread + 1e-06)
    kernels = (centre * scale).astype(bf16).reshape(2, FAN, chans)
    rows = kernels.transpose(2, 0, 1).reshape(chans, KCOLS)
    small = jnp.concatenate([gn_params.T, scale.reshape(2, chans).T, jnp.zeros((chans, 2), f32)], 1)
    tail = jnp.concatenate(list(pieces(small)) + [jnp.zeros((chans, LANES - 24), bf16)], 1)
    return jnp.concatenate([rows, tail], 1)


def adamw(weight, first, second, grad, correction, rate, decay):
    first_new = 0.5 * first + 0.5 * grad
    second_new = 0.5 * second + 0.5 * grad * grad
    update = first_new / correction / (jnp.sqrt(second_new / correction) + 1e-08)
    return (weight - rate * (update + decay * weight), first_new, second_new)


def plain_gather(images, cots, timg, tcot, kshard, narrow):
    share = narrow // 8
    x = lax.all_to_all(images, "narrow", 0, 1, tiled=True)
    cot = lax.all_to_all(cots, "narrow", 0, 1, tiled=True)
    ktp = lax.all_gather(kshard, "narrow", axis=0, tiled=True)
    own = (lax.axis_index("narrow") // share) * LANES

    def pick(v):
        return lax.dynamic_slice_in_dim(lax.all_gather(v, "narrow", axis=0, tiled=True), own, LANES, 1)

    return x, cot, pick(timg), pick(tcot), ktp


def plain_reduce(block, part, clip_conv, test_conv, clip_gn, test_gn, raw, raw_gn, length, chans):
    examples = block.shape[0]
    ob = lax.all_to_all(block, "narrow", 1, 0, tiled=True)
    op = lax.all_to_all(part, "narrow", 1, 0, tiled=True)
    own = lax.axis_index("narrow") * chans
    rows = lax.psum(clip_conv, ("wide", "narrow"))
    rows = lax.dynamic_slice_in_dim(rows, own, chans, 1)
    gn_rows = lax.dynamic_slice_in_dim(lax.psum(clip_gn.astype(bf16), ("wide", "narrow")), own, chans, 0)
    red = rows.reshape(2, 9, chans, 2, LANES).transpose(0, 3, 1, 2, 4).reshape(4, 9, chans, LANES)
    red = jnp.concatenate([red, jnp.broadcast_to(gn_rows, (4, 1, chans, LANES))], 1)
    d = lax.psum(test_conv, ("wide", "narrow")).astype(f32)
    d_gn = lax.psum(test_gn.astype(bf16), ("wide", "narrow")).astype(f32)
    dir_sq = jnp.sum(d * d) + jnp.sum(d_gn * d_gn)
    inner = jnp.sum(raw * d, axis=(1, 2, 3)) + jnp.sum(raw_gn * d_gn, axis=(1, 2))
    size = length[:, 0, 0]
    factor = CLIP / jnp.maximum(size, CLIP)
    influence = factor * inner * math.sqrt(18 * C * C + 4 * C) / (CLIP * jnp.sqrt(dir_sq + 1e-06))
    figures = lax.all_gather(jnp.stack([size, influence], 1), "narrow", axis=0)
    return ob, op, red, figures[:, :, :, None]


def local(
    images,
    cotangent,
    test_images,
    test_cotangent,
    pair_index,
    example_count,
    aug_count,
    conv_weight,
    gn_params,
    conv_moment1,
    conv_moment2,
    gn_moment1,
    gn_moment2,
    noise_conv,
    noise_gn,
    step_count,
):
    n_wide, narrow = lax.axis_size("wide"), lax.axis_size("narrow")
    held, chans = images.shape[0], images.shape[1]
    examples = held // narrow
    share = narrow // 8
    me = lax.axis_index("narrow")
    slots = jnp.arange(AUG, dtype=jnp.int32)
    live = jnp.arange(held, dtype=jnp.int32) < example_count[0]
    weights = jnp.where(
        live[:, None] & (slots[None, :] < aug_count[:, None]),
        1.0 / aug_count.astype(f32)[:, None],
        f32(0.0),
    )
    pixels = jnp.repeat(weights, PIX, axis=1)
    pairs = pair_index % AUG
    signs = jnp.sum((pairs[:, 0:1] == slots[None, :]).astype(f32), 0) - jnp.sum(
        (pairs[:, 1:2] == slots[None, :]).astype(f32), 0
    )
    sign_pixels = jnp.repeat(signs, PIX).reshape(8, LANES) * (1.0 / share)
    wl = lax.dynamic_slice_in_dim(pixels, me * examples, examples, 0)[:, None, :]
    sg = lax.dynamic_slice_in_dim(sign_pixels, me // share, 1, 0)
    kshard = kernel_rows(conv_weight, gn_params)
    timg, tcot = test_images[0], test_cotangent[0]
    direct = n_wide == 4 and narrow == 8
    if direct:
        x, cot, xt, ct, ktp = gather(images, cotangent, timg, tcot, kshard, examples)
    else:
        x, cot, xt, ct, ktp = plain_gather(images, cotangent, timg, tcot, kshard, narrow)
    block, part, clip_conv, test_conv, clip_gn, test_gn, raw, raw_gn, length = compute(x, cot, xt, ct, ktp, wl, sg)
    send = reduce_all if direct else plain_reduce
    block_out, op, red, figures = send(
        block, part, clip_conv, test_conv, clip_gn, test_gn, raw, raw_gn, length, chans
    )
    input_grad = cotangent.astype(f32) * pixels[:, None, :] + op.astype(f32)
    lengths = figures[:, :, 0, 0].reshape(held)
    influence = figures[:, :, 1, 0].reshape(held)
    sum_conv = red[:, :9].reshape(2, 2, 9, chans, LANES).transpose(0, 2, 1, 4, 3)
    sum_conv = sum_conv.reshape(2, 3, 3, C, chans).astype(f32)
    sum_norm = red[0, 9, :, :4].T.astype(f32)
    total = held * n_wide
    noisy_conv = (sum_conv + math.sqrt(total) * noise_conv) / total
    noisy_norm = (sum_norm + math.sqrt(total) * noise_gn) / total
    correction = 1.0 - jnp.power(f32(0.5), step_count[0].astype(f32))
    conv_new, conv_first, conv_second = adamw(
        conv_weight, conv_moment1, conv_moment2, noisy_conv, correction, 1.0 / math.sqrt(9 * C), 0.1
    )
    gn_new, gn_first, gn_second = adamw(
        gn_params, gn_moment1, gn_moment2, noisy_norm, correction, 0.1, 0.0
    )
    return (
        block_out,
        input_grad,
        lengths,
        influence,
        conv_new,
        conv_new.astype(bf16),
        conv_first,
        conv_second,
        gn_new,
        gn_first,
        gn_second,
    )


def solution(mesh):
    in_specs = (
        P("wide", "narrow", None),
        P("wide", "narrow", None),
        P("wide", "narrow", None),
        P("wide", "narrow", None),
        P("wide", None),
        P("wide"),
        P("wide"),
        P(None, None, None, None, "narrow"),
        P(None, "narrow"),
        P(None, None, None, None, "narrow"),
        P(None, None, None, None, "narrow"),
        P(None, "narrow"),
        P(None, "narrow"),
        P(None, None, None, None, "narrow"),
        P(None, "narrow"),
        P(),
    )
    out_specs = (
        P("wide", "narrow", None),
        P("wide", "narrow", None),
        P("wide"),
        P("wide"),
        P(None, None, None, None, "narrow"),
        P(None, None, None, None, "narrow"),
        P(None, None, None, None, "narrow"),
        P(None, None, None, None, "narrow"),
        P(None, "narrow"),
        P(None, "narrow"),
        P(None, "narrow"),
    )
    return jax.shard_map(local, mesh=mesh, in_specs=in_specs, out_specs=out_specs, check_vma=False)
```

```python
import functools
import math

import jax
import jax.numpy as jnp
from jax import lax
from jax.experimental import pallas as pl
from jax.experimental.pallas import tpu as pltpu
from jax.sharding import PartitionSpec as P

C = 256
MAP = 8
GROUPS = 16
AUG = 16
PIX = MAP * MAP
FAN = 9 * C
LANES = 128
CLIP = 6.0 * C
MESH = pl.DeviceIdType.MESH
f32 = jnp.float32
bf16 = jnp.bfloat16
KCOLS = 2 * FAN


def lane_tile(index):
    return pl.ds(pl.multiple_of(index * LANES, LANES), LANES)


def group_sum(tile):
    return tile.reshape(GROUPS, C // GROUPS, LANES).sum(1)


def spread_group(rows):
    return jnp.broadcast_to(rows[:, None, :], (GROUPS, C // GROUPS, LANES)).reshape(C, LANES)


def image_sum(rows, ones):
    return lax.dot_general(
        rows,
        ones,
        (((1,), (0,)), ((), ())),
        precision=lax.Precision.HIGHEST,
        preferred_element_type=f32,
    )


def sigmoid(z):
    return 0.5 * jnp.tanh(0.5 * z) + 0.5


def tap_masks():
    lane = lax.broadcasted_iota(jnp.int32, (1, LANES), 1)
    row = (lane // MAP) % MAP
    col = lane % MAP
    masks = []
    for r in (-1, 0, 1):
        for c in (-1, 0, 1):
            ok = (row + r >= 0) & (row + r < MAP) & (col + c >= 0) & (col + c < MAP)
            masks.append(jnp.where(ok, 1.0, 0.0).astype(f32).astype(bf16))
    return masks


def store_taps(value, col_ref, t, masks, flip):
    for tap in range(9):
        shift = (tap // 3 - 1) * MAP + (tap % 3 - 1)
        if shift == 0:
            moved = value
        else:
            moved = pltpu.roll(value, (-shift) % LANES, 1) * masks[tap]
        place = 8 - tap if flip else tap
        col_ref[place * C : (place + 1) * C, lane_tile(t)] = moved


def product(a, b):
    return jnp.dot(a, b, preferred_element_type=f32)


def product_nt(a, b):
    return lax.dot_general(a, b, (((1,), (1,)), ((), ())), preferred_element_type=f32)


class Work:
    pass


def norm_forward(wk, load, tiles, which, hat, rstd, hidden, col):
    stat = wk.stat

    @pl.loop(0, tiles)
    def _(t):
        stat[pl.ds(pl.multiple_of(t * GROUPS, GROUPS), GROUPS), :] = group_sum(load(t))

    rows = tiles * GROUPS
    stat[:rows, :] = image_sum(stat[:rows, :], wk.ones[...]) * (1.0 / (PIX * C // GROUPS))

    @pl.loop(0, tiles)
    def _(t):
        at = pl.ds(pl.multiple_of(t * GROUPS, GROUPS), GROUPS)
        centre = load(t) - spread_group(stat[at, :])
        hat[:, lane_tile(t)] = centre
        stat[at, :] = group_sum(centre * centre)

    spread = image_sum(stat[:rows, :], wk.ones[...]) * (1.0 / (PIX * C // GROUPS))
    rstd[:rows, :] = lax.rsqrt(spread + 1e-05)

    @pl.loop(0, tiles)
    def _(t):
        at = pl.ds(pl.multiple_of(t * GROUPS, GROUPS), GROUPS)
        normed = hat[:, lane_tile(t)] * spread_group(rstd[at, :])
        hat[:, lane_tile(t)] = normed
        scaled = normed * wk.gn[2 * which] + wk.gn[2 * which + 1]
        act = (scaled * sigmoid(scaled)).astype(bf16)
        hidden[:, lane_tile(t)] = act
        if col is not None:
            store_taps(act, col, t, wk.masks, False)


def norm_backward(wk, grad, tiles, which, hat, rstd, emit, acc):
    stat, stat2 = wk.stat, wk.stat2
    acc[0] = jnp.zeros((C, LANES), f32)
    acc[1] = jnp.zeros((C, LANES), f32)

    @pl.loop(0, tiles)
    def _(t):
        at = pl.ds(pl.multiple_of(t * GROUPS, GROUPS), GROUPS)
        normed = hat[:, lane_tile(t)]
        scaled = normed * wk.gn[2 * which] + wk.gn[2 * which + 1]
        gate = sigmoid(scaled)
        inner = grad[:, lane_tile(t)] * gate * (1.0 + scaled * (1.0 - gate))
        acc[0] += inner * normed
        acc[1] += inner
        inner = inner * wk.gn[2 * which]
        grad[:, lane_tile(t)] = inner
        stat[at, :] = group_sum(inner)
        stat2[at, :] = group_sum(inner * normed)

    if emit is not None:
        rows = tiles * GROUPS
        scale = 1.0 / (PIX * C // GROUPS)
        stat[:rows, :] = image_sum(stat[:rows, :], wk.ones[...]) * scale
        stat2[:rows, :] = image_sum(stat2[:rows, :], wk.ones[...]) * scale

        @pl.loop(0, tiles)
        def _(t):
            at = pl.ds(pl.multiple_of(t * GROUPS, GROUPS), GROUPS)
            value = grad[:, lane_tile(t)] - spread_group(stat[at, :])
            value = value - hat[:, lane_tile(t)] * spread_group(stat2[at, :])
            emit(t, value * spread_group(rstd[at, :]))


def matmul_cols(out, left, right, width):
    step = min(width, 256)
    for j in range(0, width, step):
        out[:, j : j + step] = product(left, right[:, j : j + step])


def fill_work(wk):
    half_a = lax.broadcasted_iota(jnp.int32, (LANES, LANES), 0) // PIX
    half_b = lax.broadcasted_iota(jnp.int32, (LANES, LANES), 1) // PIX
    wk.ones[...] = jnp.where(half_a == half_b, 1.0, 0.0).astype(f32)
    wk.masks = tap_masks()


def unpack_params(wk):
    tail = wk.ktp[:, KCOLS : KCOLS + LANES].astype(f32)
    for k in range(6):
        value = tail[:, k : k + 1] + tail[:, 8 + k : 9 + k] + tail[:, 16 + k : 17 + k]
        value = jnp.broadcast_to(value, (C, LANES))
        if k < 4:
            wk.gn[k] = value
        else:
            wk.rs[k - 4] = value


def turn_kernels(wk):
    for k in range(18):
        at = (k // 9) * FAN + (k % 9) * C
        wk.kb[k // 9, :, (k % 9) * C : (k % 9 + 1) * C] = wk.ktp[:, at : at + C].T


def cols(ref, width):
    return ref if width == ref.shape[1] else ref.at[:, :width]


def forward(wk, x_load, tiles, block_store):
    width = tiles * LANES
    norm_forward(wk, x_load, tiles, 0, wk.hat1, wk.rstd1, wk.hid1, wk.col)
    matmul_cols(wk.mid, wk.ktp[:, :FAN], cols(wk.col, width), width)
    norm_forward(
        wk,
        lambda t: wk.mid[:, lane_tile(t)],
        tiles,
        1,
        wk.hat2,
        wk.rstd2,
        wk.hid2,
        wk.col if block_store is not None else None,
    )
    if block_store is not None:
        matmul_cols(wk.mid, wk.ktp[:, FAN : 2 * FAN], cols(wk.col, width), width)

        @pl.loop(0, tiles)
        def _(t):
            block_store(t, x_load(t) + wk.mid[:, lane_tile(t)])


def backward_two(wk, cot_load, weight_load, tiles, grads):
    width = tiles * LANES

    @pl.loop(0, tiles)
    def _(t):
        store_taps((cot_load(t) * weight_load(t)).astype(bf16), wk.col, t, wk.masks, True)

    matmul_cols(wk.mid, wk.kb[1], cols(wk.col, width), width)
    for tap in range(9):
        grads[9 + tap] = product_nt(wk.col[tap * C : (tap + 1) * C, :width], wk.hid2[:, :width])


def backward_one(wk, tiles, grads, gn_out, part_store):
    width = tiles * LANES

    def emit_middle(t, value):
        store_taps(value.astype(bf16), wk.col, t, wk.masks, True)

    norm_backward(wk, wk.mid, tiles, 1, wk.hat2, wk.rstd2, emit_middle, wk.acc.at[1])
    matmul_cols(wk.mid, wk.kb[0], cols(wk.col, width), width)
    for tap in range(9):
        grads[tap] = product_nt(wk.col[tap * C : (tap + 1) * C, :width], wk.hid1[:, :width])
    norm_backward(wk, wk.mid, tiles, 0, wk.hat1, wk.rstd1, part_store, wk.acc.at[0])

    lane = lax.broadcasted_iota(jnp.int32, (1, LANES), 1)
    total = jnp.zeros((C, LANES), f32)
    for k in range(4):
        one = jnp.sum(wk.acc[k // 2, k % 2], axis=1, keepdims=True)
        total = total + jnp.where(lane == k, one, 0.0)
    gn_out[...] = total


def raw_gradient(wk, grads, sq):
    rows = 32

    @pl.loop(0, C // rows)
    def _(j):
        at = pl.ds(pl.multiple_of(j * rows, rows), rows)
        for conv in range(2):
            first = jnp.zeros((rows, C), f32)
            second = jnp.zeros((rows, C), f32)
            for tap in range(9):
                g = grads[conv * 9 + tap, at, :]
                k = wk.ktp[at, conv * FAN + tap * C : conv * FAN + (tap + 1) * C].astype(f32)
                first = first + g
                second = second + g * k
            first = jnp.sum(first, axis=1, keepdims=True) * (1.0 / FAN)
            second = jnp.sum(second, axis=1, keepdims=True)
            rs = wk.rs[conv, at, 0:1]
            squares = jnp.zeros((rows, C), f32)
            for tap in range(9):
                g = grads[conv * 9 + tap, at, :]
                k = wk.ktp[at, conv * FAN + tap * C : conv * FAN + (tap + 1) * C].astype(f32)
                value = (g - first - k * second) * rs
                grads[conv * 9 + tap, at, :] = value
                squares = squares + value * value
            fold = squares[:, :LANES] + squares[:, LANES:]
            sq[...] += fold.reshape(rows // 8, 8, LANES).sum(0)


def whole_sum(tile):
    return jnp.sum(jnp.sum(tile, axis=1, keepdims=True), axis=0, keepdims=True)


WORK_SCRATCH = [
    pltpu.VMEM((2, C, FAN), bf16),
    pltpu.VMEM((FAN, AUG * PIX), bf16),
    pltpu.VMEM((C, AUG * PIX), f32),
    pltpu.VMEM((C, AUG * PIX), f32),
    pltpu.VMEM((C, AUG * PIX), f32),
    pltpu.VMEM((C, AUG * PIX), bf16),
    pltpu.VMEM((C, AUG * PIX), bf16),
    pltpu.VMEM((LANES, LANES), f32),
    pltpu.VMEM((LANES, LANES), f32),
    pltpu.VMEM((LANES, LANES), f32),
    pltpu.VMEM((LANES, LANES), f32),
    pltpu.VMEM((LANES, LANES), f32),
    pltpu.VMEM((4, C, LANES), f32),
    pltpu.VMEM((2, C, LANES), f32),
    pltpu.VMEM((2, 2, C, LANES), f32),
]
WORK_NAMES = (
    "kb",
    "col",
    "mid",
    "hat1",
    "hat2",
    "hid1",
    "hid2",
    "stat",
    "stat2",
    "rstd1",
    "rstd2",
    "ones",
    "gn",
    "rs",
    "acc",
)


def make_work(ktp, refs):
    wk = Work()
    wk.ktp = ktp
    for name, ref in zip(WORK_NAMES, refs):
        setattr(wk, name, ref)
    return wk


def compute_kernel(
    x, cot, xt, ct, ktp, wl, sg, block, part, clipped, test, clipped_gn, test_gn, raw, raw_gn, length, *scratch
):
    examples = x.shape[0]
    wk = make_work(ktp, scratch[:-2])
    tgrad, sq = scratch[-2:]
    fill_work(wk)
    unpack_params(wk)
    turn_kernels(wk)
    forward(wk, lambda t: xt[...].astype(f32), 1, None)
    backward_two(wk, lambda t: ct[...].astype(f32), lambda t: sg[...], 1, tgrad)
    backward_one(wk, 1, tgrad, test_gn, None)
    raw_gradient(wk, tgrad, sq)

    @pl.loop(0, 18)
    def _(k):
        test[k] = tgrad[k].astype(bf16)

    sq[...] = jnp.zeros_like(sq)

    @pl.loop(0, examples)
    def _(e):
        def block_store(t, value):
            block[e, :, lane_tile(t)] = value.astype(bf16)

        def part_store(t, value):
            part[e, :, lane_tile(t)] = value.astype(bf16)

        forward(wk, lambda t: x[e, :, lane_tile(t)].astype(f32), 8, block_store)
        backward_two(
            wk,
            lambda t: cot[e, :, lane_tile(t)].astype(f32),
            lambda t: wl[e, :, lane_tile(t)],
            8,
            raw.at[e],
        )
        backward_one(wk, 8, raw.at[e], raw_gn.at[e], part_store)
        sq[...] = jnp.zeros_like(sq)
        raw_gradient(wk, raw.at[e], sq)
        gn = raw_gn[e]
        square = whole_sum(sq[...]) + whole_sum(gn * gn)
        length[e] = jnp.broadcast_to(jnp.sqrt(square), (8, LANES))

    factors = [CLIP / jnp.maximum(length[e][0:1, 0:1], CLIP) for e in range(examples)]
    total = factors[0] * raw_gn[0]
    for e in range(1, examples):
        total = total + factors[e] * raw_gn[e]
    clipped_gn[...] = total

    @pl.loop(0, 18)
    def _(k):
        total = factors[0] * raw[0, k]
        for e in range(1, examples):
            total = total + factors[e] * raw[e, k]
        clipped[k] = total.astype(bf16)


def compute(x, cot, xt, ct, ktp, wl, sg):
    examples = x.shape[0]
    out = jax.ShapeDtypeStruct
    shapes = (
        out(x.shape, bf16),
        out(x.shape, bf16),
        out((18, C, C), bf16),
        out((18, C, C), bf16),
        out((C, LANES), f32),
        out((C, LANES), f32),
        out((examples, 18, C, C), f32),
        out((examples, C, LANES), f32),
        out((examples, 8, LANES), f32),
    )
    spec = pl.BlockSpec(memory_space=pltpu.VMEM)
    return pl.pallas_call(
        compute_kernel,
        out_shape=shapes,
        in_specs=[spec] * 7,
        out_specs=(spec,) * 9,
        scratch_shapes=WORK_SCRATCH + [pltpu.VMEM((18, C, C), f32), pltpu.VMEM((8, LANES), f32)],
        compiler_params=pltpu.CompilerParams(vmem_limit_bytes=58 << 20),
    )(x, cot, xt, ct, ktp, wl, sg)


def peer_copy(src, dst, send, recv, **where):
    return pltpu.make_async_remote_copy(
        src_ref=src, dst_ref=dst, send_sem=send, recv_sem=recv, device_id=where, device_id_type=MESH
    )


def greet(peers):
    barrier = pltpu.get_barrier_semaphore()
    for where in peers:
        pl.semaphore_signal(barrier, inc=1, device_id=where, device_id_type=MESH)
    pl.semaphore_wait(barrier, len(peers))


class Exchange:
    def __init__(self, place, conv, gn, refs, sems):
        self.w, self.z, self.c, self.me = place
        self.conv, self.gn = conv, gn
        self.cb, self.cg, self.half, self.wb, self.quarter, self.zb = refs
        s_core, r_core, s_wide, r_wide, s_z, r_z = sems
        w, z, c = self.w, self.z, self.c
        sibling = self.me + 1 - 2 * c
        self.core = [
            peer_copy(conv.at[:, :, 1 - c], self.cb, s_core.at[0], r_core.at[0], narrow=sibling),
            peer_copy(gn.at[:, 1 - c], self.cg, s_core.at[1], r_core.at[1], narrow=sibling),
        ]
        self.wide, self.line = [], []
        for k in range(1, 4):
            to = lax.rem(w + k, 4)
            self.wide.append(
                peer_copy(self.half.at[to], self.wb.at[k - 1], s_wide.at[k - 1], r_wide.at[k - 1], wide=to)
            )
        for k in range(1, 4):
            to = lax.rem(z + k, 4)
            self.line.append(
                peer_copy(
                    self.quarter.at[:, to], self.zb.at[k - 1], s_z.at[k - 1], r_z.at[k - 1], narrow=to * 2 + c
                )
            )

    def start_core(self):
        for copy in self.core:
            copy.start()

    def start_wide(self):
        for copy in self.core:
            copy.wait()
        half, c = self.half, self.c
        for k in range(2):

            @pl.loop(0, 9)
            def _(tap):
                total = self.conv[k * 9 + tap, :, c].astype(f32) + self.cb[k * 9 + tap].astype(f32)
                half[k * 2, tap] = total[:, :, :LANES].astype(bf16)
                half[k * 2 + 1, tap] = total[:, :, LANES:].astype(bf16)

        half[0, 9] = (self.gn[:, c].astype(f32) + self.cg[...].astype(f32)).astype(bf16)
        for q in range(1, 4):
            half[q, 9] = jnp.zeros_like(half[q, 9])
        for copy in self.wide:
            copy.start()

    def start_line(self):
        for copy in self.wide:
            copy.wait()

        @pl.loop(0, 10)
        def _(tap):
            total = self.half[self.w, tap].astype(f32)
            for k in range(3):
                total = total + self.wb[k, tap].astype(f32)
            self.quarter[tap] = total.astype(bf16)

        for copy in self.line:
            copy.start()

    def finish(self, out):
        for copy in self.line:
            copy.wait()

        @pl.loop(0, 10)
        def _(tap):
            total = self.quarter[tap, self.z].astype(f32)
            for k in range(3):
                total = total + self.zb[k, tap].astype(f32)
            out[tap] = total.astype(bf16)


def start_all(copies):
    for copy in copies:
        copy.start()


def wait_all(copies):
    for copy in copies:
        copy.wait()


def mega_kernel(images, cots, timg, tcot, kshard, wl, sg, ob, op, red, figures, *scratch):
    n = 8
    me = lax.axis_index("narrow")
    w = lax.axis_index("wide")
    z, c = me // 2, me % 2
    sibling = me + 1 - 2 * c
    examples = images.shape[0] // n
    chans = images.shape[1]
    mine = pl.ds(pl.multiple_of(me * chans, chans), chans)
    work, rest = scratch[: len(WORK_SCRATCH)], scratch[len(WORK_SCRATCH) :]
    x, cot, xt, ct, ktp, block, part, raw, raw_gn, length, tgrad, tgn, sq = rest[:13]
    s_conv, s_gn, t_conv, t_gn, dt = rest[13:18]
    s_refs, t_refs = rest[18:24], rest[24:30]
    s_sems, t_sems = rest[30:36], rest[36:42]
    s_in, r_in, s_up, r_up, s_dn, r_dn, s_core, r_core, s_loc = rest[42:51]
    s_out, r_out, s_fin, r_fin, s_fig, r_fig = rest[51:57]
    greet(
        [{"narrow": lax.rem(me + k, n)} for k in range(1, n)]
        + [{"wide": lax.rem(w + k, 4)} for k in range(1, 4)]
    )

    def rows(zz):
        return pl.ds(pl.multiple_of((zz * 2 + c) * chans, chans), chans)

    def up(step):
        src = kshard if step == 0 else ktp.at[rows(z - step)]
        return peer_copy(src, ktp.at[rows(z - step)], s_up.at[step], r_up.at[step], narrow=me + 2)

    def down(step):
        src = kshard if step == 0 else ktp.at[rows(z + step)]
        return peer_copy(src, ktp.at[rows(z + step)], s_dn.at[step], r_dn.at[step], narrow=me - 2)

    def across(slot, zz):
        src = kshard if slot == 0 else ktp.at[rows(zz)]
        return peer_copy(src, ktp.at[rows(zz)], s_core.at[slot], r_core.at[slot], narrow=sibling)

    def spread(a, src, dst, cut):
        copies = []
        for k in range(n):
            to = lax.rem(me + k, n)
            if k == 0:
                copies.append(pltpu.make_async_copy(cut(src, to), dst, s_loc.at[a]))
            else:
                copies.append(peer_copy(cut(src, to), dst, s_in.at[a, k - 1], r_in.at[a, k - 1], narrow=to))
        return copies

    def test_cut(src, to):
        return src.at[:, pl.ds(pl.multiple_of(to * LANES, LANES), LANES)]

    def example_cut(e):
        return lambda src, to: src.at[to * examples + e]

    def give_back(a, e, src, dst):
        copies = []
        for k in range(n):
            to = lax.rem(me + k, n)
            piece = src.at[e, pl.ds(pl.multiple_of(to * chans, chans), chans)]
            place = dst.at[me * examples + e]
            slot = a * examples + e
            if k == 0:
                copies.append(pltpu.make_async_copy(piece, place, s_loc.at[6 + slot]))
            else:
                copies.append(peer_copy(piece, place, s_out.at[slot, k - 1], r_out.at[slot, k - 1], narrow=to))
        return copies

    own_k = pltpu.make_async_copy(kshard, ktp.at[mine], s_loc.at[10])
    in_test = spread(0, timg, xt.at[mine], test_cut) + spread(1, tcot, ct.at[mine], test_cut)
    in_x = [spread(2 + 2 * e, images, x.at[e, mine], example_cut(e)) for e in range(examples)]
    in_cot = [spread(3 + 2 * e, cots, cot.at[e, mine], example_cut(e)) for e in range(examples)]
    out_block = [give_back(0, e, block, ob) for e in range(examples)]
    out_part = [give_back(1, e, part, op) for e in range(examples)]

    @pl.when(z < 3)
    def _():
        up(0).start()

    @pl.when(z > 0)
    def _():
        down(0).start()

    across(0, z).start()
    own_k.start()
    start_all(in_test)
    start_all(in_x[0])
    wk = make_work(ktp, work)
    fill_work(wk)
    for step in range(1, 4):

        @pl.when(z - step >= 0)
        def _():
            up(step - 1).wait_recv()
            across(step, z - step).start()
            if step < 3:

                @pl.when(z < 3)
                def _():
                    up(step).start()

        @pl.when(z + step <= 3)
        def _():
            down(step - 1).wait_recv()
            across(3 + step, z + step).start()
            if step < 3:

                @pl.when(z > 0)
                def _():
                    down(step).start()

    for step in range(3):

        @pl.when((z < 3) & (z - step >= 0))
        def _():
            up(step).wait_send()

        @pl.when((z > 0) & (z + step <= 3))
        def _():
            down(step).wait_send()

    across(0, z).wait()
    for step in range(1, 4):

        @pl.when(z - step >= 0)
        def _():
            across(step, z - step).wait()

        @pl.when(z + step <= 3)
        def _():
            across(3 + step, z + step).wait()

    own_k.wait()
    start_all(in_cot[0])
    unpack_params(wk)
    turn_kernels(wk)
    wait_all(in_test)

    place = (w, z, c, me)
    direction = Exchange(place, t_conv, t_gn, t_refs, t_sems)
    clipped = Exchange(place, s_conv, s_gn, s_refs, s_sems)
    forward(wk, lambda t: xt[...].astype(f32), 1, None)
    backward_two(wk, lambda t: ct[...].astype(f32), lambda t: sg[me], 1, tgrad)
    backward_one(wk, 1, tgrad, tgn, None)
    raw_gradient(wk, tgrad, sq)

    @pl.loop(0, 18)
    def _(k):
        t_conv[k] = tgrad[k].astype(bf16).reshape(4, 2, chans, C)

    t_gn[...] = tgn[...].astype(bf16).reshape(4, 2, chans, LANES)
    direction.start_core()

    own = dt.at[c, w, z]
    line_ag, wide_ag = [], []
    for k in range(1, 4):
        to = lax.rem(z + k, 4)
        line_ag.append(peer_copy(own, own, s_fin.at[0, k - 1], r_fin.at[0, k - 1], narrow=to * 2 + c))
    for k in range(1, 4):
        to = lax.rem(w + k, 4)
        wide_ag.append(
            peer_copy(dt.at[c, w], dt.at[c, w], s_fin.at[1, k - 1], r_fin.at[1, k - 1], wide=to)
        )
    core_ag = peer_copy(dt.at[c], dt.at[c], s_fin.at[2, 0], r_fin.at[2, 0], narrow=sibling)

    def after_forward(e):
        if e == 0:
            direction.start_wide()
        else:
            wait_all(line_ag)
            start_all(wide_ag)

    def between(e):
        if e == 0:
            direction.start_line()
        else:
            wait_all(wide_ag)
            core_ag.start()

    def after_backward(e):
        if e == 0:
            direction.finish(own)
            start_all(line_ag)

    for e in range(examples):
        wait_all(in_x[e])
        if e + 1 < examples:
            start_all(in_x[e + 1])

        def block_store(t, value):
            block[e, :, lane_tile(t)] = value.astype(bf16)

        def part_store(t, value):
            part[e, :, lane_tile(t)] = value.astype(bf16)

        forward(wk, lambda t: x[e, :, lane_tile(t)].astype(f32), 8, block_store)
        start_all(out_block[e])
        after_forward(e)
        wait_all(in_cot[e])
        if e + 1 < examples:
            start_all(in_cot[e + 1])
        backward_two(
            wk,
            lambda t: cot[e, :, lane_tile(t)].astype(f32),
            lambda t: wl[me * examples + e, :, lane_tile(t)],
            8,
            raw.at[e],
        )
        between(e)
        backward_one(wk, 8, raw.at[e], raw_gn.at[e], part_store)
        start_all(out_part[e])
        after_backward(e)
        sq[...] = jnp.zeros_like(sq)
        raw_gradient(wk, raw.at[e], sq)
        gn = raw_gn[e]
        square = whole_sum(sq[...]) + whole_sum(gn * gn)
        length[e] = jnp.broadcast_to(jnp.sqrt(square), (8, LANES))

    factors = [CLIP / jnp.maximum(length[e][0:1, 0:1], CLIP) for e in range(examples)]
    total = factors[0] * raw_gn[0]
    for e in range(1, examples):
        total = total + factors[e] * raw_gn[e]
    s_gn[...] = total.astype(bf16).reshape(4, 2, chans, LANES)

    @pl.loop(0, 18)
    def _(k):
        total = factors[0] * raw[0, k]
        for e in range(1, examples):
            total = total + factors[e] * raw[e, k]
        s_conv[k] = total.astype(bf16).reshape(4, 2, chans, C)

    clipped.start_core()
    core_ag.wait()
    clipped.start_wide()
    inner_products(dt, raw, raw_gn, length, figures, me, chans)
    figs = []
    for k in range(1, n):
        to = lax.rem(me + k, n)
        figs.append(peer_copy(figures.at[me], figures.at[me], s_fig.at[k - 1], r_fig.at[k - 1], narrow=to))
    start_all(figs)
    clipped.start_line()
    clipped.finish(red.at[w])
    finals = []
    for k in range(1, 4):
        to = lax.rem(w + k, 4)
        finals.append(peer_copy(red.at[w], red.at[w], s_fin.at[3, k - 1], r_fin.at[3, k - 1], wide=to))
    start_all(finals)
    for e in range(examples):
        wait_all(out_block[e])
        wait_all(out_part[e])
    wait_all(figs)
    wait_all(finals)


def inner_products(dt, raw, raw_gn, length, figures, me, chans):
    examples = raw.shape[0]
    zero = jnp.zeros((chans, LANES), f32)

    def visit(index, carry):
        q, rest = index // 8, index % 8
        at = pl.ds(pl.multiple_of(rest * chans, chans), chans)
        lanes = pl.ds(pl.multiple_of((q % 2) * LANES, LANES), LANES)
        square = carry[0]
        sums = list(carry[1:])
        for tap in range(9):
            d = dt[rest % 2, q, rest // 2, tap].astype(f32)
            square = square + d * d
            for e in range(examples):
                sums[e] = sums[e] + d * raw[e, (q // 2) * 9 + tap, at, lanes]
        return (square, *sums)

    totals = lax.fori_loop(0, 32, visit, (zero,) * (examples + 1))

    def visit_gn(rest, carry):
        at = pl.ds(pl.multiple_of(rest * chans, chans), chans)
        d = dt[rest % 2, 0, rest // 2, 9].astype(f32)
        return (carry[0] + d * d,) + tuple(carry[1 + e] + d * raw_gn[e, at, :] for e in range(examples))

    totals = lax.fori_loop(0, 8, visit_gn, totals)
    dir_sq = whole_sum(totals[0])
    params = 18 * C * C + 4 * C
    top = lax.broadcasted_iota(jnp.int32, (8, LANES), 0)
    for e in range(examples):
        size = length[e]
        factor = CLIP / jnp.maximum(size, CLIP)
        influence = factor * whole_sum(totals[1 + e]) * math.sqrt(params) / (CLIP * jnp.sqrt(dir_sq + 1e-06))
        figures[me, e] = jnp.where(top == 0, size, influence)


def mega(images, cots, timg, tcot, kshard, wl, sg):
    held, chans = images.shape[0], images.shape[1]
    examples = held // 8
    out = jax.ShapeDtypeStruct
    anyspace = pl.BlockSpec(memory_space=pl.ANY)
    vmem = pl.BlockSpec(memory_space=pltpu.VMEM)
    dma = pltpu.SemaphoreType.DMA
    exchange = [
        pltpu.VMEM((18, 4, chans, C), bf16),
        pltpu.VMEM((4, chans, LANES), bf16),
        pltpu.VMEM((4, 10, 4, chans, LANES), bf16),
        pltpu.VMEM((3, 10, 4, chans, LANES), bf16),
        pltpu.VMEM((10, 4, chans, LANES), bf16),
        pltpu.VMEM((3, 10, chans, LANES), bf16),
    ]
    sems = [dma((2,)), dma((2,)), dma((3,)), dma((3,)), dma((3,)), dma((3,))]
    scratch = [
        pltpu.VMEM((examples, C, AUG * PIX), bf16),
        pltpu.VMEM((examples, C, AUG * PIX), bf16),
        pltpu.VMEM((C, LANES), bf16),
        pltpu.VMEM((C, LANES), bf16),
        pltpu.VMEM((C, KCOLS + LANES), bf16),
        pltpu.VMEM((examples, C, AUG * PIX), bf16),
        pltpu.VMEM((examples, C, AUG * PIX), bf16),
        pltpu.VMEM((examples, 18, C, C), f32),
        pltpu.VMEM((examples, C, LANES), f32),
        pltpu.VMEM((examples, 8, LANES), f32),
        pltpu.VMEM((18, C, C), f32),
        pltpu.VMEM((C, LANES), f32),
        pltpu.VMEM((8, LANES), f32),
        pltpu.VMEM((18, 4, 2, chans, C), bf16),
        pltpu.VMEM((4, 2, chans, LANES), bf16),
        pltpu.VMEM((18, 4, 2, chans, C), bf16),
        pltpu.VMEM((4, 2, chans, LANES), bf16),
        pltpu.VMEM((2, 4, 4, 10, chans, LANES), bf16),
    ]
    kinds = 2 + 2 * examples
    moves = [
        dma((kinds, 7)),
        dma((kinds, 7)),
        dma((3,)),
        dma((3,)),
        dma((3,)),
        dma((3,)),
        dma((7,)),
        dma((7,)),
        dma((11,)),
        dma((2 * examples, 7)),
        dma((2 * examples, 7)),
        dma((4, 3)),
        dma((4, 3)),
        dma((7,)),
        dma((7,)),
    ]
    return pl.pallas_call(
        mega_kernel,
        out_shape=(
            out((held, chans, AUG * PIX), bf16),
            out((held, chans, AUG * PIX), bf16),
            out((4, 10, chans, LANES), bf16),
            out((8, examples, 8, LANES), f32),
        ),
        in_specs=[anyspace] * 5 + [vmem] * 2,
        out_specs=(anyspace, anyspace, vmem, vmem),
        scratch_shapes=WORK_SCRATCH + scratch + exchange + exchange + sems + sems + moves,
        compiler_params=pltpu.CompilerParams(collective_id=0, has_side_effects=True, vmem_limit_bytes=60 << 20),
    )(images, cots, timg, tcot, kshard, wl, sg)


def pieces(v):
    high = lax.reduce_precision(v, 8, 7)
    rest = v - high
    mid = lax.reduce_precision(rest, 8, 7)
    low = rest - mid
    return high.astype(bf16), mid.astype(bf16), low.astype(bf16)


def kernel_rows(conv_weight, gn_params):
    chans = conv_weight.shape[4]
    centre = conv_weight - jnp.mean(conv_weight, axis=(1, 2, 3), keepdims=True)
    spread = jnp.mean(centre * centre, axis=(1, 2, 3), keepdims=True)
    scale = lax.rsqrt(FAN * spread + 1e-06)
    kernels = (centre * scale).astype(bf16).reshape(2, FAN, chans)
    rows = kernels.transpose(2, 0, 1).reshape(chans, KCOLS)
    small = jnp.concatenate([gn_params.T, scale.reshape(2, chans).T, jnp.zeros((chans, 2), f32)], 1)
    tail = jnp.concatenate(list(pieces(small)) + [jnp.zeros((chans, LANES - 24), bf16)], 1)
    return jnp.concatenate([rows, tail], 1)


def adamw(weight, first, second, grad, correction, rate, decay):
    first_new = 0.5 * first + 0.5 * grad
    second_new = 0.5 * second + 0.5 * grad * grad
    update = first_new / correction / (jnp.sqrt(second_new / correction) + 1e-08)
    return (weight - rate * (update + decay * weight), first_new, second_new)


def plain_gather(images, cots, timg, tcot, kshard, narrow):
    share = narrow // 8
    x = lax.all_to_all(images, "narrow", 0, 1, tiled=True)
    cot = lax.all_to_all(cots, "narrow", 0, 1, tiled=True)
    ktp = lax.all_gather(kshard, "narrow", axis=0, tiled=True)
    own = (lax.axis_index("narrow") // share) * LANES

    def pick(v):
        return lax.dynamic_slice_in_dim(lax.all_gather(v, "narrow", axis=0, tiled=True), own, LANES, 1)

    return x, cot, pick(timg), pick(tcot), ktp


def plain_reduce(block, part, clip_conv, test_conv, clip_gn, test_gn, raw, raw_gn, length, chans):
    examples = block.shape[0]
    ob = lax.all_to_all(block, "narrow", 1, 0, tiled=True)
    op = lax.all_to_all(part, "narrow", 1, 0, tiled=True)
    own = lax.axis_index("narrow") * chans
    rows = lax.psum(clip_conv, ("wide", "narrow"))
    rows = lax.dynamic_slice_in_dim(rows, own, chans, 1)
    gn_rows = lax.dynamic_slice_in_dim(lax.psum(clip_gn.astype(bf16), ("wide", "narrow")), own, chans, 0)
    red = rows.reshape(2, 9, chans, 2, LANES).transpose(0, 3, 1, 2, 4).reshape(4, 9, chans, LANES)
    red = jnp.concatenate([red, jnp.broadcast_to(gn_rows, (4, 1, chans, LANES))], 1)
    d = lax.psum(test_conv, ("wide", "narrow")).astype(f32)
    d_gn = lax.psum(test_gn.astype(bf16), ("wide", "narrow")).astype(f32)
    dir_sq = jnp.sum(d * d) + jnp.sum(d_gn * d_gn)
    inner = jnp.sum(raw * d, axis=(1, 2, 3)) + jnp.sum(raw_gn * d_gn, axis=(1, 2))
    size = length[:, 0, 0]
    factor = CLIP / jnp.maximum(size, CLIP)
    influence = factor * inner * math.sqrt(18 * C * C + 4 * C) / (CLIP * jnp.sqrt(dir_sq + 1e-06))
    figures = lax.all_gather(jnp.stack([size, influence], 1), "narrow", axis=0)
    return ob, op, red, figures[:, :, :, None]


def local(
    images,
    cotangent,
    test_images,
    test_cotangent,
    pair_index,
    example_count,
    aug_count,
    conv_weight,
    gn_params,
    conv_moment1,
    conv_moment2,
    gn_moment1,
    gn_moment2,
    noise_conv,
    noise_gn,
    step_count,
):
    n_wide, narrow = lax.axis_size("wide"), lax.axis_size("narrow")
    held, chans = images.shape[0], images.shape[1]
    examples = held // narrow
    share = narrow // 8
    me = lax.axis_index("narrow")
    slots = jnp.arange(AUG, dtype=jnp.int32)
    live = jnp.arange(held, dtype=jnp.int32) < example_count[0]
    weights = jnp.where(
        live[:, None] & (slots[None, :] < aug_count[:, None]),
        1.0 / aug_count.astype(f32)[:, None],
        f32(0.0),
    )
    pixels = jnp.repeat(weights, PIX, axis=1)
    pairs = pair_index % AUG
    signs = jnp.sum((pairs[:, 0:1] == slots[None, :]).astype(f32), 0) - jnp.sum(
        (pairs[:, 1:2] == slots[None, :]).astype(f32), 0
    )
    sign_pixels = jnp.repeat(signs, PIX).reshape(8, LANES) * (1.0 / share)
    kshard = kernel_rows(conv_weight, gn_params)
    timg, tcot = test_images[0], test_cotangent[0]
    direct = n_wide == 4 and narrow == 8
    if direct:
        block_out, op, red, figures = mega(
            images, cotangent, timg, tcot, kshard, pixels[:, None, :], sign_pixels[:, None, :]
        )
    else:
        wl = lax.dynamic_slice_in_dim(pixels, me * examples, examples, 0)[:, None, :]
        sg = lax.dynamic_slice_in_dim(sign_pixels, me // share, 1, 0)
        x, cot, xt, ct, ktp = plain_gather(images, cotangent, timg, tcot, kshard, narrow)
        parts = compute(x, cot, xt, ct, ktp, wl, sg)
        block_out, op, red, figures = plain_reduce(*parts, chans)
    input_grad = cotangent.astype(f32) * pixels[:, None, :] + op.astype(f32)
    lengths = figures[:, :, 0, 0].reshape(held)
    influence = figures[:, :, 1, 0].reshape(held)
    sum_conv = red[:, :9].reshape(2, 2, 9, chans, LANES).transpose(0, 2, 1, 4, 3)
    sum_conv = sum_conv.reshape(2, 3, 3, C, chans).astype(f32)
    sum_norm = red[0, 9, :, :4].T.astype(f32)
    total = held * n_wide
    noisy_conv = (sum_conv + math.sqrt(total) * noise_conv) / total
    noisy_norm = (sum_norm + math.sqrt(total) * noise_gn) / total
    correction = 1.0 - jnp.power(f32(0.5), step_count[0].astype(f32))
    conv_new, conv_first, conv_second = adamw(
        conv_weight, conv_moment1, conv_moment2, noisy_conv, correction, 1.0 / math.sqrt(9 * C), 0.1
    )
    gn_new, gn_first, gn_second = adamw(
        gn_params, gn_moment1, gn_moment2, noisy_norm, correction, 0.1, 0.0
    )
    return (
        block_out,
        input_grad,
        lengths,
        influence,
        conv_new,
        conv_new.astype(bf16),
        conv_first,
        conv_second,
        gn_new,
        gn_first,
        gn_second,
    )


def solution(mesh):
    in_specs = (
        P("wide", "narrow", None),
        P("wide", "narrow", None),
        P("wide", "narrow", None),
        P("wide", "narrow", None),
        P("wide", None),
        P("wide"),
        P("wide"),
        P(None, None, None, None, "narrow"),
        P(None, "narrow"),
        P(None, None, None, None, "narrow"),
        P(None, None, None, None, "narrow"),
        P(None, "narrow"),
        P(None, "narrow"),
        P(None, None, None, None, "narrow"),
        P(None, "narrow"),
        P(),
    )
    out_specs = (
        P("wide", "narrow", None),
        P("wide", "narrow", None),
        P("wide"),
        P("wide"),
        P(None, None, None, None, "narrow"),
        P(None, None, None, None, "narrow"),
        P(None, None, None, None, "narrow"),
        P(None, None, None, None, "narrow"),
        P(None, "narrow"),
        P(None, "narrow"),
        P(None, "narrow"),
    )
    return jax.shard_map(local, mesh=mesh, in_specs=in_specs, out_specs=out_specs, check_vma=False)
```

```python
import functools
import math

import jax
import jax.numpy as jnp
from jax import lax
from jax.experimental import pallas as pl
from jax.experimental.pallas import tpu as pltpu
from jax.sharding import PartitionSpec as P

C = 256
MAP = 8
GROUPS = 16
AUG = 16
PIX = MAP * MAP
FAN = 9 * C
LANES = 128
CLIP = 6.0 * C
MESH = pl.DeviceIdType.MESH
f32 = jnp.float32
bf16 = jnp.bfloat16
KCOLS = 2 * FAN


def lane_tile(index):
    return pl.ds(pl.multiple_of(index * LANES, LANES), LANES)


def group_sum(tile):
    return tile.reshape(GROUPS, C // GROUPS, LANES).sum(1)


def spread_group(rows):
    return jnp.broadcast_to(rows[:, None, :], (GROUPS, C // GROUPS, LANES)).reshape(C, LANES)


def image_sum(rows, ones):
    return lax.dot_general(
        rows,
        ones,
        (((1,), (0,)), ((), ())),
        precision=lax.Precision.HIGHEST,
        preferred_element_type=f32,
    )


def sigmoid(z):
    return 0.5 * jnp.tanh(0.5 * z) + 0.5


def tap_masks():
    lane = lax.broadcasted_iota(jnp.int32, (1, LANES), 1)
    row = (lane // MAP) % MAP
    col = lane % MAP
    masks = []
    for r in (-1, 0, 1):
        for c in (-1, 0, 1):
            ok = (row + r >= 0) & (row + r < MAP) & (col + c >= 0) & (col + c < MAP)
            masks.append(jnp.where(ok, 1.0, 0.0).astype(f32).astype(bf16))
    return masks


def store_taps(value, col_ref, t, masks, flip):
    for tap in range(9):
        shift = (tap // 3 - 1) * MAP + (tap % 3 - 1)
        if shift == 0:
            moved = value
        else:
            moved = pltpu.roll(value, (-shift) % LANES, 1) * masks[tap]
        place = 8 - tap if flip else tap
        col_ref[place * C : (place + 1) * C, lane_tile(t)] = moved


def product(a, b):
    return jnp.dot(a, b, preferred_element_type=f32)


def product_nt(a, b):
    return lax.dot_general(a, b, (((1,), (1,)), ((), ())), preferred_element_type=f32)


class Work:
    pass


def norm_forward(wk, load, tiles, which, hat, rstd, hidden, col):
    stat = wk.stat

    @pl.loop(0, tiles)
    def _(t):
        stat[pl.ds(pl.multiple_of(t * GROUPS, GROUPS), GROUPS), :] = group_sum(load(t))

    rows = tiles * GROUPS
    stat[:rows, :] = image_sum(stat[:rows, :], wk.ones[...]) * (1.0 / (PIX * C // GROUPS))

    @pl.loop(0, tiles)
    def _(t):
        at = pl.ds(pl.multiple_of(t * GROUPS, GROUPS), GROUPS)
        centre = load(t) - spread_group(stat[at, :])
        hat[:, lane_tile(t)] = centre
        stat[at, :] = group_sum(centre * centre)

    spread = image_sum(stat[:rows, :], wk.ones[...]) * (1.0 / (PIX * C // GROUPS))
    rstd[:rows, :] = lax.rsqrt(spread + 1e-05)

    @pl.loop(0, tiles)
    def _(t):
        at = pl.ds(pl.multiple_of(t * GROUPS, GROUPS), GROUPS)
        normed = hat[:, lane_tile(t)] * spread_group(rstd[at, :])
        hat[:, lane_tile(t)] = normed
        scaled = normed * wk.gn[2 * which] + wk.gn[2 * which + 1]
        act = (scaled * sigmoid(scaled)).astype(bf16)
        hidden[:, lane_tile(t)] = act
        if col is not None:
            store_taps(act, col, t, wk.masks, False)


def norm_backward(wk, grad, tiles, which, hat, rstd, emit, acc):
    stat, stat2 = wk.stat, wk.stat2
    acc[0] = jnp.zeros((C, LANES), f32)
    acc[1] = jnp.zeros((C, LANES), f32)

    @pl.loop(0, tiles)
    def _(t):
        at = pl.ds(pl.multiple_of(t * GROUPS, GROUPS), GROUPS)
        normed = hat[:, lane_tile(t)]
        scaled = normed * wk.gn[2 * which] + wk.gn[2 * which + 1]
        gate = sigmoid(scaled)
        inner = grad[:, lane_tile(t)] * gate * (1.0 + scaled * (1.0 - gate))
        acc[0] += inner * normed
        acc[1] += inner
        inner = inner * wk.gn[2 * which]
        grad[:, lane_tile(t)] = inner
        stat[at, :] = group_sum(inner)
        stat2[at, :] = group_sum(inner * normed)

    if emit is not None:
        rows = tiles * GROUPS
        scale = 1.0 / (PIX * C // GROUPS)
        stat[:rows, :] = image_sum(stat[:rows, :], wk.ones[...]) * scale
        stat2[:rows, :] = image_sum(stat2[:rows, :], wk.ones[...]) * scale

        @pl.loop(0, tiles)
        def _(t):
            at = pl.ds(pl.multiple_of(t * GROUPS, GROUPS), GROUPS)
            value = grad[:, lane_tile(t)] - spread_group(stat[at, :])
            value = value - hat[:, lane_tile(t)] * spread_group(stat2[at, :])
            emit(t, value * spread_group(rstd[at, :]))


def matmul_cols(out, left, right, width):
    step = min(width, 256)
    for j in range(0, width, step):
        out[:, j : j + step] = product(left, right[:, j : j + step])


def fill_work(wk):
    half_a = lax.broadcasted_iota(jnp.int32, (LANES, LANES), 0) // PIX
    half_b = lax.broadcasted_iota(jnp.int32, (LANES, LANES), 1) // PIX
    wk.ones[...] = jnp.where(half_a == half_b, 1.0, 0.0).astype(f32)
    wk.masks = tap_masks()


def unpack_params(wk, tail):
    tail = tail.astype(f32)
    for k in range(6):
        value = tail[:, k : k + 1] + tail[:, 8 + k : 9 + k] + tail[:, 16 + k : 17 + k]
        value = jnp.broadcast_to(value, (C, LANES))
        if k < 4:
            wk.gn[k] = value
        else:
            wk.rs[k - 4] = value


def turn_kernel(wk, conv):
    for tap in range(9):
        wk.kb[conv, :, tap * C : (tap + 1) * C] = wk.kf[conv, :, tap * C : (tap + 1) * C].T


def cols(ref, width):
    return ref if width == ref.shape[1] else ref.at[:, :width]


def forward(wk, x_load, tiles, block_store, early=None):
    width = tiles * LANES
    norm_forward(wk, x_load, tiles, 0, wk.hat1, wk.rstd1, wk.hid1, wk.col)
    if early is not None:
        early()
    matmul_cols(wk.mid, wk.kf[0], cols(wk.col, width), width)
    norm_forward(
        wk,
        lambda t: wk.mid[:, lane_tile(t)],
        tiles,
        1,
        wk.hat2,
        wk.rstd2,
        wk.hid2,
        wk.col if block_store is not None else None,
    )
    if block_store is not None:
        matmul_cols(wk.mid, wk.kf[1], cols(wk.col, width), width)

        @pl.loop(0, tiles)
        def _(t):
            block_store(t, x_load(t) + wk.mid[:, lane_tile(t)])


def backward_two(wk, cot_load, weight_load, tiles, grads):
    width = tiles * LANES

    @pl.loop(0, tiles)
    def _(t):
        store_taps((cot_load(t) * weight_load(t)).astype(bf16), wk.col, t, wk.masks, True)

    matmul_cols(wk.mid, wk.kb[1], cols(wk.col, width), width)
    for tap in range(9):
        grads[9 + tap] = product_nt(wk.col[tap * C : (tap + 1) * C, :width], wk.hid2[:, :width])


def backward_one(wk, tiles, grads, gn_out, part_store):
    width = tiles * LANES

    def emit_middle(t, value):
        store_taps(value.astype(bf16), wk.col, t, wk.masks, True)

    norm_backward(wk, wk.mid, tiles, 1, wk.hat2, wk.rstd2, emit_middle, wk.acc.at[1])
    matmul_cols(wk.mid, wk.kb[0], cols(wk.col, width), width)
    for tap in range(9):
        grads[tap] = product_nt(wk.col[tap * C : (tap + 1) * C, :width], wk.hid1[:, :width])
    norm_backward(wk, wk.mid, tiles, 0, wk.hat1, wk.rstd1, part_store, wk.acc.at[0])

    lane = lax.broadcasted_iota(jnp.int32, (1, LANES), 1)
    total = jnp.zeros((C, LANES), f32)
    for k in range(4):
        one = jnp.sum(wk.acc[k // 2, k % 2], axis=1, keepdims=True)
        total = total + jnp.where(lane == k, one, 0.0)
    gn_out[...] = total


def raw_gradient(wk, grads, sq):
    rows = 32

    @pl.loop(0, C // rows)
    def _(j):
        at = pl.ds(pl.multiple_of(j * rows, rows), rows)
        for conv in range(2):
            first = jnp.zeros((rows, C), f32)
            second = jnp.zeros((rows, C), f32)
            for tap in range(9):
                g = grads[conv * 9 + tap, at, :]
                k = wk.kf[conv, at, tap * C : (tap + 1) * C].astype(f32)
                first = first + g
                second = second + g * k
            first = jnp.sum(first, axis=1, keepdims=True) * (1.0 / FAN)
            second = jnp.sum(second, axis=1, keepdims=True)
            rs = wk.rs[conv, at, 0:1]
            squares = jnp.zeros((rows, C), f32)
            for tap in range(9):
                g = grads[conv * 9 + tap, at, :]
                k = wk.kf[conv, at, tap * C : (tap + 1) * C].astype(f32)
                value = (g - first - k * second) * rs
                grads[conv * 9 + tap, at, :] = value
                squares = squares + value * value
            fold = squares[:, :LANES] + squares[:, LANES:]
            sq[...] += fold.reshape(rows // 8, 8, LANES).sum(0)


def whole_sum(tile):
    return jnp.sum(jnp.sum(tile, axis=1, keepdims=True), axis=0, keepdims=True)


WORK_SCRATCH = [
    pltpu.VMEM((2, C, FAN), bf16),
    pltpu.VMEM((2, C, FAN), bf16),
    pltpu.VMEM((FAN, AUG * PIX), bf16),
    pltpu.VMEM((C, AUG * PIX), f32),
    pltpu.VMEM((C, AUG * PIX), f32),
    pltpu.VMEM((C, AUG * PIX), f32),
    pltpu.VMEM((C, AUG * PIX), bf16),
    pltpu.VMEM((C, AUG * PIX), bf16),
    pltpu.VMEM((LANES, LANES), f32),
    pltpu.VMEM((LANES, LANES), f32),
    pltpu.VMEM((LANES, LANES), f32),
    pltpu.VMEM((LANES, LANES), f32),
    pltpu.VMEM((LANES, LANES), f32),
    pltpu.VMEM((4, C, LANES), f32),
    pltpu.VMEM((2, C, LANES), f32),
    pltpu.VMEM((2, 2, C, LANES), f32),
]
WORK_NAMES = (
    "kf",
    "kb",
    "col",
    "mid",
    "hat1",
    "hat2",
    "hid1",
    "hid2",
    "stat",
    "stat2",
    "rstd1",
    "rstd2",
    "ones",
    "gn",
    "rs",
    "acc",
)


def make_work(refs):
    wk = Work()
    for name, ref in zip(WORK_NAMES, refs):
        setattr(wk, name, ref)
    return wk


def compute_kernel(
    x, cot, xt, ct, ktp, wl, sg, block, part, clipped, test, clipped_gn, test_gn, raw, raw_gn, length, *scratch
):
    examples = x.shape[0]
    wk = make_work(scratch[:-2])
    tgrad, sq = scratch[-2:]
    fill_work(wk)
    unpack_params(wk, ktp[:, KCOLS : KCOLS + LANES])
    for conv in range(2):
        wk.kf[conv] = ktp[:, conv * FAN : (conv + 1) * FAN]
        turn_kernel(wk, conv)
    forward(wk, lambda t: xt[...].astype(f32), 1, None)
    backward_two(wk, lambda t: ct[...].astype(f32), lambda t: sg[...], 1, tgrad)
    backward_one(wk, 1, tgrad, test_gn, None)
    raw_gradient(wk, tgrad, sq)

    @pl.loop(0, 18)
    def _(k):
        test[k] = tgrad[k].astype(bf16)

    sq[...] = jnp.zeros_like(sq)

    @pl.loop(0, examples)
    def _(e):
        def block_store(t, value):
            block[e, :, lane_tile(t)] = value.astype(bf16)

        def part_store(t, value):
            part[e, :, lane_tile(t)] = value.astype(bf16)

        forward(wk, lambda t: x[e, :, lane_tile(t)].astype(f32), 8, block_store)
        backward_two(
            wk,
            lambda t: cot[e, :, lane_tile(t)].astype(f32),
            lambda t: wl[e, :, lane_tile(t)],
            8,
            raw.at[e],
        )
        backward_one(wk, 8, raw.at[e], raw_gn.at[e], part_store)
        sq[...] = jnp.zeros_like(sq)
        raw_gradient(wk, raw.at[e], sq)
        gn = raw_gn[e]
        square = whole_sum(sq[...]) + whole_sum(gn * gn)
        length[e] = jnp.broadcast_to(jnp.sqrt(square), (8, LANES))

    factors = [CLIP / jnp.maximum(length[e][0:1, 0:1], CLIP) for e in range(examples)]
    total = factors[0] * raw_gn[0]
    for e in range(1, examples):
        total = total + factors[e] * raw_gn[e]
    clipped_gn[...] = total

    @pl.loop(0, 18)
    def _(k):
        total = factors[0] * raw[0, k]
        for e in range(1, examples):
            total = total + factors[e] * raw[e, k]
        clipped[k] = total.astype(bf16)


def compute(x, cot, xt, ct, ktp, wl, sg):
    examples = x.shape[0]
    out = jax.ShapeDtypeStruct
    shapes = (
        out(x.shape, bf16),
        out(x.shape, bf16),
        out((18, C, C), bf16),
        out((18, C, C), bf16),
        out((C, LANES), f32),
        out((C, LANES), f32),
        out((examples, 18, C, C), f32),
        out((examples, C, LANES), f32),
        out((examples, 8, LANES), f32),
    )
    spec = pl.BlockSpec(memory_space=pltpu.VMEM)
    return pl.pallas_call(
        compute_kernel,
        out_shape=shapes,
        in_specs=[spec] * 7,
        out_specs=(spec,) * 9,
        scratch_shapes=WORK_SCRATCH + [pltpu.VMEM((18, C, C), f32), pltpu.VMEM((8, LANES), f32)],
        compiler_params=pltpu.CompilerParams(vmem_limit_bytes=58 << 20),
    )(x, cot, xt, ct, ktp, wl, sg)


def peer_copy(src, dst, send, recv, **where):
    return pltpu.make_async_remote_copy(
        src_ref=src, dst_ref=dst, send_sem=send, recv_sem=recv, device_id=where, device_id_type=MESH
    )


def greet(peers):
    barrier = pltpu.get_barrier_semaphore()
    for where in peers:
        pl.semaphore_signal(barrier, inc=1, device_id=where, device_id_type=MESH)
    pl.semaphore_wait(barrier, len(peers))


class Exchange:
    def __init__(self, place, conv, gn, refs, sems):
        self.w, self.z, self.c, self.me = place
        self.conv, self.gn = conv, gn
        self.cb, self.cg, self.half, self.wb, self.quarter, self.zb = refs
        s_core, r_core, s_wide, r_wide, s_z, r_z = sems
        w, z, c = self.w, self.z, self.c
        sibling = self.me + 1 - 2 * c
        self.core = [
            peer_copy(conv.at[:, :, 1 - c], self.cb, s_core.at[0], r_core.at[0], narrow=sibling),
            peer_copy(gn.at[:, 1 - c], self.cg, s_core.at[1], r_core.at[1], narrow=sibling),
        ]
        self.wide, self.line = [], []
        for k in range(1, 4):
            to = lax.rem(w + k, 4)
            self.wide.append(
                peer_copy(self.half.at[to], self.wb.at[k - 1], s_wide.at[k - 1], r_wide.at[k - 1], wide=to)
            )
        for k in range(1, 4):
            to = lax.rem(z + k, 4)
            self.line.append(
                peer_copy(
                    self.quarter.at[:, to], self.zb.at[k - 1], s_z.at[k - 1], r_z.at[k - 1], narrow=to * 2 + c
                )
            )

    def clear(self):
        for q in range(1, 4):
            self.half[q, 9] = jnp.zeros_like(self.half[q, 9])

    def start_core(self):
        for copy in self.core:
            copy.start()

    def start_wide(self):
        for copy in self.core:
            copy.wait()
        half, c = self.half, self.c
        for k in range(2):

            @pl.loop(0, 9)
            def _(tap):
                total = self.conv[k * 9 + tap, :, c].astype(f32) + self.cb[k * 9 + tap].astype(f32)
                half[k * 2, tap] = total[:, :, :LANES].astype(bf16)
                half[k * 2 + 1, tap] = total[:, :, LANES:].astype(bf16)

        half[0, 9] = (self.gn[:, c].astype(f32) + self.cg[...].astype(f32)).astype(bf16)
        for copy in self.wide:
            copy.start()

    def start_line(self):
        for copy in self.wide:
            copy.wait()

        @pl.loop(0, 10)
        def _(tap):
            total = self.half[self.w, tap].astype(f32)
            for k in range(3):
                total = total + self.wb[k, tap].astype(f32)
            self.quarter[tap] = total.astype(bf16)

        for copy in self.line:
            copy.start()

    def finish(self, out):
        for copy in self.line:
            copy.wait()

        @pl.loop(0, 10)
        def _(tap):
            total = self.quarter[tap, self.z].astype(f32)
            for k in range(3):
                total = total + self.zb[k, tap].astype(f32)
            out[tap] = total.astype(bf16)


def start_all(copies):
    for copy in copies:
        copy.start()


def wait_all(copies):
    for copy in copies:
        copy.wait()


UNITS = 20


def own_kernels(weight, gain, shard):
    chans = weight.shape[1]
    lane = lax.broadcasted_iota(jnp.int32, (chans, LANES), 1)
    eye = lax.broadcasted_iota(jnp.int32, (chans, chans), 0) == lax.broadcasted_iota(
        jnp.int32, (chans, chans), 1
    )
    values = [
        jnp.sum(jnp.where(eye, jnp.broadcast_to(gain[k : k + 1, :], (chans, chans)), 0.0), axis=1, keepdims=True)
        for k in range(4)
    ]
    for conv in range(2):
        total = jnp.zeros((chans, C), f32)
        for tap in range(9):
            total = total + weight[conv * 9 + tap]
        mean = jnp.sum(total, axis=1, keepdims=True) * (1.0 / FAN)
        total = jnp.zeros((chans, C), f32)
        for tap in range(9):
            centre = weight[conv * 9 + tap] - mean
            total = total + centre * centre
        spread = jnp.sum(total, axis=1, keepdims=True) * (1.0 / FAN)
        scale = lax.rsqrt(FAN * spread + 1e-06)
        values.append(scale)
        for tap in range(9):
            kernel = ((weight[conv * 9 + tap] - mean) * scale).astype(bf16)
            shard[conv, 2 * tap] = kernel[:, :LANES]
            shard[conv, 2 * tap + 1] = kernel[:, LANES:]
    tail = jnp.zeros((chans, LANES), f32)
    for k, value in enumerate(values):
        high = value.astype(bf16).astype(f32)
        mid = (value - high).astype(bf16).astype(f32)
        low = value - high - mid
        tail = tail + jnp.where(lane == k, high, 0.0)
        tail = tail + jnp.where(lane == 8 + k, mid, 0.0)
        tail = tail + jnp.where(lane == 16 + k, low, 0.0)
    shard[0, 18] = tail.astype(bf16)
    zero = jnp.zeros((chans, LANES), bf16)
    shard[0, 19] = zero
    shard[1, 18] = zero
    shard[1, 19] = zero


def mega_kernel(
    images, cots, timg, tcot, weight, gain, pairs, alive, counts, ob, op, red_out, gn_out, norms, infl, *scratch
):
    n = 8
    me = lax.axis_index("narrow")
    w = lax.axis_index("wide")
    z, c = me // 2, me % 2
    sibling = me + 1 - 2 * c
    examples = images.shape[0] // n
    chans = images.shape[1]
    mine = pl.ds(pl.multiple_of(me * chans, chans), chans)
    work, rest = scratch[: len(WORK_SCRATCH)], scratch[len(WORK_SCRATCH) :]
    x, cot, xt, ct, shard, ktp, block, part, raw, raw_gn, length, tgrad, tgn, sq = rest[:14]
    s_conv, s_gn, t_conv, t_gn, dt, red, figures = rest[14:21]
    s_refs, t_refs = rest[21:27], rest[27:33]
    s_sems, t_sems = rest[33:39], rest[39:45]
    s_in, r_in, s_kz, r_kz, s_kw, r_kw, s_kc, r_kc, s_loc = rest[45:54]
    s_out, r_out, s_fin, r_fin, s_fig, r_fig = rest[54:60]
    greet(
        [{"narrow": lax.rem(me + k, n)} for k in range(1, n)]
        + [{"wide": lax.rem(w + k, 4)} for k in range(1, 4)]
    )

    def spread(a, src, dst, cut):
        copies = []
        for k in range(n):
            to = lax.rem(me + k, n)
            if k == 0:
                copies.append(pltpu.make_async_copy(cut(src, to), dst, s_loc.at[a]))
            else:
                copies.append(peer_copy(cut(src, to), dst, s_in.at[a, k - 1], r_in.at[a, k - 1], narrow=to))
        return copies

    def test_cut(src, to):
        return src.at[:, pl.ds(pl.multiple_of(to * LANES, LANES), LANES)]

    def example_cut(e):
        return lambda src, to: src.at[to * examples + e]

    def give_back(a, e, src, dst):
        copies = []
        for k in range(n):
            to = lax.rem(me + k, n)
            piece = src.at[e, pl.ds(pl.multiple_of(to * chans, chans), chans)]
            place = dst.at[me * examples + e]
            slot = a * examples + e
            if k == 0:
                copies.append(pltpu.make_async_copy(piece, place, s_loc.at[6 + slot]))
            else:
                copies.append(peer_copy(piece, place, s_out.at[slot, k - 1], r_out.at[slot, k - 1], narrow=to))
        return copies

    in_test = spread(0, timg, xt.at[mine], test_cut) + spread(1, tcot, ct.at[mine], test_cut)
    in_x = [spread(2 + 2 * e, images, x.at[e, mine], example_cut(e)) for e in range(examples)]
    in_cot = [spread(3 + 2 * e, cots, cot.at[e, mine], example_cut(e)) for e in range(examples)]
    out_block = [give_back(0, e, block, ob) for e in range(examples)]
    out_part = [give_back(1, e, part, op) for e in range(examples)]
    fifth = pl.ds(w * (UNITS // 4), UNITS // 4)
    k_line, k_wide, k_core = [], [], []
    for conv in range(2):
        k_line.append(
            [
                peer_copy(
                    shard.at[conv, fifth],
                    ktp.at[conv, fifth, z, c],
                    s_kz.at[conv, k - 1],
                    r_kz.at[conv, k - 1],
                    narrow=lax.rem(z + k, 4) * 2 + c,
                )
                for k in range(1, 4)
            ]
        )
        held = ktp.at[conv, fifth, :, c]
        k_wide.append(
            [
                peer_copy(held, held, s_kw.at[conv, k - 1], r_kw.at[conv, k - 1], wide=lax.rem(w + k, 4))
                for k in range(1, 4)
            ]
        )
        held = ktp.at[conv, :, :, c]
        k_core.append(peer_copy(held, held, s_kc.at[conv], r_kc.at[conv], narrow=sibling))

    start_all(in_test)
    own_kernels(weight, gain, shard)
    for conv in range(2):
        start_all(k_line[conv])
    for e in range(examples):
        start_all(in_x[e])
        start_all(in_cot[e])
    wk = make_work(work)
    fill_work(wk)
    place = (w, z, c, me)
    direction = Exchange(place, t_conv, t_gn, t_refs, t_sems)
    clipped = Exchange(place, s_conv, s_gn, s_refs, s_sems)
    direction.clear()
    clipped.clear()
    for conv in range(2):
        ktp[conv, fifth, z, c] = shard[conv, fifth]
    lane = lax.broadcasted_iota(jnp.int32, (1, LANES), 1)
    half = lane // PIX
    sign = jnp.zeros((1, LANES), f32)
    for p in range(pairs.shape[0]):
        sign = sign + jnp.where(lax.rem(pairs[p, 0], AUG) == me * 2 + half, 1.0, 0.0)
        sign = sign - jnp.where(lax.rem(pairs[p, 1], AUG) == me * 2 + half, 1.0, 0.0)

    def slot_weight(e):
        count = counts[me * examples + e]
        live = jnp.where(me * examples + e < alive[0], count, 0)
        each = 1.0 / jnp.full((1, LANES), count.astype(f32))
        return lambda t: jnp.where(t * 2 + half < live, each, 0.0)

    for conv in range(2):
        wait_all(k_line[conv])
        start_all(k_wide[conv])
    for conv in range(2):
        wait_all(k_wide[conv])
        k_core[conv].start()

    def kernel_arrived(conv):
        k_core[conv].wait()
        if conv == 0:
            unpack_params(wk, ktp[0, 18].reshape(C, LANES))
        for unit in range(18):
            wk.kf[conv, :, unit * LANES : (unit + 1) * LANES] = ktp[conv, unit].reshape(C, LANES)
        turn_kernel(wk, conv)

    kernel_arrived(0)
    wait_all(in_test)
    forward(wk, lambda t: xt[...].astype(f32), 1, None)
    kernel_arrived(1)
    backward_two(wk, lambda t: ct[...].astype(f32), lambda t: sign, 1, tgrad)
    backward_one(wk, 1, tgrad, tgn, None)
    raw_gradient(wk, tgrad, sq)

    @pl.loop(0, 18)
    def _(k):
        t_conv[k] = tgrad[k].astype(bf16).reshape(4, 2, chans, C)

    t_gn[...] = tgn[...].astype(bf16).reshape(4, 2, chans, LANES)
    direction.start_core()

    own = dt.at[c, w, z]
    line_ag, wide_ag = [], []
    for k in range(1, 4):
        to = lax.rem(z + k, 4)
        line_ag.append(peer_copy(own, own, s_fin.at[0, k - 1], r_fin.at[0, k - 1], narrow=to * 2 + c))
    for k in range(1, 4):
        to = lax.rem(w + k, 4)
        wide_ag.append(
            peer_copy(dt.at[c, w], dt.at[c, w], s_fin.at[1, k - 1], r_fin.at[1, k - 1], wide=to)
        )
    core_ag = peer_copy(dt.at[c], dt.at[c], s_fin.at[2, 0], r_fin.at[2, 0], narrow=sibling)

    def after_forward(e):
        if e == 1:
            wait_all(line_ag)
            start_all(wide_ag)
            start_all(out_block[1])

    def between(e):
        if e == 0:
            direction.start_line()

    def after_backward(e):
        if e == 0:
            direction.finish(own)
            start_all(line_ag)
            start_all(out_block[0])
        start_all(out_part[e])

    for e in range(examples):
        wait_all(in_x[e])

        def block_store(t, value):
            block[e, :, lane_tile(t)] = value.astype(bf16)

        def part_store(t, value):
            part[e, :, lane_tile(t)] = value.astype(bf16)

        forward(
            wk,
            lambda t: x[e, :, lane_tile(t)].astype(f32),
            8,
            block_store,
            direction.start_wide if e == 0 else None,
        )
        after_forward(e)
        wait_all(in_cot[e])
        backward_two(wk, lambda t: cot[e, :, lane_tile(t)].astype(f32), slot_weight(e), 8, raw.at[e])
        between(e)
        backward_one(wk, 8, raw.at[e], raw_gn.at[e], part_store)
        after_backward(e)
        sq[...] = jnp.zeros_like(sq)
        raw_gradient(wk, raw.at[e], sq)
        gn = raw_gn[e]
        square = whole_sum(sq[...]) + whole_sum(gn * gn)
        length[e] = jnp.broadcast_to(jnp.sqrt(square), (8, LANES))

    factors = [CLIP / jnp.maximum(length[e][0:1, 0:1], CLIP) for e in range(examples)]
    total = factors[0] * raw_gn[0]
    for e in range(1, examples):
        total = total + factors[e] * raw_gn[e]
    s_gn[...] = total.astype(bf16).reshape(4, 2, chans, LANES)

    @pl.loop(0, 18)
    def _(k):
        total = factors[0] * raw[0, k]
        for e in range(1, examples):
            total = total + factors[e] * raw[e, k]
        s_conv[k] = total.astype(bf16).reshape(4, 2, chans, C)

    clipped.start_core()
    wait_all(wide_ag)
    core_ag.start()
    clipped.start_wide()
    core_ag.wait()
    inner_products(dt, raw, raw_gn, length, figures, me, chans)
    figs = []
    for k in range(1, n):
        to = lax.rem(me + k, n)
        figs.append(peer_copy(figures.at[me], figures.at[me], s_fig.at[k - 1], r_fig.at[k - 1], narrow=to))
    start_all(figs)
    clipped.start_line()
    clipped.finish(red.at[w])
    finals = []
    for k in range(1, 4):
        to = lax.rem(w + k, 4)
        finals.append(peer_copy(red.at[w], red.at[w], s_fin.at[3, k - 1], r_fin.at[3, k - 1], wide=to))
    start_all(finals)
    wait_all(figs)
    slot = lax.broadcasted_iota(jnp.int32, (8, LANES), 1)
    table = jnp.zeros((8, LANES), f32)
    for k in range(n):
        for e in range(examples):
            table = table + jnp.where(slot == k * examples + e, figures[k, e], 0.0)
    norms[...] = table[0:1, : n * examples]
    infl[...] = table[1:2, : n * examples]
    for e in range(examples):
        wait_all(out_block[e])
        wait_all(out_part[e])
    wait_all(finals)
    gn_out[...] = red[0, 9]
    for conv in range(2):
        for tap in range(9):
            red_out[conv * 9 + tap, :, :LANES] = red[conv * 2, tap]
            red_out[conv * 9 + tap, :, LANES:] = red[conv * 2 + 1, tap]


def inner_products(dt, raw, raw_gn, length, figures, me, chans):
    examples = raw.shape[0]
    zero = jnp.zeros((chans, LANES), f32)

    def visit(index, carry):
        q, rest = index // 8, index % 8
        at = pl.ds(pl.multiple_of(rest * chans, chans), chans)
        lanes = pl.ds(pl.multiple_of((q % 2) * LANES, LANES), LANES)
        square = carry[0]
        sums = list(carry[1:])
        for tap in range(9):
            d = dt[rest % 2, q, rest // 2, tap].astype(f32)
            square = square + d * d
            for e in range(examples):
                sums[e] = sums[e] + d * raw[e, (q // 2) * 9 + tap, at, lanes]
        return (square, *sums)

    totals = lax.fori_loop(0, 32, visit, (zero,) * (examples + 1))

    def visit_gn(rest, carry):
        at = pl.ds(pl.multiple_of(rest * chans, chans), chans)
        d = dt[rest % 2, 0, rest // 2, 9].astype(f32)
        return (carry[0] + d * d,) + tuple(carry[1 + e] + d * raw_gn[e, at, :] for e in range(examples))

    totals = lax.fori_loop(0, 8, visit_gn, totals)
    dir_sq = whole_sum(totals[0])
    params = 18 * C * C + 4 * C
    top = lax.broadcasted_iota(jnp.int32, (8, LANES), 0)
    for e in range(examples):
        size = length[e]
        factor = CLIP / jnp.maximum(size, CLIP)
        influence = factor * whole_sum(totals[1 + e]) * math.sqrt(params) / (CLIP * jnp.sqrt(dir_sq + 1e-06))
        figures[me, e] = jnp.where(top == 0, size, influence)


def mega(images, cots, timg, tcot, weight, gain, pairs, alive, counts):
    held, chans = images.shape[0], images.shape[1]
    examples = held // 8
    out = jax.ShapeDtypeStruct
    anyspace = pl.BlockSpec(memory_space=pl.ANY)
    vmem = pl.BlockSpec(memory_space=pltpu.VMEM)
    smem = pl.BlockSpec(memory_space=pltpu.SMEM)
    dma = pltpu.SemaphoreType.DMA
    exchange = [
        pltpu.VMEM((18, 4, chans, C), bf16),
        pltpu.VMEM((4, chans, LANES), bf16),
        pltpu.VMEM((4, 10, 4, chans, LANES), bf16),
        pltpu.VMEM((3, 10, 4, chans, LANES), bf16),
        pltpu.VMEM((10, 4, chans, LANES), bf16),
        pltpu.VMEM((3, 10, chans, LANES), bf16),
    ]
    sems = [dma((2,)), dma((2,)), dma((3,)), dma((3,)), dma((3,)), dma((3,))]
    scratch = [
        pltpu.VMEM((examples, C, AUG * PIX), bf16),
        pltpu.VMEM((examples, C, AUG * PIX), bf16),
        pltpu.VMEM((C, LANES), bf16),
        pltpu.VMEM((C, LANES), bf16),
        pltpu.VMEM((2, UNITS, chans, LANES), bf16),
        pltpu.VMEM((2, UNITS, 4, 2, chans, LANES), bf16),
        pltpu.VMEM((examples, C, AUG * PIX), bf16),
        pltpu.VMEM((examples, C, AUG * PIX), bf16),
        pltpu.VMEM((examples, 18, C, C), f32),
        pltpu.VMEM((examples, C, LANES), f32),
        pltpu.VMEM((examples, 8, LANES), f32),
        pltpu.VMEM((18, C, C), f32),
        pltpu.VMEM((C, LANES), f32),
        pltpu.VMEM((8, LANES), f32),
        pltpu.VMEM((18, 4, 2, chans, C), bf16),
        pltpu.VMEM((4, 2, chans, LANES), bf16),
        pltpu.VMEM((18, 4, 2, chans, C), bf16),
        pltpu.VMEM((4, 2, chans, LANES), bf16),
        pltpu.VMEM((2, 4, 4, 10, chans, LANES), bf16),
        pltpu.VMEM((4, 10, chans, LANES), bf16),
        pltpu.VMEM((8, examples, 8, LANES), f32),
    ]
    kinds = 2 + 2 * examples
    moves = [
        dma((kinds, 7)),
        dma((kinds, 7)),
        dma((2, 3)),
        dma((2, 3)),
        dma((2, 3)),
        dma((2, 3)),
        dma((2,)),
        dma((2,)),
        dma((11,)),
        dma((2 * examples, 7)),
        dma((2 * examples, 7)),
        dma((4, 3)),
        dma((4, 3)),
        dma((7,)),
        dma((7,)),
    ]
    return pl.pallas_call(
        mega_kernel,
        out_shape=(
            out((held, chans, AUG * PIX), bf16),
            out((held, chans, AUG * PIX), bf16),
            out((18, chans, C), bf16),
            out((chans, LANES), bf16),
            out((1, held), f32),
            out((1, held), f32),
        ),
        in_specs=[anyspace] * 4 + [vmem] * 2 + [smem] * 3,
        out_specs=(anyspace, anyspace) + (vmem,) * 4,
        scratch_shapes=WORK_SCRATCH + scratch + exchange + exchange + sems + sems + moves,
        compiler_params=pltpu.CompilerParams(collective_id=0, has_side_effects=True, vmem_limit_bytes=60 << 20),
    )(images, cots, timg, tcot, weight, gain, pairs, alive, counts)


def pieces(v):
    high = lax.reduce_precision(v, 8, 7)
    rest = v - high
    mid = lax.reduce_precision(rest, 8, 7)
    low = rest - mid
    return high.astype(bf16), mid.astype(bf16), low.astype(bf16)


def kernel_rows(conv_weight, gn_params):
    chans = conv_weight.shape[4]
    centre = conv_weight - jnp.mean(conv_weight, axis=(1, 2, 3), keepdims=True)
    spread = jnp.mean(centre * centre, axis=(1, 2, 3), keepdims=True)
    scale = lax.rsqrt(FAN * spread + 1e-06)
    kernels = (centre * scale).astype(bf16).reshape(2, FAN, chans)
    rows = kernels.transpose(2, 0, 1).reshape(chans, KCOLS)
    small = jnp.concatenate([gn_params.T, scale.reshape(2, chans).T, jnp.zeros((chans, 2), f32)], 1)
    tail = jnp.concatenate(list(pieces(small)) + [jnp.zeros((chans, LANES - 24), bf16)], 1)
    return jnp.concatenate([rows, tail], 1)


def adamw(weight, first, second, grad, correction, rate, decay):
    first_new = 0.5 * first + 0.5 * grad
    second_new = 0.5 * second + 0.5 * grad * grad
    update = first_new / correction / (jnp.sqrt(second_new / correction) + 1e-08)
    return (weight - rate * (update + decay * weight), first_new, second_new)


def plain_gather(images, cots, timg, tcot, kshard, narrow):
    share = narrow // 8
    x = lax.all_to_all(images, "narrow", 0, 1, tiled=True)
    cot = lax.all_to_all(cots, "narrow", 0, 1, tiled=True)
    ktp = lax.all_gather(kshard, "narrow", axis=0, tiled=True)
    own = (lax.axis_index("narrow") // share) * LANES

    def pick(v):
        return lax.dynamic_slice_in_dim(lax.all_gather(v, "narrow", axis=0, tiled=True), own, LANES, 1)

    return x, cot, pick(timg), pick(tcot), ktp


def plain_reduce(block, part, clip_conv, test_conv, clip_gn, test_gn, raw, raw_gn, length, chans):
    examples = block.shape[0]
    ob = lax.all_to_all(block, "narrow", 1, 0, tiled=True)
    op = lax.all_to_all(part, "narrow", 1, 0, tiled=True)
    own = lax.axis_index("narrow") * chans
    rows = lax.psum(clip_conv, ("wide", "narrow"))
    rows = lax.dynamic_slice_in_dim(rows, own, chans, 1)
    gn_rows = lax.dynamic_slice_in_dim(lax.psum(clip_gn.astype(bf16), ("wide", "narrow")), own, chans, 0)
    d = lax.psum(test_conv, ("wide", "narrow")).astype(f32)
    d_gn = lax.psum(test_gn.astype(bf16), ("wide", "narrow")).astype(f32)
    dir_sq = jnp.sum(d * d) + jnp.sum(d_gn * d_gn)
    inner = jnp.sum(raw * d, axis=(1, 2, 3)) + jnp.sum(raw_gn * d_gn, axis=(1, 2))
    size = length[:, 0, 0]
    factor = CLIP / jnp.maximum(size, CLIP)
    influence = factor * inner * math.sqrt(18 * C * C + 4 * C) / (CLIP * jnp.sqrt(dir_sq + 1e-06))
    figures = lax.all_gather(jnp.stack([size, influence], 1), "narrow", axis=0)
    return ob, op, rows, gn_rows, figures[:, :, 0], figures[:, :, 1]


def local(
    images,
    cotangent,
    test_images,
    test_cotangent,
    pair_index,
    example_count,
    aug_count,
    conv_weight,
    gn_params,
    conv_moment1,
    conv_moment2,
    gn_moment1,
    gn_moment2,
    noise_conv,
    noise_gn,
    step_count,
):
    n_wide, narrow = lax.axis_size("wide"), lax.axis_size("narrow")
    held, chans = images.shape[0], images.shape[1]
    examples = held // narrow
    share = narrow // 8
    me = lax.axis_index("narrow")
    slots = jnp.arange(AUG, dtype=jnp.int32)
    live = jnp.arange(held, dtype=jnp.int32) < example_count[0]
    weights = jnp.where(
        live[:, None] & (slots[None, :] < aug_count[:, None]),
        1.0 / aug_count.astype(f32)[:, None],
        f32(0.0),
    )
    pixels = jnp.repeat(weights, PIX, axis=1)
    pairs = pair_index % AUG
    signs = jnp.sum((pairs[:, 0:1] == slots[None, :]).astype(f32), 0) - jnp.sum(
        (pairs[:, 1:2] == slots[None, :]).astype(f32), 0
    )
    sign_pixels = jnp.repeat(signs, PIX).reshape(8, LANES) * (1.0 / share)
    timg, tcot = test_images[0], test_cotangent[0]
    if n_wide == 4 and narrow == 8:
        weight = conv_weight.transpose(0, 1, 2, 4, 3).reshape(18, chans, C)
        outs = mega(
            images, cotangent, timg, tcot, weight, gn_params, pair_index, example_count, aug_count
        )
    else:
        kshard = kernel_rows(conv_weight, gn_params)
        wl = lax.dynamic_slice_in_dim(pixels, me * examples, examples, 0)[:, None, :]
        sg = lax.dynamic_slice_in_dim(sign_pixels, me // share, 1, 0)
        x, cot, xt, ct, ktp = plain_gather(images, cotangent, timg, tcot, kshard, narrow)
        parts = compute(x, cot, xt, ct, ktp, wl, sg)
        outs = plain_reduce(*parts, chans)
    block_out, op, red, red_gn, lengths, influence = outs
    input_grad = cotangent.astype(f32) * pixels[:, None, :] + op.astype(f32)
    lengths, influence = lengths.reshape(held), influence.reshape(held)
    sum_conv = red.reshape(2, 3, 3, chans, C).transpose(0, 1, 2, 4, 3).astype(f32)
    sum_norm = red_gn[:, :4].T.astype(f32)
    total = held * n_wide
    noisy_conv = (sum_conv + math.sqrt(total) * noise_conv) / total
    noisy_norm = (sum_norm + math.sqrt(total) * noise_gn) / total
    correction = 1.0 - jnp.power(f32(0.5), step_count[0].astype(f32))
    conv_new, conv_first, conv_second = adamw(
        conv_weight, conv_moment1, conv_moment2, noisy_conv, correction, 1.0 / math.sqrt(9 * C), 0.1
    )
    gn_new, gn_first, gn_second = adamw(
        gn_params, gn_moment1, gn_moment2, noisy_norm, correction, 0.1, 0.0
    )
    return (
        block_out,
        input_grad,
        lengths,
        influence,
        conv_new,
        conv_new.astype(bf16),
        conv_first,
        conv_second,
        gn_new,
        gn_first,
        gn_second,
    )


def solution(mesh):
    in_specs = (
        P("wide", "narrow", None),
        P("wide", "narrow", None),
        P("wide", "narrow", None),
        P("wide", "narrow", None),
        P("wide", None),
        P("wide"),
        P("wide"),
        P(None, None, None, None, "narrow"),
        P(None, "narrow"),
        P(None, None, None, None, "narrow"),
        P(None, None, None, None, "narrow"),
        P(None, "narrow"),
        P(None, "narrow"),
        P(None, None, None, None, "narrow"),
        P(None, "narrow"),
        P(),
    )
    out_specs = (
        P("wide", "narrow", None),
        P("wide", "narrow", None),
        P("wide"),
        P("wide"),
        P(None, None, None, None, "narrow"),
        P(None, None, None, None, "narrow"),
        P(None, None, None, None, "narrow"),
        P(None, None, None, None, "narrow"),
        P(None, "narrow"),
        P(None, "narrow"),
        P(None, "narrow"),
    )
    return jax.shard_map(local, mesh=mesh, in_specs=in_specs, out_specs=out_specs, check_vma=False)
```

```python
import functools
import math

import jax
import jax.numpy as jnp
from jax import lax
from jax.experimental import pallas as pl
from jax.experimental.pallas import tpu as pltpu
from jax.sharding import PartitionSpec as P

C = 256
MAP = 8
GROUPS = 16
AUG = 16
PIX = MAP * MAP
FAN = 9 * C
LANES = 128
CLIP = 6.0 * C
MESH = pl.DeviceIdType.MESH
f32 = jnp.float32
bf16 = jnp.bfloat16
KCOLS = 2 * FAN


def lane_tile(index):
    return pl.ds(pl.multiple_of(index * LANES, LANES), LANES)


def group_sum(tile):
    return tile.reshape(GROUPS, C // GROUPS, LANES).sum(1)


def spread_group(rows):
    return jnp.broadcast_to(rows[:, None, :], (GROUPS, C // GROUPS, LANES)).reshape(C, LANES)


def image_sum(rows, ones):
    return lax.dot_general(
        rows,
        ones,
        (((1,), (0,)), ((), ())),
        precision=lax.Precision.HIGHEST,
        preferred_element_type=f32,
    )


def sigmoid(z):
    return 0.5 * jnp.tanh(0.5 * z) + 0.5


def tap_masks():
    lane = lax.broadcasted_iota(jnp.int32, (1, LANES), 1)
    row = (lane // MAP) % MAP
    col = lane % MAP
    masks = []
    for r in (-1, 0, 1):
        for c in (-1, 0, 1):
            ok = (row + r >= 0) & (row + r < MAP) & (col + c >= 0) & (col + c < MAP)
            masks.append(jnp.where(ok, 1.0, 0.0).astype(f32).astype(bf16))
    return masks


def store_taps(value, col_ref, t, masks, flip):
    for tap in range(9):
        shift = (tap // 3 - 1) * MAP + (tap % 3 - 1)
        if shift == 0:
            moved = value
        else:
            moved = pltpu.roll(value, (-shift) % LANES, 1) * masks[tap]
        place = 8 - tap if flip else tap
        col_ref[place * C : (place + 1) * C, lane_tile(t)] = moved


def product(a, b):
    return jnp.dot(a, b, preferred_element_type=f32)


def product_nt(a, b):
    return lax.dot_general(a, b, (((1,), (1,)), ((), ())), preferred_element_type=f32)


class Work:
    pass


def norm_forward(wk, load, tiles, which, hat, rstd, hidden, col):
    stat = wk.stat

    @pl.loop(0, tiles)
    def _(t):
        stat[pl.ds(pl.multiple_of(t * GROUPS, GROUPS), GROUPS), :] = group_sum(load(t))

    rows = tiles * GROUPS
    stat[:rows, :] = image_sum(stat[:rows, :], wk.ones[...]) * (1.0 / (PIX * C // GROUPS))

    @pl.loop(0, tiles)
    def _(t):
        at = pl.ds(pl.multiple_of(t * GROUPS, GROUPS), GROUPS)
        centre = load(t) - spread_group(stat[at, :])
        hat[:, lane_tile(t)] = centre
        stat[at, :] = group_sum(centre * centre)

    spread = image_sum(stat[:rows, :], wk.ones[...]) * (1.0 / (PIX * C // GROUPS))
    rstd[:rows, :] = lax.rsqrt(spread + 1e-05)

    @pl.loop(0, tiles)
    def _(t):
        at = pl.ds(pl.multiple_of(t * GROUPS, GROUPS), GROUPS)
        normed = hat[:, lane_tile(t)] * spread_group(rstd[at, :])
        hat[:, lane_tile(t)] = normed
        scaled = normed * wk.gn[2 * which] + wk.gn[2 * which + 1]
        act = (scaled * sigmoid(scaled)).astype(bf16)
        hidden[:, lane_tile(t)] = act
        if col is not None:
            store_taps(act, col, t, wk.masks, False)


def norm_backward(wk, grad, tiles, which, hat, rstd, emit, acc):
    stat, stat2 = wk.stat, wk.stat2
    acc[0] = jnp.zeros((C, LANES), f32)
    acc[1] = jnp.zeros((C, LANES), f32)

    @pl.loop(0, tiles)
    def _(t):
        at = pl.ds(pl.multiple_of(t * GROUPS, GROUPS), GROUPS)
        normed = hat[:, lane_tile(t)]
        scaled = normed * wk.gn[2 * which] + wk.gn[2 * which + 1]
        gate = sigmoid(scaled)
        inner = grad[:, lane_tile(t)] * gate * (1.0 + scaled * (1.0 - gate))
        acc[0] += inner * normed
        acc[1] += inner
        inner = inner * wk.gn[2 * which]
        grad[:, lane_tile(t)] = inner
        stat[at, :] = group_sum(inner)
        stat2[at, :] = group_sum(inner * normed)

    if emit is not None:
        rows = tiles * GROUPS
        scale = 1.0 / (PIX * C // GROUPS)
        stat[:rows, :] = image_sum(stat[:rows, :], wk.ones[...]) * scale
        stat2[:rows, :] = image_sum(stat2[:rows, :], wk.ones[...]) * scale

        @pl.loop(0, tiles)
        def _(t):
            at = pl.ds(pl.multiple_of(t * GROUPS, GROUPS), GROUPS)
            value = grad[:, lane_tile(t)] - spread_group(stat[at, :])
            value = value - hat[:, lane_tile(t)] * spread_group(stat2[at, :])
            emit(t, value * spread_group(rstd[at, :]))


def matmul_cols(out, left, right, width):
    step = min(width, 256)
    for j in range(0, width, step):
        out[:, j : j + step] = product(left, right[:, j : j + step])


def fill_work(wk):
    half_a = lax.broadcasted_iota(jnp.int32, (LANES, LANES), 0) // PIX
    half_b = lax.broadcasted_iota(jnp.int32, (LANES, LANES), 1) // PIX
    wk.ones[...] = jnp.where(half_a == half_b, 1.0, 0.0).astype(f32)
    wk.masks = tap_masks()


def unpack_params(wk, tail):
    tail = tail.astype(f32)
    for k in range(6):
        value = tail[:, k : k + 1] + tail[:, 8 + k : 9 + k] + tail[:, 16 + k : 17 + k]
        value = jnp.broadcast_to(value, (C, LANES))
        if k < 4:
            wk.gn[k] = value
        else:
            wk.rs[k - 4] = value


def turn_kernel(wk, conv):
    for tap in range(9):
        wk.kb[conv, :, tap * C : (tap + 1) * C] = wk.kf[conv, :, tap * C : (tap + 1) * C].T


def cols(ref, width):
    return ref if width == ref.shape[1] else ref.at[:, :width]


def forward(wk, x_load, tiles, block_store, early=None):
    width = tiles * LANES
    norm_forward(wk, x_load, tiles, 0, wk.hat1, wk.rstd1, wk.hid1, wk.col)
    if early is not None:
        early()
    matmul_cols(wk.mid, wk.kf[0], cols(wk.col, width), width)
    norm_forward(
        wk,
        lambda t: wk.mid[:, lane_tile(t)],
        tiles,
        1,
        wk.hat2,
        wk.rstd2,
        wk.hid2,
        wk.col if block_store is not None else None,
    )
    if block_store is not None:
        matmul_cols(wk.mid, wk.kf[1], cols(wk.col, width), width)

        @pl.loop(0, tiles)
        def _(t):
            block_store(t, x_load(t) + wk.mid[:, lane_tile(t)])


def backward_two(wk, cot_load, weight_load, tiles, grads):
    width = tiles * LANES

    @pl.loop(0, tiles)
    def _(t):
        store_taps((cot_load(t) * weight_load(t)).astype(bf16), wk.col, t, wk.masks, True)

    matmul_cols(wk.mid, wk.kb[1], cols(wk.col, width), width)
    for tap in range(9):
        grads[9 + tap] = product_nt(wk.col[tap * C : (tap + 1) * C, :width], wk.hid2[:, :width])


def backward_one(wk, tiles, grads, gn_out, part_store):
    width = tiles * LANES

    def emit_middle(t, value):
        store_taps(value.astype(bf16), wk.col, t, wk.masks, True)

    norm_backward(wk, wk.mid, tiles, 1, wk.hat2, wk.rstd2, emit_middle, wk.acc.at[1])
    matmul_cols(wk.mid, wk.kb[0], cols(wk.col, width), width)
    for tap in range(9):
        grads[tap] = product_nt(wk.col[tap * C : (tap + 1) * C, :width], wk.hid1[:, :width])
    norm_backward(wk, wk.mid, tiles, 0, wk.hat1, wk.rstd1, part_store, wk.acc.at[0])

    lane = lax.broadcasted_iota(jnp.int32, (1, LANES), 1)
    total = jnp.zeros((C, LANES), f32)
    for k in range(4):
        one = jnp.sum(wk.acc[k // 2, k % 2], axis=1, keepdims=True)
        total = total + jnp.where(lane == k, one, 0.0)
    gn_out[...] = total


def raw_gradient(wk, grads, sq):
    rows = 32

    @pl.loop(0, C // rows)
    def _(j):
        at = pl.ds(pl.multiple_of(j * rows, rows), rows)
        for conv in range(2):
            first = jnp.zeros((rows, C), f32)
            second = jnp.zeros((rows, C), f32)
            for tap in range(9):
                g = grads[conv * 9 + tap, at, :]
                k = wk.kf[conv, at, tap * C : (tap + 1) * C].astype(f32)
                first = first + g
                second = second + g * k
            first = jnp.sum(first, axis=1, keepdims=True) * (1.0 / FAN)
            second = jnp.sum(second, axis=1, keepdims=True)
            rs = wk.rs[conv, at, 0:1]
            squares = jnp.zeros((rows, C), f32)
            for tap in range(9):
                g = grads[conv * 9 + tap, at, :]
                k = wk.kf[conv, at, tap * C : (tap + 1) * C].astype(f32)
                value = (g - first - k * second) * rs
                grads[conv * 9 + tap, at, :] = value
                squares = squares + value * value
            fold = squares[:, :LANES] + squares[:, LANES:]
            sq[...] += fold.reshape(rows // 8, 8, LANES).sum(0)


def whole_sum(tile):
    return jnp.sum(jnp.sum(tile, axis=1, keepdims=True), axis=0, keepdims=True)


WORK_SCRATCH = [
    pltpu.VMEM((2, C, FAN), bf16),
    pltpu.VMEM((2, C, FAN), bf16),
    pltpu.VMEM((FAN, AUG * PIX), bf16),
    pltpu.VMEM((C, AUG * PIX), f32),
    pltpu.VMEM((C, AUG * PIX), f32),
    pltpu.VMEM((C, AUG * PIX), f32),
    pltpu.VMEM((C, AUG * PIX), bf16),
    pltpu.VMEM((C, AUG * PIX), bf16),
    pltpu.VMEM((LANES, LANES), f32),
    pltpu.VMEM((LANES, LANES), f32),
    pltpu.VMEM((LANES, LANES), f32),
    pltpu.VMEM((LANES, LANES), f32),
    pltpu.VMEM((LANES, LANES), f32),
    pltpu.VMEM((4, C, LANES), f32),
    pltpu.VMEM((2, C, LANES), f32),
    pltpu.VMEM((2, 2, C, LANES), f32),
]
WORK_NAMES = (
    "kf",
    "kb",
    "col",
    "mid",
    "hat1",
    "hat2",
    "hid1",
    "hid2",
    "stat",
    "stat2",
    "rstd1",
    "rstd2",
    "ones",
    "gn",
    "rs",
    "acc",
)


def make_work(refs):
    wk = Work()
    for name, ref in zip(WORK_NAMES, refs):
        setattr(wk, name, ref)
    return wk


def compute_kernel(
    x, cot, xt, ct, ktp, wl, sg, block, part, clipped, test, clipped_gn, test_gn, raw, raw_gn, length, *scratch
):
    examples = x.shape[0]
    wk = make_work(scratch[:-2])
    tgrad, sq = scratch[-2:]
    fill_work(wk)
    unpack_params(wk, ktp[:, KCOLS : KCOLS + LANES])
    for conv in range(2):
        wk.kf[conv] = ktp[:, conv * FAN : (conv + 1) * FAN]
        turn_kernel(wk, conv)
    forward(wk, lambda t: xt[...].astype(f32), 1, None)
    backward_two(wk, lambda t: ct[...].astype(f32), lambda t: sg[...], 1, tgrad)
    backward_one(wk, 1, tgrad, test_gn, None)
    raw_gradient(wk, tgrad, sq)

    @pl.loop(0, 18)
    def _(k):
        test[k] = tgrad[k].astype(bf16)

    sq[...] = jnp.zeros_like(sq)

    @pl.loop(0, examples)
    def _(e):
        def block_store(t, value):
            block[e, :, lane_tile(t)] = value.astype(bf16)

        def part_store(t, value):
            part[e, :, lane_tile(t)] = value.astype(bf16)

        forward(wk, lambda t: x[e, :, lane_tile(t)].astype(f32), 8, block_store)
        backward_two(
            wk,
            lambda t: cot[e, :, lane_tile(t)].astype(f32),
            lambda t: wl[e, :, lane_tile(t)],
            8,
            raw.at[e],
        )
        backward_one(wk, 8, raw.at[e], raw_gn.at[e], part_store)
        sq[...] = jnp.zeros_like(sq)
        raw_gradient(wk, raw.at[e], sq)
        gn = raw_gn[e]
        square = whole_sum(sq[...]) + whole_sum(gn * gn)
        length[e] = jnp.broadcast_to(jnp.sqrt(square), (8, LANES))

    factors = [CLIP / jnp.maximum(length[e][0:1, 0:1], CLIP) for e in range(examples)]
    total = factors[0] * raw_gn[0]
    for e in range(1, examples):
        total = total + factors[e] * raw_gn[e]
    clipped_gn[...] = total

    @pl.loop(0, 18)
    def _(k):
        total = factors[0] * raw[0, k]
        for e in range(1, examples):
            total = total + factors[e] * raw[e, k]
        clipped[k] = total.astype(bf16)


def compute(x, cot, xt, ct, ktp, wl, sg):
    examples = x.shape[0]
    out = jax.ShapeDtypeStruct
    shapes = (
        out(x.shape, bf16),
        out(x.shape, bf16),
        out((18, C, C), bf16),
        out((18, C, C), bf16),
        out((C, LANES), f32),
        out((C, LANES), f32),
        out((examples, 18, C, C), f32),
        out((examples, C, LANES), f32),
        out((examples, 8, LANES), f32),
    )
    spec = pl.BlockSpec(memory_space=pltpu.VMEM)
    return pl.pallas_call(
        compute_kernel,
        out_shape=shapes,
        in_specs=[spec] * 7,
        out_specs=(spec,) * 9,
        scratch_shapes=WORK_SCRATCH + [pltpu.VMEM((18, C, C), f32), pltpu.VMEM((8, LANES), f32)],
        compiler_params=pltpu.CompilerParams(vmem_limit_bytes=58 << 20),
    )(x, cot, xt, ct, ktp, wl, sg)


def peer_copy(src, dst, send, recv, **where):
    return pltpu.make_async_remote_copy(
        src_ref=src, dst_ref=dst, send_sem=send, recv_sem=recv, device_id=where, device_id_type=MESH
    )


def greet(peers):
    barrier = pltpu.get_barrier_semaphore()
    for where in peers:
        pl.semaphore_signal(barrier, inc=1, device_id=where, device_id_type=MESH)
    pl.semaphore_wait(barrier, len(peers))


class Exchange:
    def __init__(self, place, conv, gn, refs, sems):
        self.w, self.z, self.c, self.me = place
        self.conv, self.gn = conv, gn
        self.cb, self.cg, self.half, self.wb, self.quarter, self.zb = refs
        s_core, r_core, s_wide, r_wide, s_z, r_z = sems
        w, z, c = self.w, self.z, self.c
        sibling = self.me + 1 - 2 * c
        self.core = [
            peer_copy(conv.at[:, :, 1 - c], self.cb, s_core.at[0], r_core.at[0], narrow=sibling),
            peer_copy(gn.at[:, 1 - c], self.cg, s_core.at[1], r_core.at[1], narrow=sibling),
        ]
        self.wide, self.line = [], []
        for k in range(1, 4):
            to = lax.rem(w + k, 4)
            self.wide.append(
                peer_copy(self.half.at[to], self.wb.at[k - 1], s_wide.at[k - 1], r_wide.at[k - 1], wide=to)
            )
        for k in range(1, 4):
            to = lax.rem(z + k, 4)
            self.line.append(
                peer_copy(
                    self.quarter.at[:, to], self.zb.at[k - 1], s_z.at[k - 1], r_z.at[k - 1], narrow=to * 2 + c
                )
            )

    def clear(self):
        for q in range(1, 4):
            self.half[q, 9] = jnp.zeros_like(self.half[q, 9])

    def start_core(self):
        for copy in self.core:
            copy.start()

    def start_wide(self):
        for copy in self.core:
            copy.wait()
        half, c = self.half, self.c
        for k in range(2):

            @pl.loop(0, 9)
            def _(tap):
                total = self.conv[k * 9 + tap, :, c].astype(f32) + self.cb[k * 9 + tap].astype(f32)
                half[k * 2, tap] = total[:, :, :LANES].astype(bf16)
                half[k * 2 + 1, tap] = total[:, :, LANES:].astype(bf16)

        half[0, 9] = (self.gn[:, c].astype(f32) + self.cg[...].astype(f32)).astype(bf16)
        for copy in self.wide:
            copy.start()

    def start_line(self):
        for copy in self.wide:
            copy.wait()

        @pl.loop(0, 10)
        def _(tap):
            total = self.half[self.w, tap].astype(f32)
            for k in range(3):
                total = total + self.wb[k, tap].astype(f32)
            self.quarter[tap] = total.astype(bf16)

        for copy in self.line:
            copy.start()

    def finish(self, out):
        for copy in self.line:
            copy.wait()

        @pl.loop(0, 10)
        def _(tap):
            total = self.quarter[tap, self.z].astype(f32)
            for k in range(3):
                total = total + self.zb[k, tap].astype(f32)
            out[tap] = total.astype(bf16)


def start_all(copies):
    for copy in copies:
        copy.start()


def wait_all(copies):
    for copy in copies:
        copy.wait()


UNITS = 20


def own_kernels(weight, gain, shard):
    chans = weight.shape[1]
    lane = lax.broadcasted_iota(jnp.int32, (chans, LANES), 1)
    eye = lax.broadcasted_iota(jnp.int32, (chans, chans), 0) == lax.broadcasted_iota(
        jnp.int32, (chans, chans), 1
    )
    values = [
        jnp.sum(jnp.where(eye, jnp.broadcast_to(gain[k : k + 1, :], (chans, chans)), 0.0), axis=1, keepdims=True)
        for k in range(4)
    ]
    for conv in range(2):
        total = jnp.zeros((chans, C), f32)
        for tap in range(9):
            total = total + weight[conv * 9 + tap]
        mean = jnp.sum(total, axis=1, keepdims=True) * (1.0 / FAN)
        total = jnp.zeros((chans, C), f32)
        for tap in range(9):
            centre = weight[conv * 9 + tap] - mean
            total = total + centre * centre
        spread = jnp.sum(total, axis=1, keepdims=True) * (1.0 / FAN)
        scale = lax.rsqrt(FAN * spread + 1e-06)
        values.append(scale)
        for tap in range(9):
            kernel = ((weight[conv * 9 + tap] - mean) * scale).astype(bf16)
            shard[conv, 2 * tap] = kernel[:, :LANES]
            shard[conv, 2 * tap + 1] = kernel[:, LANES:]
    tail = jnp.zeros((chans, LANES), f32)
    for k, value in enumerate(values):
        high = value.astype(bf16).astype(f32)
        mid = (value - high).astype(bf16).astype(f32)
        low = value - high - mid
        tail = tail + jnp.where(lane == k, high, 0.0)
        tail = tail + jnp.where(lane == 8 + k, mid, 0.0)
        tail = tail + jnp.where(lane == 16 + k, low, 0.0)
    shard[0, 18] = tail.astype(bf16)
    zero = jnp.zeros((chans, LANES), bf16)
    shard[0, 19] = zero
    shard[1, 18] = zero
    shard[1, 19] = zero


def mega_kernel(
    images, cots, timg, tcot, weight, gain, pairs, alive, counts, ob, op, red_out, gn_out, norms, infl, *scratch
):
    n = 8
    me = lax.axis_index("narrow")
    w = lax.axis_index("wide")
    z, c = me // 2, me % 2
    sibling = me + 1 - 2 * c
    examples = images.shape[0] // n
    chans = images.shape[1]
    mine = pl.ds(pl.multiple_of(me * chans, chans), chans)
    work, rest = scratch[: len(WORK_SCRATCH)], scratch[len(WORK_SCRATCH) :]
    x, cot, xt, ct, shard, ktp, block, part, raw, raw_gn, length, tgrad, tgn, sq = rest[:14]
    s_conv, s_gn, t_conv, t_gn, dt, red, figures = rest[14:21]
    s_refs, t_refs = rest[21:27], rest[27:33]
    s_sems, t_sems = rest[33:39], rest[39:45]
    s_in, r_in, s_kz, r_kz, s_kw, r_kw, s_kc, r_kc, s_loc = rest[45:54]
    s_out, r_out, s_fin, r_fin, s_fig, r_fig = rest[54:60]
    greet(
        [{"narrow": lax.rem(me + k, n)} for k in range(1, n)]
        + [{"wide": lax.rem(w + k, 4)} for k in range(1, 4)]
    )

    def spread(a, src, dst, cut):
        copies = []
        for k in range(n):
            to = lax.rem(me + k, n)
            if k == 0:
                copies.append(pltpu.make_async_copy(cut(src, to), dst, s_loc.at[a]))
            else:
                copies.append(peer_copy(cut(src, to), dst, s_in.at[a, k - 1], r_in.at[a, k - 1], narrow=to))
        return copies

    def test_cut(src, to):
        return src.at[:, pl.ds(pl.multiple_of(to * LANES, LANES), LANES)]

    def example_cut(e):
        return lambda src, to: src.at[to * examples + e]

    def give_back(a, e, src, dst):
        copies = []
        for k in range(n):
            to = lax.rem(me + k, n)
            piece = src.at[e, pl.ds(pl.multiple_of(to * chans, chans), chans)]
            place = dst.at[me * examples + e]
            slot = a * examples + e
            if k == 0:
                copies.append(pltpu.make_async_copy(piece, place, s_loc.at[6 + slot]))
            else:
                copies.append(peer_copy(piece, place, s_out.at[slot, k - 1], r_out.at[slot, k - 1], narrow=to))
        return copies

    in_test = spread(0, timg, xt.at[mine], test_cut) + spread(1, tcot, ct.at[mine], test_cut)
    in_x = [spread(2 + 2 * e, images, x.at[e, mine], example_cut(e)) for e in range(examples)]
    in_cot = [spread(3 + 2 * e, cots, cot.at[e, mine], example_cut(e)) for e in range(examples)]
    out_block = [give_back(0, e, block, ob) for e in range(examples)]
    out_part = [give_back(1, e, part, op) for e in range(examples)]
    fifth = pl.ds(w * (UNITS // 4), UNITS // 4)
    k_line, k_wide, k_core = [], [], []
    for conv in range(2):
        k_line.append(
            [
                peer_copy(
                    shard.at[conv, fifth],
                    ktp.at[conv, fifth, z, c],
                    s_kz.at[conv, k - 1],
                    r_kz.at[conv, k - 1],
                    narrow=lax.rem(z + k, 4) * 2 + c,
                )
                for k in range(1, 4)
            ]
        )
        held = ktp.at[conv, fifth, :, c]
        k_wide.append(
            [
                peer_copy(held, held, s_kw.at[conv, k - 1], r_kw.at[conv, k - 1], wide=lax.rem(w + k, 4))
                for k in range(1, 4)
            ]
        )
        held = ktp.at[conv, :, :, c]
        k_core.append(peer_copy(held, held, s_kc.at[conv], r_kc.at[conv], narrow=sibling))

    start_all(in_test)
    own_kernels(weight, gain, shard)
    for conv in range(2):
        start_all(k_line[conv])
    for e in range(examples):
        start_all(in_x[e])
        start_all(in_cot[e])
    wk = make_work(work)
    fill_work(wk)
    place = (w, z, c, me)
    direction = Exchange(place, t_conv, t_gn, t_refs, t_sems)
    clipped = Exchange(place, s_conv, s_gn, s_refs, s_sems)
    direction.clear()
    clipped.clear()
    for conv in range(2):
        ktp[conv, fifth, z, c] = shard[conv, fifth]
    lane = lax.broadcasted_iota(jnp.int32, (1, LANES), 1)
    half = lane // PIX
    sign = jnp.zeros((1, LANES), f32)
    for p in range(pairs.shape[1]):
        sign = sign + jnp.where(lax.rem(pairs[0, p], AUG) == me * 2 + half, 1.0, 0.0)
        sign = sign - jnp.where(lax.rem(pairs[1, p], AUG) == me * 2 + half, 1.0, 0.0)

    def slot_weight(e):
        count = counts[me * examples + e]
        live = jnp.where(me * examples + e < alive[0], count, 0)
        each = 1.0 / jnp.full((1, LANES), count.astype(f32))
        return lambda t: jnp.where(t * 2 + half < live, each, 0.0)

    for conv in range(2):
        wait_all(k_line[conv])
        start_all(k_wide[conv])

    def kernel_arrived(conv):
        wait_all(k_wide[conv])
        k_core[conv].start()
        k_core[conv].wait()
        if conv == 0:
            unpack_params(wk, ktp[0, 18].reshape(C, LANES))
        for unit in range(18):
            wk.kf[conv, :, unit * LANES : (unit + 1) * LANES] = ktp[conv, unit].reshape(C, LANES)
        turn_kernel(wk, conv)

    kernel_arrived(0)
    wait_all(in_test)
    forward(wk, lambda t: xt[...].astype(f32), 1, None)
    kernel_arrived(1)
    backward_two(wk, lambda t: ct[...].astype(f32), lambda t: sign, 1, tgrad)
    backward_one(wk, 1, tgrad, tgn, None)
    raw_gradient(wk, tgrad, sq)

    @pl.loop(0, 18)
    def _(k):
        t_conv[k] = tgrad[k].astype(bf16).reshape(4, 2, chans, C)

    t_gn[...] = tgn[...].astype(bf16).reshape(4, 2, chans, LANES)
    direction.start_core()

    own = dt.at[c, w, z]
    line_ag, wide_ag = [], []
    for k in range(1, 4):
        to = lax.rem(z + k, 4)
        line_ag.append(peer_copy(own, own, s_fin.at[0, k - 1], r_fin.at[0, k - 1], narrow=to * 2 + c))
    for k in range(1, 4):
        to = lax.rem(w + k, 4)
        wide_ag.append(
            peer_copy(dt.at[c, w], dt.at[c, w], s_fin.at[1, k - 1], r_fin.at[1, k - 1], wide=to)
        )
    core_ag = peer_copy(dt.at[c], dt.at[c], s_fin.at[2, 0], r_fin.at[2, 0], narrow=sibling)

    def after_forward(e):
        if e == 1:
            wait_all(line_ag)
            start_all(wide_ag)
            start_all(out_block[1])

    def between(e):
        if e == 0:
            direction.start_line()

    def after_backward(e):
        if e == 0:
            direction.finish(own)
            start_all(line_ag)
            start_all(out_block[0])
        start_all(out_part[e])

    for e in range(examples):
        wait_all(in_x[e])

        def block_store(t, value):
            block[e, :, lane_tile(t)] = value.astype(bf16)

        def part_store(t, value):
            part[e, :, lane_tile(t)] = value.astype(bf16)

        forward(
            wk,
            lambda t: x[e, :, lane_tile(t)].astype(f32),
            8,
            block_store,
            direction.start_wide if e == 0 else None,
        )
        after_forward(e)
        wait_all(in_cot[e])
        backward_two(wk, lambda t: cot[e, :, lane_tile(t)].astype(f32), slot_weight(e), 8, raw.at[e])
        between(e)
        backward_one(wk, 8, raw.at[e], raw_gn.at[e], part_store)
        after_backward(e)
        sq[...] = jnp.zeros_like(sq)
        raw_gradient(wk, raw.at[e], sq)
        gn = raw_gn[e]
        square = whole_sum(sq[...]) + whole_sum(gn * gn)
        length[e] = jnp.broadcast_to(jnp.sqrt(square), (8, LANES))

    factors = [CLIP / jnp.maximum(length[e][0:1, 0:1], CLIP) for e in range(examples)]
    total = factors[0] * raw_gn[0]
    for e in range(1, examples):
        total = total + factors[e] * raw_gn[e]
    s_gn[...] = total.astype(bf16).reshape(4, 2, chans, LANES)

    @pl.loop(0, 18)
    def _(k):
        total = factors[0] * raw[0, k]
        for e in range(1, examples):
            total = total + factors[e] * raw[e, k]
        s_conv[k] = total.astype(bf16).reshape(4, 2, chans, C)

    clipped.start_core()
    wait_all(wide_ag)
    core_ag.start()
    clipped.start_wide()
    core_ag.wait()
    inner_products(dt, raw, raw_gn, length, figures, me, chans)
    figs = []
    for k in range(1, n):
        to = lax.rem(me + k, n)
        figs.append(peer_copy(figures.at[me], figures.at[me], s_fig.at[k - 1], r_fig.at[k - 1], narrow=to))
    start_all(figs)
    clipped.start_line()
    clipped.finish(red.at[w])
    finals = []
    for k in range(1, 4):
        to = lax.rem(w + k, 4)
        finals.append(peer_copy(red.at[w], red.at[w], s_fin.at[3, k - 1], r_fin.at[3, k - 1], wide=to))
    start_all(finals)
    wait_all(figs)
    slot = lax.broadcasted_iota(jnp.int32, (8, LANES), 1)
    table = jnp.zeros((8, LANES), f32)
    for k in range(n):
        for e in range(examples):
            table = table + jnp.where(slot == k * examples + e, figures[k, e], 0.0)
    norms[...] = table[0:1, : n * examples]
    infl[...] = table[1:2, : n * examples]
    for e in range(examples):
        wait_all(out_block[e])
        wait_all(out_part[e])
    wait_all(finals)
    gn_out[...] = red[0, 9]
    for conv in range(2):
        for tap in range(9):
            red_out[conv * 9 + tap, :, :LANES] = red[conv * 2, tap]
            red_out[conv * 9 + tap, :, LANES:] = red[conv * 2 + 1, tap]


def inner_products(dt, raw, raw_gn, length, figures, me, chans):
    examples = raw.shape[0]
    zero = jnp.zeros((chans, LANES), f32)

    def visit(index, carry):
        q, rest = index // 8, index % 8
        at = pl.ds(pl.multiple_of(rest * chans, chans), chans)
        lanes = pl.ds(pl.multiple_of((q % 2) * LANES, LANES), LANES)
        square = carry[0]
        sums = list(carry[1:])
        for tap in range(9):
            d = dt[rest % 2, q, rest // 2, tap].astype(f32)
            square = square + d * d
            for e in range(examples):
                sums[e] = sums[e] + d * raw[e, (q // 2) * 9 + tap, at, lanes]
        return (square, *sums)

    totals = lax.fori_loop(0, 32, visit, (zero,) * (examples + 1))

    def visit_gn(rest, carry):
        at = pl.ds(pl.multiple_of(rest * chans, chans), chans)
        d = dt[rest % 2, 0, rest // 2, 9].astype(f32)
        return (carry[0] + d * d,) + tuple(carry[1 + e] + d * raw_gn[e, at, :] for e in range(examples))

    totals = lax.fori_loop(0, 8, visit_gn, totals)
    dir_sq = whole_sum(totals[0])
    params = 18 * C * C + 4 * C
    top = lax.broadcasted_iota(jnp.int32, (8, LANES), 0)
    for e in range(examples):
        size = length[e]
        factor = CLIP / jnp.maximum(size, CLIP)
        influence = factor * whole_sum(totals[1 + e]) * math.sqrt(params) / (CLIP * jnp.sqrt(dir_sq + 1e-06))
        figures[me, e] = jnp.where(top == 0, size, influence)


def mega(images, cots, timg, tcot, weight, gain, pairs, alive, counts):
    held, chans = images.shape[0], images.shape[1]
    examples = held // 8
    out = jax.ShapeDtypeStruct
    anyspace = pl.BlockSpec(memory_space=pl.ANY)
    vmem = pl.BlockSpec(memory_space=pltpu.VMEM)
    smem = pl.BlockSpec(memory_space=pltpu.SMEM)
    dma = pltpu.SemaphoreType.DMA
    exchange = [
        pltpu.VMEM((18, 4, chans, C), bf16),
        pltpu.VMEM((4, chans, LANES), bf16),
        pltpu.VMEM((4, 10, 4, chans, LANES), bf16),
        pltpu.VMEM((3, 10, 4, chans, LANES), bf16),
        pltpu.VMEM((10, 4, chans, LANES), bf16),
        pltpu.VMEM((3, 10, chans, LANES), bf16),
    ]
    sems = [dma((2,)), dma((2,)), dma((3,)), dma((3,)), dma((3,)), dma((3,))]
    scratch = [
        pltpu.VMEM((examples, C, AUG * PIX), bf16),
        pltpu.VMEM((examples, C, AUG * PIX), bf16),
        pltpu.VMEM((C, LANES), bf16),
        pltpu.VMEM((C, LANES), bf16),
        pltpu.VMEM((2, UNITS, chans, LANES), bf16),
        pltpu.VMEM((2, UNITS, 4, 2, chans, LANES), bf16),
        pltpu.VMEM((examples, C, AUG * PIX), bf16),
        pltpu.VMEM((examples, C, AUG * PIX), bf16),
        pltpu.VMEM((examples, 18, C, C), f32),
        pltpu.VMEM((examples, C, LANES), f32),
        pltpu.VMEM((examples, 8, LANES), f32),
        pltpu.VMEM((18, C, C), f32),
        pltpu.VMEM((C, LANES), f32),
        pltpu.VMEM((8, LANES), f32),
        pltpu.VMEM((18, 4, 2, chans, C), bf16),
        pltpu.VMEM((4, 2, chans, LANES), bf16),
        pltpu.VMEM((18, 4, 2, chans, C), bf16),
        pltpu.VMEM((4, 2, chans, LANES), bf16),
        pltpu.VMEM((2, 4, 4, 10, chans, LANES), bf16),
        pltpu.VMEM((4, 10, chans, LANES), bf16),
        pltpu.VMEM((8, examples, 8, LANES), f32),
    ]
    kinds = 2 + 2 * examples
    moves = [
        dma((kinds, 7)),
        dma((kinds, 7)),
        dma((2, 3)),
        dma((2, 3)),
        dma((2, 3)),
        dma((2, 3)),
        dma((2,)),
        dma((2,)),
        dma((11,)),
        dma((2 * examples, 7)),
        dma((2 * examples, 7)),
        dma((4, 3)),
        dma((4, 3)),
        dma((7,)),
        dma((7,)),
    ]
    return pl.pallas_call(
        mega_kernel,
        out_shape=(
            out((held, chans, AUG * PIX), bf16),
            out((held, chans, AUG * PIX), bf16),
            out((18, chans, C), bf16),
            out((chans, LANES), bf16),
            out((1, held), f32),
            out((1, held), f32),
        ),
        in_specs=[anyspace] * 4 + [vmem] * 2 + [smem] * 3,
        out_specs=(anyspace, anyspace) + (vmem,) * 4,
        scratch_shapes=WORK_SCRATCH + scratch + exchange + exchange + sems + sems + moves,
        compiler_params=pltpu.CompilerParams(collective_id=0, has_side_effects=True, vmem_limit_bytes=60 << 20),
    )(images, cots, timg, tcot, weight, gain, pairs, alive, counts)


def update(weight, first, second, grad, correction, rate, decay):
    first_new = 0.5 * first + 0.5 * grad
    second_new = 0.5 * second + 0.5 * grad * grad
    step = first_new / correction / (jnp.sqrt(second_new / correction) + 1e-08)
    return weight - rate * (step + decay * weight), first_new, second_new


def tail_kernel(
    total, alive, counts, steps, ob, op, cots, red, red_gn, weight, m1, m2, noise, gw, g1, g2, gnoise, norms, infl,
    block_out, grad_out, new, low, first, second, gnew, gfirst, gsecond, norms_out, infl_out
):
    step = pl.program_id(0)
    held = ob.shape[0]
    block_out[...] = ob[...]
    image = lax.broadcasted_iota(jnp.int32, (1, AUG * PIX), 1) // PIX
    for j in range(held):
        e = step * held + j
        count = counts[e]
        live = jnp.where(e < alive[0], count, 0)
        each = 1.0 / jnp.full((1, AUG * PIX), count.astype(f32))
        row = jnp.where(image < live, each, 0.0)
        grad_out[j] = cots[j].astype(f32) * row + op[j].astype(f32)
    correction = 1.0 - jnp.exp2(jnp.full((1, 1), -steps[0].astype(f32)))
    grad = (red[...].astype(f32) + math.sqrt(total) * noise[...]) * (1.0 / total)
    value, one, two = update(weight[...], m1[...], m2[...], grad, correction, 1.0 / math.sqrt(FAN), 0.1)
    new[...] = value
    low[...] = value.astype(bf16)
    first[...] = one
    second[...] = two

    @pl.when(step == 0)
    def _():
        chans = red_gn.shape[0]
        eye = lax.broadcasted_iota(jnp.int32, (chans, chans), 0) == lax.broadcasted_iota(
            jnp.int32, (chans, chans), 1
        )
        for k in range(4):
            column = red_gn[:, k : k + 1].astype(f32)
            row = jnp.sum(jnp.where(eye, jnp.broadcast_to(column, (chans, chans)), 0.0), axis=0, keepdims=True)
            at = slice(k, k + 1)
            grad = (row + math.sqrt(total) * gnoise[at, :]) * (1.0 / total)
            value, one, two = update(gw[at, :], g1[at, :], g2[at, :], grad, correction, 0.1, 0.0)
            gnew[at, :] = value
            gfirst[at, :] = one
            gsecond[at, :] = two
        norms_out[...] = norms[...]
        infl_out[...] = infl[...]


def finish(total, alive, counts, steps, ob, op, cots, red, red_gn, conv, gn, norms, infl):
    held, chans = ob.shape[0], ob.shape[1]
    grid = 4
    rows = 18 * chans
    smem = pl.BlockSpec(memory_space=pltpu.SMEM)
    images = pl.BlockSpec((held // grid, chans, AUG * PIX), lambda i: (i, 0, 0))
    part = pl.BlockSpec((rows // grid, C), lambda i: (i, 0))

    def whole(v):
        return pl.BlockSpec(v.shape, lambda i: (0,) * len(v.shape))

    def out(v, kind=None):
        return jax.ShapeDtypeStruct(v.shape, kind or v.dtype)

    flat = [v.transpose(0, 1, 2, 4, 3).reshape(rows, C) for v in conv]
    outs = pl.pallas_call(
        functools.partial(tail_kernel, total),
        grid=(grid,),
        out_shape=[out(ob), out(ob, f32)]
        + [out(flat[0]), out(flat[0], bf16), out(flat[0]), out(flat[0])]
        + [out(gn[0])] * 3
        + [out(norms), out(infl)],
        in_specs=[smem] * 3
        + [images] * 3
        + [part, whole(red_gn)]
        + [part] * 4
        + [whole(gn[0])] * 4
        + [whole(norms), whole(infl)],
        out_specs=[images] * 2 + [part] * 4 + [whole(gn[0])] * 3 + [whole(norms), whole(infl)],
        compiler_params=pltpu.CompilerParams(vmem_limit_bytes=62 << 20),
    )(alive, counts, steps, ob, op, cots, red.reshape(rows, C), red_gn, *flat, *gn, norms, infl)

    def back(v):
        return v.reshape(2, 3, 3, chans, C).transpose(0, 1, 2, 4, 3)

    block_out, grad_out, new, low, first, second, gnew, gfirst, gsecond, norms, infl = outs
    return (
        block_out,
        grad_out,
        norms.reshape(held),
        infl.reshape(held),
        back(new),
        back(low),
        back(first),
        back(second),
        gnew,
        gfirst,
        gsecond,
    )


def pieces(v):
    high = lax.reduce_precision(v, 8, 7)
    rest = v - high
    mid = lax.reduce_precision(rest, 8, 7)
    low = rest - mid
    return high.astype(bf16), mid.astype(bf16), low.astype(bf16)


def kernel_rows(conv_weight, gn_params):
    chans = conv_weight.shape[4]
    centre = conv_weight - jnp.mean(conv_weight, axis=(1, 2, 3), keepdims=True)
    spread = jnp.mean(centre * centre, axis=(1, 2, 3), keepdims=True)
    scale = lax.rsqrt(FAN * spread + 1e-06)
    kernels = (centre * scale).astype(bf16).reshape(2, FAN, chans)
    rows = kernels.transpose(2, 0, 1).reshape(chans, KCOLS)
    small = jnp.concatenate([gn_params.T, scale.reshape(2, chans).T, jnp.zeros((chans, 2), f32)], 1)
    tail = jnp.concatenate(list(pieces(small)) + [jnp.zeros((chans, LANES - 24), bf16)], 1)
    return jnp.concatenate([rows, tail], 1)


def plain_gather(images, cots, timg, tcot, kshard, narrow):
    share = narrow // 8
    x = lax.all_to_all(images, "narrow", 0, 1, tiled=True)
    cot = lax.all_to_all(cots, "narrow", 0, 1, tiled=True)
    ktp = lax.all_gather(kshard, "narrow", axis=0, tiled=True)
    own = (lax.axis_index("narrow") // share) * LANES

    def pick(v):
        return lax.dynamic_slice_in_dim(lax.all_gather(v, "narrow", axis=0, tiled=True), own, LANES, 1)

    return x, cot, pick(timg), pick(tcot), ktp


def plain_reduce(block, part, clip_conv, test_conv, clip_gn, test_gn, raw, raw_gn, length, chans):
    examples = block.shape[0]
    ob = lax.all_to_all(block, "narrow", 1, 0, tiled=True)
    op = lax.all_to_all(part, "narrow", 1, 0, tiled=True)
    own = lax.axis_index("narrow") * chans
    rows = lax.psum(clip_conv, ("wide", "narrow"))
    rows = lax.dynamic_slice_in_dim(rows, own, chans, 1)
    gn_rows = lax.dynamic_slice_in_dim(lax.psum(clip_gn.astype(bf16), ("wide", "narrow")), own, chans, 0)
    d = lax.psum(test_conv, ("wide", "narrow")).astype(f32)
    d_gn = lax.psum(test_gn.astype(bf16), ("wide", "narrow")).astype(f32)
    dir_sq = jnp.sum(d * d) + jnp.sum(d_gn * d_gn)
    inner = jnp.sum(raw * d, axis=(1, 2, 3)) + jnp.sum(raw_gn * d_gn, axis=(1, 2))
    size = length[:, 0, 0]
    factor = CLIP / jnp.maximum(size, CLIP)
    influence = factor * inner * math.sqrt(18 * C * C + 4 * C) / (CLIP * jnp.sqrt(dir_sq + 1e-06))
    figures = lax.all_gather(jnp.stack([size, influence], 1), "narrow", axis=0)
    return ob, op, rows, gn_rows, figures[:, :, 0], figures[:, :, 1]


def local(
    images,
    cotangent,
    test_images,
    test_cotangent,
    pair_index,
    example_count,
    aug_count,
    conv_weight,
    gn_params,
    conv_moment1,
    conv_moment2,
    gn_moment1,
    gn_moment2,
    noise_conv,
    noise_gn,
    step_count,
):
    n_wide, narrow = lax.axis_size("wide"), lax.axis_size("narrow")
    held, chans = images.shape[0], images.shape[1]
    examples = held // narrow
    share = narrow // 8
    me = lax.axis_index("narrow")
    timg, tcot = test_images[0], test_cotangent[0]
    if n_wide == 4 and narrow == 8:
        weight = conv_weight.transpose(0, 1, 2, 4, 3).reshape(18, chans, C)
        outs = mega(
            images, cotangent, timg, tcot, weight, gn_params, pair_index.T, example_count, aug_count
        )
    else:
        slots = jnp.arange(AUG, dtype=jnp.int32)
        live = jnp.arange(held, dtype=jnp.int32) < example_count[0]
        weights = jnp.where(
            live[:, None] & (slots[None, :] < aug_count[:, None]),
            1.0 / aug_count.astype(f32)[:, None],
            f32(0.0),
        )
        pixels = jnp.repeat(weights, PIX, axis=1)
        pairs = pair_index % AUG
        signs = jnp.sum((pairs[:, 0:1] == slots[None, :]).astype(f32), 0) - jnp.sum(
            (pairs[:, 1:2] == slots[None, :]).astype(f32), 0
        )
        sign_pixels = jnp.repeat(signs, PIX).reshape(8, LANES) * (1.0 / share)
        kshard = kernel_rows(conv_weight, gn_params)
        wl = lax.dynamic_slice_in_dim(pixels, me * examples, examples, 0)[:, None, :]
        sg = lax.dynamic_slice_in_dim(sign_pixels, me // share, 1, 0)
        x, cot, xt, ct, ktp = plain_gather(images, cotangent, timg, tcot, kshard, narrow)
        parts = compute(x, cot, xt, ct, ktp, wl, sg)
        outs = plain_reduce(*parts, chans)
    block_out, op, red, red_gn, lengths, influence = outs
    return finish(
        held * n_wide,
        example_count,
        aug_count,
        step_count,
        block_out,
        op,
        cotangent,
        red,
        red_gn,
        (conv_weight, conv_moment1, conv_moment2, noise_conv),
        (gn_params, gn_moment1, gn_moment2, noise_gn),
        lengths.reshape(1, held),
        influence.reshape(1, held),
    )


def solution(mesh):
    in_specs = (
        P("wide", "narrow", None),
        P("wide", "narrow", None),
        P("wide", "narrow", None),
        P("wide", "narrow", None),
        P("wide", None),
        P("wide"),
        P("wide"),
        P(None, None, None, None, "narrow"),
        P(None, "narrow"),
        P(None, None, None, None, "narrow"),
        P(None, None, None, None, "narrow"),
        P(None, "narrow"),
        P(None, "narrow"),
        P(None, None, None, None, "narrow"),
        P(None, "narrow"),
        P(),
    )
    out_specs = (
        P("wide", "narrow", None),
        P("wide", "narrow", None),
        P("wide"),
        P("wide"),
        P(None, None, None, None, "narrow"),
        P(None, None, None, None, "narrow"),
        P(None, None, None, None, "narrow"),
        P(None, None, None, None, "narrow"),
        P(None, "narrow"),
        P(None, "narrow"),
        P(None, "narrow"),
    )
    return jax.shard_map(local, mesh=mesh, in_specs=in_specs, out_specs=out_specs, check_vma=False)
```

```python
import functools
import math

import jax
import jax.numpy as jnp
from jax import lax
from jax.experimental import pallas as pl
from jax.experimental.pallas import tpu as pltpu
from jax.sharding import PartitionSpec as P

C = 256
MAP = 8
GROUPS = 16
AUG = 16
PIX = MAP * MAP
FAN = 9 * C
LANES = 128
CLIP = 6.0 * C
MESH = pl.DeviceIdType.MESH
f32 = jnp.float32
bf16 = jnp.bfloat16
KCOLS = 2 * FAN


def lane_tile(index):
    return pl.ds(pl.multiple_of(index * LANES, LANES), LANES)


def group_sum(tile):
    return tile.reshape(GROUPS, C // GROUPS, LANES).sum(1)


def spread_group(rows):
    return jnp.broadcast_to(rows[:, None, :], (GROUPS, C // GROUPS, LANES)).reshape(C, LANES)


def image_sum(rows, ones):
    high = rows.astype(bf16)
    rest = rows - high.astype(f32)
    mid = rest.astype(bf16)
    low = (rest - mid.astype(f32)).astype(bf16)
    return product(jnp.concatenate([high, mid, low], axis=1), ones)


def sigmoid(z):
    return 0.5 * jnp.tanh(0.5 * z) + 0.5


def tap_masks():
    lane = lax.broadcasted_iota(jnp.int32, (1, LANES), 1)
    row = (lane // MAP) % MAP
    col = lane % MAP
    masks = []
    for r in (-1, 0, 1):
        for c in (-1, 0, 1):
            ok = (row + r >= 0) & (row + r < MAP) & (col + c >= 0) & (col + c < MAP)
            masks.append(jnp.where(ok, 1.0, 0.0).astype(f32).astype(bf16))
    return masks


def store_taps(value, col_ref, t, masks, flip):
    for tap in range(9):
        shift = (tap // 3 - 1) * MAP + (tap % 3 - 1)
        if shift == 0:
            moved = value
        else:
            moved = pltpu.roll(value, (-shift) % LANES, 1) * masks[tap]
        place = 8 - tap if flip else tap
        col_ref[place * C : (place + 1) * C, lane_tile(t)] = moved


def product(a, b):
    return jnp.dot(a, b, preferred_element_type=f32)


def product_nt(a, b):
    return lax.dot_general(a, b, (((1,), (1,)), ((), ())), preferred_element_type=f32)


class Work:
    pass


def norm_forward(wk, load, tiles, which, hat, rstd, hidden, col):
    stat = wk.stat

    @pl.loop(0, tiles, unroll=tiles)
    def _(t):
        stat[pl.ds(pl.multiple_of(t * GROUPS, GROUPS), GROUPS), :] = group_sum(load(t))

    rows = tiles * GROUPS
    stat[:rows, :] = image_sum(stat[:rows, :], wk.ones[...]) * (1.0 / (PIX * C // GROUPS))

    @pl.loop(0, tiles, unroll=tiles)
    def _(t):
        at = pl.ds(pl.multiple_of(t * GROUPS, GROUPS), GROUPS)
        centre = load(t) - spread_group(stat[at, :])
        hat[:, lane_tile(t)] = centre
        stat[at, :] = group_sum(centre * centre)

    spread = image_sum(stat[:rows, :], wk.ones[...]) * (1.0 / (PIX * C // GROUPS))
    rstd[:rows, :] = lax.rsqrt(spread + 1e-05)

    @pl.loop(0, tiles, unroll=tiles)
    def _(t):
        at = pl.ds(pl.multiple_of(t * GROUPS, GROUPS), GROUPS)
        normed = hat[:, lane_tile(t)] * spread_group(rstd[at, :])
        hat[:, lane_tile(t)] = normed
        scaled = normed * wk.gn[2 * which] + wk.gn[2 * which + 1]
        act = (scaled * sigmoid(scaled)).astype(bf16)
        hidden[:, lane_tile(t)] = act
        if col is not None:
            store_taps(act, col, t, wk.masks, False)


def norm_backward(wk, grad, tiles, which, hat, rstd, emit, acc):
    stat, stat2 = wk.stat, wk.stat2
    acc[0] = jnp.zeros((C, LANES), f32)
    acc[1] = jnp.zeros((C, LANES), f32)

    @pl.loop(0, tiles, unroll=tiles)
    def _(t):
        at = pl.ds(pl.multiple_of(t * GROUPS, GROUPS), GROUPS)
        normed = hat[:, lane_tile(t)]
        scaled = normed * wk.gn[2 * which] + wk.gn[2 * which + 1]
        gate = sigmoid(scaled)
        inner = grad[:, lane_tile(t)] * gate * (1.0 + scaled * (1.0 - gate))
        acc[0] += inner * normed
        acc[1] += inner
        inner = inner * wk.gn[2 * which]
        grad[:, lane_tile(t)] = inner
        stat[at, :] = group_sum(inner)
        stat2[at, :] = group_sum(inner * normed)

    if emit is not None:
        rows = tiles * GROUPS
        scale = 1.0 / (PIX * C // GROUPS)
        stat[:rows, :] = image_sum(stat[:rows, :], wk.ones[...]) * scale
        stat2[:rows, :] = image_sum(stat2[:rows, :], wk.ones[...]) * scale

        @pl.loop(0, tiles, unroll=tiles)
        def _(t):
            at = pl.ds(pl.multiple_of(t * GROUPS, GROUPS), GROUPS)
            value = grad[:, lane_tile(t)] - spread_group(stat[at, :])
            value = value - hat[:, lane_tile(t)] * spread_group(stat2[at, :])
            emit(t, value * spread_group(rstd[at, :]))


def matmul_cols(out, left, right, width):
    step = min(width, 256)
    for j in range(0, width, step):
        out[:, j : j + step] = product(left, right[:, j : j + step])


def fill_work(wk):
    half_a = (lax.broadcasted_iota(jnp.int32, (3 * LANES, LANES), 0) // PIX) % 2
    half_b = lax.broadcasted_iota(jnp.int32, (3 * LANES, LANES), 1) // PIX
    wk.ones[...] = jnp.where(half_a == half_b, 1.0, 0.0).astype(f32).astype(bf16)
    wk.masks = tap_masks()


def unpack_params(wk, tail):
    tail = tail.astype(f32)
    for k in range(6):
        value = tail[:, k : k + 1] + tail[:, 8 + k : 9 + k] + tail[:, 16 + k : 17 + k]
        value = jnp.broadcast_to(value, (C, LANES))
        if k < 4:
            wk.gn[k] = value
        else:
            wk.rs[k - 4] = value


def turn_kernel(wk, conv):
    for tap in range(9):
        wk.kb[conv, :, tap * C : (tap + 1) * C] = wk.kf[conv, :, tap * C : (tap + 1) * C].T


def cols(ref, width):
    return ref if width == ref.shape[1] else ref.at[:, :width]


def forward(wk, x_load, tiles, block_store, early=None):
    width = tiles * LANES
    norm_forward(wk, x_load, tiles, 0, wk.hat1, wk.rstd1, wk.hid1, wk.col)
    if early is not None:
        early()
    matmul_cols(wk.mid, wk.kf[0], cols(wk.col, width), width)
    norm_forward(
        wk,
        lambda t: wk.mid[:, lane_tile(t)],
        tiles,
        1,
        wk.hat2,
        wk.rstd2,
        wk.hid2,
        wk.col if block_store is not None else None,
    )
    if block_store is not None:
        matmul_cols(wk.mid, wk.kf[1], cols(wk.col, width), width)

        @pl.loop(0, tiles, unroll=tiles)
        def _(t):
            block_store(t, x_load(t) + wk.mid[:, lane_tile(t)])


def backward_two(wk, cot_load, weight_load, tiles, grads):
    width = tiles * LANES

    @pl.loop(0, tiles, unroll=tiles)
    def _(t):
        store_taps((cot_load(t) * weight_load(t)).astype(bf16), wk.col, t, wk.masks, True)

    matmul_cols(wk.mid, wk.kb[1], cols(wk.col, width), width)
    for tap in range(9):
        grads[9 + tap] = product_nt(wk.col[tap * C : (tap + 1) * C, :width], wk.hid2[:, :width])


def backward_one(wk, tiles, grads, gn_out, part_store):
    width = tiles * LANES

    def emit_middle(t, value):
        store_taps(value.astype(bf16), wk.col, t, wk.masks, True)

    norm_backward(wk, wk.mid, tiles, 1, wk.hat2, wk.rstd2, emit_middle, wk.acc.at[1])
    matmul_cols(wk.mid, wk.kb[0], cols(wk.col, width), width)
    for tap in range(9):
        grads[tap] = product_nt(wk.col[tap * C : (tap + 1) * C, :width], wk.hid1[:, :width])
    norm_backward(wk, wk.mid, tiles, 0, wk.hat1, wk.rstd1, part_store, wk.acc.at[0])

    lane = lax.broadcasted_iota(jnp.int32, (1, LANES), 1)
    total = jnp.zeros((C, LANES), f32)
    for k in range(4):
        one = jnp.sum(wk.acc[k // 2, k % 2], axis=1, keepdims=True)
        total = total + jnp.where(lane == k, one, 0.0)
    gn_out[...] = total


def raw_gradient(wk, grads, sq):
    rows = 32

    @pl.loop(0, C // rows)
    def _(j):
        at = pl.ds(pl.multiple_of(j * rows, rows), rows)
        for conv in range(2):
            first = jnp.zeros((rows, C), f32)
            second = jnp.zeros((rows, C), f32)
            for tap in range(9):
                g = grads[conv * 9 + tap, at, :]
                k = wk.kf[conv, at, tap * C : (tap + 1) * C].astype(f32)
                first = first + g
                second = second + g * k
            first = jnp.sum(first, axis=1, keepdims=True) * (1.0 / FAN)
            second = jnp.sum(second, axis=1, keepdims=True)
            rs = wk.rs[conv, at, 0:1]
            squares = jnp.zeros((rows, C), f32)
            for tap in range(9):
                g = grads[conv * 9 + tap, at, :]
                k = wk.kf[conv, at, tap * C : (tap + 1) * C].astype(f32)
                value = (g - first - k * second) * rs
                grads[conv * 9 + tap, at, :] = value
                squares = squares + value * value
            fold = squares[:, :LANES] + squares[:, LANES:]
            sq[...] += fold.reshape(rows // 8, 8, LANES).sum(0)


def whole_sum(tile):
    return jnp.sum(jnp.sum(tile, axis=1, keepdims=True), axis=0, keepdims=True)


WORK_SCRATCH = [
    pltpu.VMEM((2, C, FAN), bf16),
    pltpu.VMEM((2, C, FAN), bf16),
    pltpu.VMEM((FAN, AUG * PIX), bf16),
    pltpu.VMEM((C, AUG * PIX), f32),
    pltpu.VMEM((C, AUG * PIX), f32),
    pltpu.VMEM((C, AUG * PIX), f32),
    pltpu.VMEM((C, AUG * PIX), bf16),
    pltpu.VMEM((C, AUG * PIX), bf16),
    pltpu.VMEM((LANES, LANES), f32),
    pltpu.VMEM((LANES, LANES), f32),
    pltpu.VMEM((LANES, LANES), f32),
    pltpu.VMEM((LANES, LANES), f32),
    pltpu.VMEM((3 * LANES, LANES), bf16),
    pltpu.VMEM((4, C, LANES), f32),
    pltpu.VMEM((2, C, LANES), f32),
    pltpu.VMEM((2, 2, C, LANES), f32),
]
WORK_NAMES = (
    "kf",
    "kb",
    "col",
    "mid",
    "hat1",
    "hat2",
    "hid1",
    "hid2",
    "stat",
    "stat2",
    "rstd1",
    "rstd2",
    "ones",
    "gn",
    "rs",
    "acc",
)


def make_work(refs):
    wk = Work()
    for name, ref in zip(WORK_NAMES, refs):
        setattr(wk, name, ref)
    return wk


def compute_kernel(
    x, cot, xt, ct, ktp, wl, sg, block, part, clipped, test, clipped_gn, test_gn, raw, raw_gn, length, *scratch
):
    examples = x.shape[0]
    wk = make_work(scratch[:-2])
    tgrad, sq = scratch[-2:]
    fill_work(wk)
    unpack_params(wk, ktp[:, KCOLS : KCOLS + LANES])
    for conv in range(2):
        wk.kf[conv] = ktp[:, conv * FAN : (conv + 1) * FAN]
        turn_kernel(wk, conv)
    forward(wk, lambda t: xt[...].astype(f32), 1, None)
    backward_two(wk, lambda t: ct[...].astype(f32), lambda t: sg[...], 1, tgrad)
    backward_one(wk, 1, tgrad, test_gn, None)
    raw_gradient(wk, tgrad, sq)

    @pl.loop(0, 18)
    def _(k):
        test[k] = tgrad[k].astype(bf16)

    sq[...] = jnp.zeros_like(sq)

    @pl.loop(0, examples)
    def _(e):
        def block_store(t, value):
            block[e, :, lane_tile(t)] = value.astype(bf16)

        def part_store(t, value):
            part[e, :, lane_tile(t)] = value.astype(bf16)

        forward(wk, lambda t: x[e, :, lane_tile(t)].astype(f32), 8, block_store)
        backward_two(
            wk,
            lambda t: cot[e, :, lane_tile(t)].astype(f32),
            lambda t: wl[e, :, lane_tile(t)],
            8,
            raw.at[e],
        )
        backward_one(wk, 8, raw.at[e], raw_gn.at[e], part_store)
        sq[...] = jnp.zeros_like(sq)
        raw_gradient(wk, raw.at[e], sq)
        gn = raw_gn[e]
        square = whole_sum(sq[...]) + whole_sum(gn * gn)
        length[e] = jnp.broadcast_to(jnp.sqrt(square), (8, LANES))

    factors = [CLIP / jnp.maximum(length[e][0:1, 0:1], CLIP) for e in range(examples)]
    total = factors[0] * raw_gn[0]
    for e in range(1, examples):
        total = total + factors[e] * raw_gn[e]
    clipped_gn[...] = total

    @pl.loop(0, 18)
    def _(k):
        total = factors[0] * raw[0, k]
        for e in range(1, examples):
            total = total + factors[e] * raw[e, k]
        clipped[k] = total.astype(bf16)


def compute(x, cot, xt, ct, ktp, wl, sg):
    examples = x.shape[0]
    out = jax.ShapeDtypeStruct
    shapes = (
        out(x.shape, bf16),
        out(x.shape, bf16),
        out((18, C, C), bf16),
        out((18, C, C), bf16),
        out((C, LANES), f32),
        out((C, LANES), f32),
        out((examples, 18, C, C), f32),
        out((examples, C, LANES), f32),
        out((examples, 8, LANES), f32),
    )
    spec = pl.BlockSpec(memory_space=pltpu.VMEM)
    return pl.pallas_call(
        compute_kernel,
        out_shape=shapes,
        in_specs=[spec] * 7,
        out_specs=(spec,) * 9,
        scratch_shapes=WORK_SCRATCH + [pltpu.VMEM((18, C, C), f32), pltpu.VMEM((8, LANES), f32)],
        compiler_params=pltpu.CompilerParams(vmem_limit_bytes=58 << 20),
    )(x, cot, xt, ct, ktp, wl, sg)


def peer_copy(src, dst, send, recv, **where):
    return pltpu.make_async_remote_copy(
        src_ref=src, dst_ref=dst, send_sem=send, recv_sem=recv, device_id=where, device_id_type=MESH
    )


def greet(peers):
    barrier = pltpu.get_barrier_semaphore()
    for where in peers:
        pl.semaphore_signal(barrier, inc=1, device_id=where, device_id_type=MESH)
    pl.semaphore_wait(barrier, len(peers))


def near_of(z, c):
    return (z + 1 - 2 * (z % 2)) * 2 + c


def far_of(z, c):
    return lax.rem(z + 2, 4) * 2 + c


GRID = 2
A = 4
B = 8
D = 5
E = 6
F = 2


class Exchange:
    def __init__(self, place, conv, gn, refs, sems):
        self.w, self.z, self.c, self.me = place
        self.conv, self.gn = conv, gn
        self.cb, self.cg, self.half, self.wb, self.quarter, self.nb, self.mid, self.fb = refs
        s_core, r_core, s_wide, r_wide, s_z, r_z = sems
        w, z, c = self.w, self.z, self.c
        sibling = self.me + 1 - 2 * c
        self.core = [
            peer_copy(conv.at[:, :, 1 - c], self.cb, s_core.at[0], r_core.at[0], narrow=sibling),
            peer_copy(gn.at[:, 1 - c], self.cg, s_core.at[1], r_core.at[1], narrow=sibling),
        ]
        self.wide = []
        for k in range(1, 4):
            to = lax.rem(w + k, 4)
            self.wide.append(
                peer_copy(self.half.at[to], self.wb.at[k - 1], s_wide.at[k - 1], r_wide.at[k - 1], wide=to)
            )
        self.p, self.h = z % 2, z // 2
        self.near = peer_copy(
            self.quarter.at[:, :, 1 - self.p], self.nb, s_z.at[0], r_z.at[0], narrow=near_of(z, c)
        )
        self.far = peer_copy(self.mid.at[:, 1 - self.h], self.fb, s_z.at[1], r_z.at[1], narrow=far_of(z, c))

    def clear(self):
        for q in range(1, 4):
            self.half[q, 9] = jnp.zeros_like(self.half[q, 9])

    def start_core(self):
        start_all(self.core)

    def start_wide(self):
        wait_all(self.core)
        half, c = self.half, self.c
        for k in range(2):

            @pl.loop(0, 9)
            def _(tap):
                total = self.conv[k * 9 + tap, :, c].astype(f32) + self.cb[k * 9 + tap].astype(f32)
                half[k * 2, tap] = total[:, :, :LANES].astype(bf16)
                half[k * 2 + 1, tap] = total[:, :, LANES:].astype(bf16)

        half[0, 9] = (self.gn[:, c].astype(f32) + self.cg[...].astype(f32)).astype(bf16)
        start_all(self.wide)

    def start_near(self):
        wait_all(self.wide)

        @pl.loop(0, 10)
        def _(tap):
            for zz in range(4):
                total = self.half[self.w, tap, zz].astype(f32)
                for k in range(3):
                    total = total + self.wb[k, tap, zz].astype(f32)
                self.quarter[tap, zz // 2, zz % 2] = total.astype(bf16)

        start_all([self.near])

    def start_far(self):
        wait_all([self.near])

        @pl.loop(0, 10)
        def _(tap):
            total = self.quarter[tap, :, self.p].astype(f32) + self.nb[tap].astype(f32)
            self.mid[tap] = total.astype(bf16)

        start_all([self.far])

    def finish(self, out):
        wait_all([self.far])

        @pl.loop(0, 10)
        def _(tap):
            out[tap] = (self.mid[tap, self.h].astype(f32) + self.fb[tap].astype(f32)).astype(bf16)


def start_all(copies):
    for copy in copies:
        copy.start()


def wait_all(copies):
    for copy in copies:
        copy.wait()


UNITS = 20


def own_kernels(weight, gain, shard, sent):
    chans = weight.shape[1]
    lane = lax.broadcasted_iota(jnp.int32, (chans, LANES), 1)
    eye = lax.broadcasted_iota(jnp.int32, (chans, chans), 0) == lax.broadcasted_iota(
        jnp.int32, (chans, chans), 1
    )
    values = [
        jnp.sum(jnp.where(eye, jnp.broadcast_to(gain[k : k + 1, :], (chans, chans)), 0.0), axis=1, keepdims=True)
        for k in range(4)
    ]
    means = []
    for conv in range(2):
        total = jnp.zeros((chans, C), f32)
        for tap in range(9):
            total = total + weight[conv * 9 + tap]
        mean = jnp.sum(total, axis=1, keepdims=True) * (1.0 / FAN)
        total = jnp.zeros((chans, C), f32)
        for tap in range(9):
            centre = weight[conv * 9 + tap] - mean
            total = total + centre * centre
        spread = jnp.sum(total, axis=1, keepdims=True) * (1.0 / FAN)
        means.append(mean)
        values.append(lax.rsqrt(FAN * spread + 1e-06))
    tail = jnp.zeros((chans, LANES), f32)
    for k, value in enumerate(values):
        high = value.astype(bf16).astype(f32)
        mid = (value - high).astype(bf16).astype(f32)
        low = value - high - mid
        tail = tail + jnp.where(lane == k, high, 0.0)
        tail = tail + jnp.where(lane == 8 + k, mid, 0.0)
        tail = tail + jnp.where(lane == 16 + k, low, 0.0)
    zero = jnp.zeros((chans, LANES), bf16)
    for conv in range(2):
        for tap in range(9):
            kernel = ((weight[conv * 9 + tap] - means[conv]) * values[4 + conv]).astype(bf16)
            shard[conv, 2 * tap] = kernel[:, :LANES]
            shard[conv, 2 * tap + 1] = kernel[:, LANES:]
        shard[conv, 18] = tail.astype(bf16) if conv == 0 else zero
        shard[conv, 19] = zero
        sent(conv)


def mega_kernel(
    images, cots, timg, tcot, weight, gain, pairs, alive, counts, ob, op, red_out, gn_out, norms, infl, *scratch
):
    n = 8
    me = lax.axis_index("narrow")
    w = lax.axis_index("wide")
    z, c = me // 2, me % 2
    sibling = me + 1 - 2 * c
    examples = images.shape[0] // n
    chans = images.shape[1]
    mine = pl.ds(pl.multiple_of(me * chans, chans), chans)
    work, rest = scratch[: len(WORK_SCRATCH)], scratch[len(WORK_SCRATCH) :]
    x, cot, xt, ct, shard, ktp, block, part, raw, raw_gn, length, tgrad, tgn, sq = rest[:14]
    s_conv, s_gn, t_conv, t_gn, dt, red, figures = rest[14:21]
    s_refs, t_refs = rest[21:29], rest[29:37]
    s_sems, t_sems = rest[37:43], rest[43:49]
    s_in, r_in, s_kz, r_kz, s_kw, r_kw, s_kc, r_kc, s_loc = rest[49:58]
    s_out, r_out, s_fin, r_fin, s_fig, r_fig = rest[58:64]
    greet(
        [{"narrow": lax.rem(me + k, n)} for k in range(1, n)]
        + [{"wide": lax.rem(w + k, 4)} for k in range(1, 4)]
    )

    def spread(a, src, dst, cut):
        copies = []
        for k in range(n):
            to = lax.rem(me + k, n)
            if k == 0:
                copies.append(pltpu.make_async_copy(cut(src, to), dst, s_loc.at[a]))
            else:
                copies.append(peer_copy(cut(src, to), dst, s_in.at[a, k - 1], r_in.at[a, k - 1], narrow=to))
        return copies

    def test_cut(src, to):
        return src.at[:, pl.ds(pl.multiple_of(to * LANES, LANES), LANES)]

    def example_cut(e):
        return lambda src, to: src.at[to * examples + e]

    def give_back(a, e, src, dst):
        copies = []
        for k in range(n):
            to = lax.rem(me + k, n)
            piece = src.at[e, pl.ds(pl.multiple_of(to * chans, chans), chans)]
            place = dst.at[me * examples + e]
            slot = a * examples + e
            if k == 0:
                copies.append(pltpu.make_async_copy(piece, place, s_loc.at[6 + slot]))
            else:
                copies.append(peer_copy(piece, place, s_out.at[slot, k - 1], r_out.at[slot, k - 1], narrow=to))
        return copies

    in_test = spread(0, timg, xt.at[mine], test_cut) + spread(1, tcot, ct.at[mine], test_cut)
    in_x = [spread(2 + 2 * e, images, x.at[e, mine], example_cut(e)) for e in range(examples)]
    in_cot = [spread(3 + 2 * e, cots, cot.at[e, mine], example_cut(e)) for e in range(examples)]
    out_block = [give_back(0, e, block, ob) for e in range(examples)]
    out_part = [give_back(1, e, part, op) for e in range(examples)]
    fifth = pl.ds(w * (UNITS // 4), UNITS // 4)
    h, p = z // 2, z % 2
    k_far, k_near, k_wide, k_core = [], [], [], []
    for conv in range(2):
        k_far.append(
            [
                peer_copy(
                    shard.at[conv, fifth],
                    ktp.at[conv, fifth, h, p, c],
                    s_kz.at[conv, 0],
                    r_kz.at[conv, 0],
                    narrow=far_of(z, c),
                )
            ]
        )
        held = ktp.at[conv, fifth, :, p, c]
        k_near.append([peer_copy(held, held, s_kz.at[conv, 1], r_kz.at[conv, 1], narrow=near_of(z, c))])
        held = ktp.at[conv, fifth, :, :, c]
        k_wide.append(
            [
                peer_copy(held, held, s_kw.at[conv, k - 1], r_kw.at[conv, k - 1], wide=lax.rem(w + k, 4))
                for k in range(1, 4)
            ]
        )
        held = ktp.at[conv, :, :, :, c]
        k_core.append([peer_copy(held, held, s_kc.at[conv], r_kc.at[conv], narrow=sibling)])

    own_kernels(weight, gain, shard, lambda conv: start_all(k_far[conv]))
    start_all(in_test)
    for conv in range(2):
        ktp[conv, fifth, h, p, c] = shard[conv, fifth]
    for conv in range(2):
        wait_all(k_far[conv])
        start_all(k_near[conv])
    for e in range(examples):
        start_all(in_x[e])
        start_all(in_cot[e])
    wk = make_work(work)
    fill_work(wk)
    place = (w, z, c, me)
    direction = Exchange(place, t_conv, t_gn, t_refs, t_sems)
    clipped = Exchange(place, s_conv, s_gn, s_refs, s_sems)
    direction.clear()
    clipped.clear()
    lane = lax.broadcasted_iota(jnp.int32, (1, LANES), 1)
    half = lane // PIX
    sign = jnp.zeros((1, LANES), f32)
    for p in range(pairs.shape[1]):
        sign = sign + jnp.where(lax.rem(pairs[0, p], AUG) == me * 2 + half, 1.0, 0.0)
        sign = sign - jnp.where(lax.rem(pairs[1, p], AUG) == me * 2 + half, 1.0, 0.0)

    def slot_weight(e):
        count = counts[me * examples + e]
        live = jnp.where(me * examples + e < alive[0], count, 0)
        each = 1.0 / jnp.full((1, LANES), count.astype(f32))
        return lambda t: jnp.where(t * 2 + half < live, each, 0.0)

    for conv in range(2):
        wait_all(k_near[conv])
        start_all(k_wide[conv])

    def kernel_arrived(conv):
        wait_all(k_wide[conv])
        start_all(k_core[conv])
        wait_all(k_core[conv])
        if conv == 0:
            unpack_params(wk, ktp[0, 18].reshape(C, LANES))
        for unit in range(18):
            wk.kf[conv, :, unit * LANES : (unit + 1) * LANES] = ktp[conv, unit].reshape(C, LANES)
        turn_kernel(wk, conv)

    kernel_arrived(0)
    wait_all(in_test)
    forward(wk, lambda t: xt[...].astype(f32), 1, None)
    kernel_arrived(1)
    backward_two(wk, lambda t: ct[...].astype(f32), lambda t: sign, 1, tgrad)
    backward_one(wk, 1, tgrad, tgn, None)
    raw_gradient(wk, tgrad, sq)

    @pl.loop(0, 18)
    def _(k):
        t_conv[k] = tgrad[k].astype(bf16).reshape(4, 2, chans, C)

    t_gn[...] = tgn[...].astype(bf16).reshape(4, 2, chans, LANES)
    direction.start_core()

    own = dt.at[c, w, z // 2, z % 2]
    both = dt.at[c, w, :, z % 2]
    far_ag = [peer_copy(own, own, s_fin.at[0, 0], r_fin.at[0, 0], narrow=far_of(z, c))]
    near_ag = [peer_copy(both, both, s_fin.at[0, 1], r_fin.at[0, 1], narrow=near_of(z, c))]
    wide_ag = []
    for k in range(1, 4):
        to = lax.rem(w + k, 4)
        wide_ag.append(
            peer_copy(dt.at[c, w], dt.at[c, w], s_fin.at[1, k - 1], r_fin.at[1, k - 1], wide=to)
        )
    core_ag = [peer_copy(dt.at[c], dt.at[c], s_fin.at[2, 0], r_fin.at[2, 0], narrow=sibling)]

    def early_forward(e):
        if e == 0:
            direction.start_wide()

    def between(e):
        if e == 1:
            direction.start_far()
            start_all(out_block[0][A:])

    def after_raw(e):
        if e == 0:
            direction.start_near()
            start_all(out_block[0][:A])
        else:
            direction.finish(own)
            start_all(far_ag)
            start_all(out_part[0][:D])

    for e in range(examples):
        wait_all(in_x[e])

        def block_store(t, value):
            block[e, :, lane_tile(t)] = value.astype(bf16)

        def part_store(t, value):
            part[e, :, lane_tile(t)] = value.astype(bf16)

        forward(
            wk,
            lambda t: x[e, :, lane_tile(t)].astype(f32),
            8,
            block_store,
            functools.partial(early_forward, e),
        )
        wait_all(in_cot[e])
        backward_two(wk, lambda t: cot[e, :, lane_tile(t)].astype(f32), slot_weight(e), 8, raw.at[e])
        between(e)
        backward_one(wk, 8, raw.at[e], raw_gn.at[e], part_store)
        sq[...] = jnp.zeros_like(sq)
        raw_gradient(wk, raw.at[e], sq)
        gn = raw_gn[e]
        square = whole_sum(sq[...]) + whole_sum(gn * gn)
        length[e] = jnp.broadcast_to(jnp.sqrt(square), (8, LANES))
        after_raw(e)

    factors = [CLIP / jnp.maximum(length[e][0:1, 0:1], CLIP) for e in range(examples)]
    total = factors[0] * raw_gn[0]
    for e in range(1, examples):
        total = total + factors[e] * raw_gn[e]
    s_gn[...] = total.astype(bf16).reshape(4, 2, chans, LANES)

    @pl.loop(0, 18)
    def _(k):
        total = factors[0] * raw[0, k]
        for e in range(1, examples):
            total = total + factors[e] * raw[e, k]
        s_conv[k] = total.astype(bf16).reshape(4, 2, chans, C)

    clipped.start_core()
    clipped.start_wide()
    wait_all(far_ag)
    start_all(near_ag)
    start_all(out_part[0][D:])
    start_all(out_block[1][:E])
    wait_all(near_ag)
    start_all(wide_ag)
    clipped.start_near()
    start_all(out_block[1][E:])
    start_all(out_part[1][:F])
    clipped.start_far()
    start_all(out_part[1][F:])
    clipped.finish(red.at[w])
    finals = []
    for k in range(1, 4):
        to = lax.rem(w + k, 4)
        finals.append(peer_copy(red.at[w], red.at[w], s_fin.at[3, k - 1], r_fin.at[3, k - 1], wide=to))
    start_all(finals)
    wait_all(wide_ag)
    start_all(core_ag)
    wait_all(core_ag)
    inner_products(dt, raw, raw_gn, length, figures, me, chans)
    figs = []
    for k in range(1, n):
        to = lax.rem(me + k, n)
        figs.append(peer_copy(figures.at[me], figures.at[me], s_fig.at[k - 1], r_fig.at[k - 1], narrow=to))
    start_all(figs)
    wait_all(figs)
    slot = lax.broadcasted_iota(jnp.int32, (8, LANES), 1)
    table = jnp.zeros((8, LANES), f32)
    for k in range(n):
        for e in range(examples):
            table = table + jnp.where(slot == k * examples + e, figures[k, e], 0.0)
    norms[...] = table[0:1, : n * examples]
    infl[...] = table[1:2, : n * examples]
    for e in range(examples):
        wait_all(out_block[e])
        wait_all(out_part[e])
    wait_all(finals)
    gn_out[...] = red[0, 9]
    for conv in range(2):
        for tap in range(9):
            red_out[conv * 9 + tap, :, :LANES] = red[conv * 2, tap]
            red_out[conv * 9 + tap, :, LANES:] = red[conv * 2 + 1, tap]


def inner_products(dt, raw, raw_gn, length, figures, me, chans):
    examples = raw.shape[0]
    zero = jnp.zeros((chans, LANES), f32)

    def visit(index, carry):
        q, rest = index // 8, index % 8
        at = pl.ds(pl.multiple_of(rest * chans, chans), chans)
        lanes = pl.ds(pl.multiple_of((q % 2) * LANES, LANES), LANES)
        square = carry[0]
        sums = list(carry[1:])
        for tap in range(9):
            d = dt[rest % 2, q, rest // 4, (rest // 2) % 2, tap].astype(f32)
            square = square + d * d
            for e in range(examples):
                sums[e] = sums[e] + d * raw[e, (q // 2) * 9 + tap, at, lanes]
        return (square, *sums)

    totals = lax.fori_loop(0, 32, visit, (zero,) * (examples + 1))

    def visit_gn(rest, carry):
        at = pl.ds(pl.multiple_of(rest * chans, chans), chans)
        d = dt[rest % 2, 0, rest // 4, (rest // 2) % 2, 9].astype(f32)
        return (carry[0] + d * d,) + tuple(carry[1 + e] + d * raw_gn[e, at, :] for e in range(examples))

    totals = lax.fori_loop(0, 8, visit_gn, totals)
    dir_sq = whole_sum(totals[0])
    params = 18 * C * C + 4 * C
    top = lax.broadcasted_iota(jnp.int32, (8, LANES), 0)
    for e in range(examples):
        size = length[e]
        factor = CLIP / jnp.maximum(size, CLIP)
        influence = factor * whole_sum(totals[1 + e]) * math.sqrt(params) / (CLIP * jnp.sqrt(dir_sq + 1e-06))
        figures[me, e] = jnp.where(top == 0, size, influence)


def mega(images, cots, timg, tcot, weight, gain, pairs, alive, counts):
    held, chans = images.shape[0], images.shape[1]
    examples = held // 8
    out = jax.ShapeDtypeStruct
    anyspace = pl.BlockSpec(memory_space=pl.ANY)
    vmem = pl.BlockSpec(memory_space=pltpu.VMEM)
    smem = pl.BlockSpec(memory_space=pltpu.SMEM)
    dma = pltpu.SemaphoreType.DMA
    exchange = [
        pltpu.VMEM((18, 4, chans, C), bf16),
        pltpu.VMEM((4, chans, LANES), bf16),
        pltpu.VMEM((4, 10, 4, chans, LANES), bf16),
        pltpu.VMEM((3, 10, 4, chans, LANES), bf16),
        pltpu.VMEM((10, 2, 2, chans, LANES), bf16),
        pltpu.VMEM((10, 2, chans, LANES), bf16),
        pltpu.VMEM((10, 2, chans, LANES), bf16),
        pltpu.VMEM((10, chans, LANES), bf16),
    ]
    sems = [dma((2,)), dma((2,)), dma((3,)), dma((3,)), dma((2,)), dma((2,))]
    scratch = [
        pltpu.VMEM((examples, C, AUG * PIX), bf16),
        pltpu.VMEM((examples, C, AUG * PIX), bf16),
        pltpu.VMEM((C, LANES), bf16),
        pltpu.VMEM((C, LANES), bf16),
        pltpu.VMEM((2, UNITS, chans, LANES), bf16),
        pltpu.VMEM((2, UNITS, 2, 2, 2, chans, LANES), bf16),
        pltpu.VMEM((examples, C, AUG * PIX), bf16),
        pltpu.VMEM((examples, C, AUG * PIX), bf16),
        pltpu.VMEM((examples, 18, C, C), f32),
        pltpu.VMEM((examples, C, LANES), f32),
        pltpu.VMEM((examples, 8, LANES), f32),
        pltpu.VMEM((18, C, C), f32),
        pltpu.VMEM((C, LANES), f32),
        pltpu.VMEM((8, LANES), f32),
        pltpu.VMEM((18, 4, 2, chans, C), bf16),
        pltpu.VMEM((4, 2, chans, LANES), bf16),
        pltpu.VMEM((18, 4, 2, chans, C), bf16),
        pltpu.VMEM((4, 2, chans, LANES), bf16),
        pltpu.VMEM((2, 4, 2, 2, 10, chans, LANES), bf16),
        pltpu.VMEM((4, 10, chans, LANES), bf16),
        pltpu.VMEM((8, examples, 8, LANES), f32),
    ]
    kinds = 2 + 2 * examples
    moves = [
        dma((kinds, 7)),
        dma((kinds, 7)),
        dma((2, 3)),
        dma((2, 3)),
        dma((2, 3)),
        dma((2, 3)),
        dma((2,)),
        dma((2,)),
        dma((11,)),
        dma((2 * examples, 7)),
        dma((2 * examples, 7)),
        dma((4, 3)),
        dma((4, 3)),
        dma((7,)),
        dma((7,)),
    ]
    return pl.pallas_call(
        mega_kernel,
        out_shape=(
            out((held, chans, AUG * PIX), bf16),
            out((held, chans, AUG * PIX), bf16),
            out((18, chans, C), bf16),
            out((chans, LANES), bf16),
            out((1, held), f32),
            out((1, held), f32),
        ),
        in_specs=[anyspace] * 4 + [vmem] * 2 + [smem] * 3,
        out_specs=(anyspace, anyspace) + (vmem,) * 4,
        scratch_shapes=WORK_SCRATCH + scratch + exchange + exchange + sems + sems + moves,
        compiler_params=pltpu.CompilerParams(collective_id=0, has_side_effects=True, vmem_limit_bytes=60 << 20),
    )(images, cots, timg, tcot, weight, gain, pairs, alive, counts)


def update(weight, first, second, grad, correction, rate, decay):
    first_new = 0.5 * first + 0.5 * grad
    second_new = 0.5 * second + 0.5 * grad * grad
    step = first_new / correction / (jnp.sqrt(second_new / correction) + 1e-08)
    return weight - rate * (step + decay * weight), first_new, second_new


def tail_kernel(
    total, alive, counts, steps, ob, op, cots, red, red_gn, weight, m1, m2, noise, gw, g1, g2, gnoise, norms, infl,
    block_out, grad_out, new, low, first, second, gnew, gfirst, gsecond, norms_out, infl_out
):
    step = pl.program_id(0)
    held = ob.shape[0]
    block_out[...] = ob[...]
    image = lax.broadcasted_iota(jnp.int32, (1, AUG * PIX), 1) // PIX
    for j in range(held):
        e = step * held + j
        count = counts[e]
        live = jnp.where(e < alive[0], count, 0)
        each = 1.0 / jnp.full((1, AUG * PIX), count.astype(f32))
        row = jnp.where(image < live, each, 0.0)
        grad_out[j] = cots[j].astype(f32) * row + op[j].astype(f32)
    correction = 1.0 - jnp.exp2(jnp.full((1, 1), -steps[0].astype(f32)))
    grad = (red[...].astype(f32) + math.sqrt(total) * noise[...]) * (1.0 / total)
    value, one, two = update(weight[...], m1[...], m2[...], grad, correction, 1.0 / math.sqrt(FAN), 0.1)
    new[...] = value
    low[...] = value.astype(bf16)
    first[...] = one
    second[...] = two

    @pl.when(step == 0)
    def _():
        chans = red_gn.shape[0]
        eye = lax.broadcasted_iota(jnp.int32, (chans, chans), 0) == lax.broadcasted_iota(
            jnp.int32, (chans, chans), 1
        )
        for k in range(4):
            column = red_gn[:, k : k + 1].astype(f32)
            row = jnp.sum(jnp.where(eye, jnp.broadcast_to(column, (chans, chans)), 0.0), axis=0, keepdims=True)
            at = slice(k, k + 1)
            grad = (row + math.sqrt(total) * gnoise[at, :]) * (1.0 / total)
            value, one, two = update(gw[at, :], g1[at, :], g2[at, :], grad, correction, 0.1, 0.0)
            gnew[at, :] = value
            gfirst[at, :] = one
            gsecond[at, :] = two
        norms_out[...] = norms[...]
        infl_out[...] = infl[...]


def finish(total, alive, counts, steps, ob, op, cots, red, red_gn, conv, gn, norms, infl):
    held, chans = ob.shape[0], ob.shape[1]
    grid = GRID
    rows = 18 * chans
    smem = pl.BlockSpec(memory_space=pltpu.SMEM)
    images = pl.BlockSpec((held // grid, chans, AUG * PIX), lambda i: (i, 0, 0))
    part = pl.BlockSpec((rows // grid, C), lambda i: (i, 0))

    def whole(v):
        return pl.BlockSpec(v.shape, lambda i: (0,) * len(v.shape))

    def out(v, kind=None):
        return jax.ShapeDtypeStruct(v.shape, kind or v.dtype)

    flat = [v.transpose(0, 1, 2, 4, 3).reshape(rows, C) for v in conv]
    outs = pl.pallas_call(
        functools.partial(tail_kernel, total),
        grid=(grid,),
        out_shape=[out(ob), out(ob, f32)]
        + [out(flat[0]), out(flat[0], bf16), out(flat[0]), out(flat[0])]
        + [out(gn[0])] * 3
        + [out(norms), out(infl)],
        in_specs=[smem] * 3
        + [images] * 3
        + [part, whole(red_gn)]
        + [part] * 4
        + [whole(gn[0])] * 4
        + [whole(norms), whole(infl)],
        out_specs=[images] * 2 + [part] * 4 + [whole(gn[0])] * 3 + [whole(norms), whole(infl)],
        compiler_params=pltpu.CompilerParams(vmem_limit_bytes=62 << 20),
    )(alive, counts, steps, ob, op, cots, red.reshape(rows, C), red_gn, *flat, *gn, norms, infl)

    def back(v):
        return v.reshape(2, 3, 3, chans, C).transpose(0, 1, 2, 4, 3)

    block_out, grad_out, new, low, first, second, gnew, gfirst, gsecond, norms, infl = outs
    return (
        block_out,
        grad_out,
        norms.reshape(held),
        infl.reshape(held),
        back(new),
        back(low),
        back(first),
        back(second),
        gnew,
        gfirst,
        gsecond,
    )


def pieces(v):
    high = lax.reduce_precision(v, 8, 7)
    rest = v - high
    mid = lax.reduce_precision(rest, 8, 7)
    low = rest - mid
    return high.astype(bf16), mid.astype(bf16), low.astype(bf16)


def kernel_rows(conv_weight, gn_params):
    chans = conv_weight.shape[4]
    centre = conv_weight - jnp.mean(conv_weight, axis=(1, 2, 3), keepdims=True)
    spread = jnp.mean(centre * centre, axis=(1, 2, 3), keepdims=True)
    scale = lax.rsqrt(FAN * spread + 1e-06)
    kernels = (centre * scale).astype(bf16).reshape(2, FAN, chans)
    rows = kernels.transpose(2, 0, 1).reshape(chans, KCOLS)
    small = jnp.concatenate([gn_params.T, scale.reshape(2, chans).T, jnp.zeros((chans, 2), f32)], 1)
    tail = jnp.concatenate(list(pieces(small)) + [jnp.zeros((chans, LANES - 24), bf16)], 1)
    return jnp.concatenate([rows, tail], 1)


def plain_gather(images, cots, timg, tcot, kshard, narrow):
    share = narrow // 8
    x = lax.all_to_all(images, "narrow", 0, 1, tiled=True)
    cot = lax.all_to_all(cots, "narrow", 0, 1, tiled=True)
    ktp = lax.all_gather(kshard, "narrow", axis=0, tiled=True)
    own = (lax.axis_index("narrow") // share) * LANES

    def pick(v):
        return lax.dynamic_slice_in_dim(lax.all_gather(v, "narrow", axis=0, tiled=True), own, LANES, 1)

    return x, cot, pick(timg), pick(tcot), ktp


def plain_reduce(block, part, clip_conv, test_conv, clip_gn, test_gn, raw, raw_gn, length, chans):
    examples = block.shape[0]
    ob = lax.all_to_all(block, "narrow", 1, 0, tiled=True)
    op = lax.all_to_all(part, "narrow", 1, 0, tiled=True)
    own = lax.axis_index("narrow") * chans
    rows = lax.psum(clip_conv, ("wide", "narrow"))
    rows = lax.dynamic_slice_in_dim(rows, own, chans, 1)
    gn_rows = lax.dynamic_slice_in_dim(lax.psum(clip_gn.astype(bf16), ("wide", "narrow")), own, chans, 0)
    d = lax.psum(test_conv, ("wide", "narrow")).astype(f32)
    d_gn = lax.psum(test_gn.astype(bf16), ("wide", "narrow")).astype(f32)
    dir_sq = jnp.sum(d * d) + jnp.sum(d_gn * d_gn)
    inner = jnp.sum(raw * d, axis=(1, 2, 3)) + jnp.sum(raw_gn * d_gn, axis=(1, 2))
    size = length[:, 0, 0]
    factor = CLIP / jnp.maximum(size, CLIP)
    influence = factor * inner * math.sqrt(18 * C * C + 4 * C) / (CLIP * jnp.sqrt(dir_sq + 1e-06))
    figures = lax.all_gather(jnp.stack([size, influence], 1), "narrow", axis=0)
    return ob, op, rows, gn_rows, figures[:, :, 0], figures[:, :, 1]


def local(
    images,
    cotangent,
    test_images,
    test_cotangent,
    pair_index,
    example_count,
    aug_count,
    conv_weight,
    gn_params,
    conv_moment1,
    conv_moment2,
    gn_moment1,
    gn_moment2,
    noise_conv,
    noise_gn,
    step_count,
):
    n_wide, narrow = lax.axis_size("wide"), lax.axis_size("narrow")
    held, chans = images.shape[0], images.shape[1]
    examples = held // narrow
    share = narrow // 8
    me = lax.axis_index("narrow")
    timg, tcot = test_images[0], test_cotangent[0]
    if n_wide == 4 and narrow == 8:
        weight = conv_weight.transpose(0, 1, 2, 4, 3).reshape(18, chans, C)
        outs = mega(
            images, cotangent, timg, tcot, weight, gn_params, pair_index.T, example_count, aug_count
        )
    else:
        slots = jnp.arange(AUG, dtype=jnp.int32)
        live = jnp.arange(held, dtype=jnp.int32) < example_count[0]
        weights = jnp.where(
            live[:, None] & (slots[None, :] < aug_count[:, None]),
            1.0 / aug_count.astype(f32)[:, None],
            f32(0.0),
        )
        pixels = jnp.repeat(weights, PIX, axis=1)
        pairs = pair_index % AUG
        signs = jnp.sum((pairs[:, 0:1] == slots[None, :]).astype(f32), 0) - jnp.sum(
            (pairs[:, 1:2] == slots[None, :]).astype(f32), 0
        )
        sign_pixels = jnp.repeat(signs, PIX).reshape(8, LANES) * (1.0 / share)
        kshard = kernel_rows(conv_weight, gn_params)
        wl = lax.dynamic_slice_in_dim(pixels, me * examples, examples, 0)[:, None, :]
        sg = lax.dynamic_slice_in_dim(sign_pixels, me // share, 1, 0)
        x, cot, xt, ct, ktp = plain_gather(images, cotangent, timg, tcot, kshard, narrow)
        parts = compute(x, cot, xt, ct, ktp, wl, sg)
        outs = plain_reduce(*parts, chans)
    block_out, op, red, red_gn, lengths, influence = outs
    return finish(
        held * n_wide,
        example_count,
        aug_count,
        step_count,
        block_out,
        op,
        cotangent,
        red,
        red_gn,
        (conv_weight, conv_moment1, conv_moment2, noise_conv),
        (gn_params, gn_moment1, gn_moment2, noise_gn),
        lengths.reshape(1, held),
        influence.reshape(1, held),
    )


def solution(mesh):
    in_specs = (
        P("wide", "narrow", None),
        P("wide", "narrow", None),
        P("wide", "narrow", None),
        P("wide", "narrow", None),
        P("wide", None),
        P("wide"),
        P("wide"),
        P(None, None, None, None, "narrow"),
        P(None, "narrow"),
        P(None, None, None, None, "narrow"),
        P(None, None, None, None, "narrow"),
        P(None, "narrow"),
        P(None, "narrow"),
        P(None, None, None, None, "narrow"),
        P(None, "narrow"),
        P(),
    )
    out_specs = (
        P("wide", "narrow", None),
        P("wide", "narrow", None),
        P("wide"),
        P("wide"),
        P(None, None, None, None, "narrow"),
        P(None, None, None, None, "narrow"),
        P(None, None, None, None, "narrow"),
        P(None, None, None, None, "narrow"),
        P(None, "narrow"),
        P(None, "narrow"),
        P(None, "narrow"),
    )
    return jax.shard_map(local, mesh=mesh, in_specs=in_specs, out_specs=out_specs, check_vma=False)
```

```python
import functools
import math

import jax
import jax.numpy as jnp
from jax import lax
from jax.experimental import pallas as pl
from jax.experimental.pallas import tpu as pltpu
from jax.sharding import PartitionSpec as P

C = 256
MAP = 8
GROUPS = 16
AUG = 16
PIX = MAP * MAP
FAN = 9 * C
LANES = 128
CLIP = 6.0 * C
MESH = pl.DeviceIdType.MESH
f32 = jnp.float32
bf16 = jnp.bfloat16
KCOLS = 2 * FAN


def lane_tile(index):
    return pl.ds(pl.multiple_of(index * LANES, LANES), LANES)


def group_sum(tile):
    return tile.reshape(GROUPS, C // GROUPS, LANES).sum(1)


def spread_group(rows):
    return jnp.broadcast_to(rows[:, None, :], (GROUPS, C // GROUPS, LANES)).reshape(C, LANES)


def image_sum(rows, ones):
    high = rows.astype(bf16)
    rest = rows - high.astype(f32)
    mid = rest.astype(bf16)
    low = (rest - mid.astype(f32)).astype(bf16)
    return product(jnp.concatenate([high, mid, low], axis=1), ones)


def sigmoid(z):
    return 0.5 * jnp.tanh(0.5 * z) + 0.5


def tap_masks():
    lane = lax.broadcasted_iota(jnp.int32, (1, LANES), 1)
    row = (lane // MAP) % MAP
    col = lane % MAP
    masks = []
    for r in (-1, 0, 1):
        for c in (-1, 0, 1):
            ok = (row + r >= 0) & (row + r < MAP) & (col + c >= 0) & (col + c < MAP)
            masks.append(jnp.where(ok, 1.0, 0.0).astype(f32).astype(bf16))
    return masks


def store_taps(value, col_ref, t, masks, flip):
    for tap in range(9):
        shift = (tap // 3 - 1) * MAP + (tap % 3 - 1)
        if shift == 0:
            moved = value
        else:
            moved = pltpu.roll(value, (-shift) % LANES, 1) * masks[tap]
        place = 8 - tap if flip else tap
        col_ref[place * C : (place + 1) * C, lane_tile(t)] = moved


def product(a, b):
    return jnp.dot(a, b, preferred_element_type=f32)


def product_nt(a, b):
    return lax.dot_general(a, b, (((1,), (1,)), ((), ())), preferred_element_type=f32)


class Work:
    pass


def norm_forward(wk, load, tiles, which, hat, rstd, hidden, col):
    stat = wk.stat

    @pl.loop(0, tiles, unroll=tiles)
    def _(t):
        stat[pl.ds(pl.multiple_of(t * GROUPS, GROUPS), GROUPS), :] = group_sum(load(t))

    rows = tiles * GROUPS
    stat[:rows, :] = image_sum(stat[:rows, :], wk.ones[...]) * (1.0 / (PIX * C // GROUPS))

    @pl.loop(0, tiles, unroll=tiles)
    def _(t):
        at = pl.ds(pl.multiple_of(t * GROUPS, GROUPS), GROUPS)
        centre = load(t) - spread_group(stat[at, :])
        hat[:, lane_tile(t)] = centre
        stat[at, :] = group_sum(centre * centre)

    spread = image_sum(stat[:rows, :], wk.ones[...]) * (1.0 / (PIX * C // GROUPS))
    rstd[:rows, :] = lax.rsqrt(spread + 1e-05)

    @pl.loop(0, tiles, unroll=tiles)
    def _(t):
        at = pl.ds(pl.multiple_of(t * GROUPS, GROUPS), GROUPS)
        normed = hat[:, lane_tile(t)] * spread_group(rstd[at, :])
        hat[:, lane_tile(t)] = normed
        scaled = normed * wk.gn[2 * which] + wk.gn[2 * which + 1]
        act = (scaled * sigmoid(scaled)).astype(bf16)
        hidden[:, lane_tile(t)] = act
        if col is not None:
            store_taps(act, col, t, wk.masks, False)


def norm_backward(wk, grad, tiles, which, hat, rstd, emit, acc):
    stat, stat2 = wk.stat, wk.stat2
    acc[0] = jnp.zeros((C, LANES), f32)
    acc[1] = jnp.zeros((C, LANES), f32)

    @pl.loop(0, tiles, unroll=tiles)
    def _(t):
        at = pl.ds(pl.multiple_of(t * GROUPS, GROUPS), GROUPS)
        normed = hat[:, lane_tile(t)]
        scaled = normed * wk.gn[2 * which] + wk.gn[2 * which + 1]
        gate = sigmoid(scaled)
        inner = grad[:, lane_tile(t)] * gate * (1.0 + scaled * (1.0 - gate))
        acc[0] += inner * normed
        acc[1] += inner
        inner = inner * wk.gn[2 * which]
        grad[:, lane_tile(t)] = inner
        stat[at, :] = group_sum(inner)
        stat2[at, :] = group_sum(inner * normed)

    if emit is not None:
        rows = tiles * GROUPS
        scale = 1.0 / (PIX * C // GROUPS)
        stat[:rows, :] = image_sum(stat[:rows, :], wk.ones[...]) * scale
        stat2[:rows, :] = image_sum(stat2[:rows, :], wk.ones[...]) * scale

        @pl.loop(0, tiles, unroll=tiles)
        def _(t):
            at = pl.ds(pl.multiple_of(t * GROUPS, GROUPS), GROUPS)
            value = grad[:, lane_tile(t)] - spread_group(stat[at, :])
            value = value - hat[:, lane_tile(t)] * spread_group(stat2[at, :])
            emit(t, value * spread_group(rstd[at, :]))


def matmul_cols(out, left, right, width):
    step = min(width, 256)
    for j in range(0, width, step):
        out[:, j : j + step] = product(left, right[:, j : j + step])


def fill_work(wk):
    half_a = (lax.broadcasted_iota(jnp.int32, (3 * LANES, LANES), 0) // PIX) % 2
    half_b = lax.broadcasted_iota(jnp.int32, (3 * LANES, LANES), 1) // PIX
    wk.ones[...] = jnp.where(half_a == half_b, 1.0, 0.0).astype(f32).astype(bf16)
    wk.masks = tap_masks()


def unpack_params(wk, tail):
    tail = tail.astype(f32)
    for k in range(6):
        value = tail[:, k : k + 1] + tail[:, 8 + k : 9 + k] + tail[:, 16 + k : 17 + k]
        value = jnp.broadcast_to(value, (C, LANES))
        if k < 4:
            wk.gn[k] = value
        else:
            wk.rs[k - 4] = value


def turn_kernel(wk, conv):
    for tap in range(9):
        wk.kb[conv, :, tap * C : (tap + 1) * C] = wk.kf[conv, :, tap * C : (tap + 1) * C].T


def cols(ref, width):
    return ref if width == ref.shape[1] else ref.at[:, :width]


def forward(wk, x_load, tiles, block_store, early=None):
    width = tiles * LANES
    norm_forward(wk, x_load, tiles, 0, wk.hat1, wk.rstd1, wk.hid1, wk.col)
    if early is not None:
        early()
    matmul_cols(wk.mid, wk.kf[0], cols(wk.col, width), width)
    norm_forward(
        wk,
        lambda t: wk.mid[:, lane_tile(t)],
        tiles,
        1,
        wk.hat2,
        wk.rstd2,
        wk.hid2,
        wk.col if block_store is not None else None,
    )
    if block_store is not None:
        matmul_cols(wk.mid, wk.kf[1], cols(wk.col, width), width)

        @pl.loop(0, tiles, unroll=tiles)
        def _(t):
            block_store(t, x_load(t) + wk.mid[:, lane_tile(t)])


def backward_two(wk, cot_load, weight_load, tiles, grads):
    width = tiles * LANES

    @pl.loop(0, tiles, unroll=tiles)
    def _(t):
        store_taps((cot_load(t) * weight_load(t)).astype(bf16), wk.col, t, wk.masks, True)

    matmul_cols(wk.mid, wk.kb[1], cols(wk.col, width), width)
    for tap in range(9):
        grads[9 + tap] = product_nt(wk.col[tap * C : (tap + 1) * C, :width], wk.hid2[:, :width])


def backward_one(wk, tiles, grads, gn_out, part_store):
    width = tiles * LANES

    def emit_middle(t, value):
        store_taps(value.astype(bf16), wk.col, t, wk.masks, True)

    norm_backward(wk, wk.mid, tiles, 1, wk.hat2, wk.rstd2, emit_middle, wk.acc.at[1])
    matmul_cols(wk.mid, wk.kb[0], cols(wk.col, width), width)
    for tap in range(9):
        grads[tap] = product_nt(wk.col[tap * C : (tap + 1) * C, :width], wk.hid1[:, :width])
    norm_backward(wk, wk.mid, tiles, 0, wk.hat1, wk.rstd1, part_store, wk.acc.at[0])

    lane = lax.broadcasted_iota(jnp.int32, (1, LANES), 1)
    total = jnp.zeros((C, LANES), f32)
    for k in range(4):
        one = jnp.sum(wk.acc[k // 2, k % 2], axis=1, keepdims=True)
        total = total + jnp.where(lane == k, one, 0.0)
    gn_out[...] = total


def raw_gradient(wk, grads, sq):
    rows = 32

    @pl.loop(0, C // rows)
    def _(j):
        at = pl.ds(pl.multiple_of(j * rows, rows), rows)
        for conv in range(2):
            first = jnp.zeros((rows, C), f32)
            second = jnp.zeros((rows, C), f32)
            for tap in range(9):
                g = grads[conv * 9 + tap, at, :]
                k = wk.kf[conv, at, tap * C : (tap + 1) * C].astype(f32)
                first = first + g
                second = second + g * k
            first = jnp.sum(first, axis=1, keepdims=True) * (1.0 / FAN)
            second = jnp.sum(second, axis=1, keepdims=True)
            rs = wk.rs[conv, at, 0:1]
            squares = jnp.zeros((rows, C), f32)
            for tap in range(9):
                g = grads[conv * 9 + tap, at, :]
                k = wk.kf[conv, at, tap * C : (tap + 1) * C].astype(f32)
                value = (g - first - k * second) * rs
                grads[conv * 9 + tap, at, :] = value
                squares = squares + value * value
            fold = squares[:, :LANES] + squares[:, LANES:]
            sq[...] += fold.reshape(rows // 8, 8, LANES).sum(0)


def whole_sum(tile):
    return jnp.sum(jnp.sum(tile, axis=1, keepdims=True), axis=0, keepdims=True)


WORK_SCRATCH = [
    pltpu.VMEM((2, C, FAN), bf16),
    pltpu.VMEM((2, C, FAN), bf16),
    pltpu.VMEM((FAN, AUG * PIX), bf16),
    pltpu.VMEM((C, AUG * PIX), f32),
    pltpu.VMEM((C, AUG * PIX), f32),
    pltpu.VMEM((C, AUG * PIX), f32),
    pltpu.VMEM((C, AUG * PIX), bf16),
    pltpu.VMEM((C, AUG * PIX), bf16),
    pltpu.VMEM((LANES, LANES), f32),
    pltpu.VMEM((LANES, LANES), f32),
    pltpu.VMEM((LANES, LANES), f32),
    pltpu.VMEM((LANES, LANES), f32),
    pltpu.VMEM((3 * LANES, LANES), bf16),
    pltpu.VMEM((4, C, LANES), f32),
    pltpu.VMEM((2, C, LANES), f32),
    pltpu.VMEM((2, 2, C, LANES), f32),
]
WORK_NAMES = (
    "kf",
    "kb",
    "col",
    "mid",
    "hat1",
    "hat2",
    "hid1",
    "hid2",
    "stat",
    "stat2",
    "rstd1",
    "rstd2",
    "ones",
    "gn",
    "rs",
    "acc",
)


def make_work(refs):
    wk = Work()
    for name, ref in zip(WORK_NAMES, refs):
        setattr(wk, name, ref)
    return wk


def compute_kernel(
    x, cot, xt, ct, ktp, wl, sg, block, part, clipped, test, clipped_gn, test_gn, raw, raw_gn, length, *scratch
):
    examples = x.shape[0]
    wk = make_work(scratch[:-2])
    tgrad, sq = scratch[-2:]
    fill_work(wk)
    unpack_params(wk, ktp[:, KCOLS : KCOLS + LANES])
    for conv in range(2):
        wk.kf[conv] = ktp[:, conv * FAN : (conv + 1) * FAN]
        turn_kernel(wk, conv)
    forward(wk, lambda t: xt[...].astype(f32), 1, None)
    backward_two(wk, lambda t: ct[...].astype(f32), lambda t: sg[...], 1, tgrad)
    backward_one(wk, 1, tgrad, test_gn, None)
    raw_gradient(wk, tgrad, sq)

    @pl.loop(0, 18)
    def _(k):
        test[k] = tgrad[k].astype(bf16)

    sq[...] = jnp.zeros_like(sq)

    @pl.loop(0, examples)
    def _(e):
        def block_store(t, value):
            block[e, :, lane_tile(t)] = value.astype(bf16)

        def part_store(t, value):
            part[e, :, lane_tile(t)] = value.astype(bf16)

        forward(wk, lambda t: x[e, :, lane_tile(t)].astype(f32), 8, block_store)
        backward_two(
            wk,
            lambda t: cot[e, :, lane_tile(t)].astype(f32),
            lambda t: wl[e, :, lane_tile(t)],
            8,
            raw.at[e],
        )
        backward_one(wk, 8, raw.at[e], raw_gn.at[e], part_store)
        sq[...] = jnp.zeros_like(sq)
        raw_gradient(wk, raw.at[e], sq)
        gn = raw_gn[e]
        square = whole_sum(sq[...]) + whole_sum(gn * gn)
        length[e] = jnp.broadcast_to(jnp.sqrt(square), (8, LANES))

    factors = [CLIP / jnp.maximum(length[e][0:1, 0:1], CLIP) for e in range(examples)]
    total = factors[0] * raw_gn[0]
    for e in range(1, examples):
        total = total + factors[e] * raw_gn[e]
    clipped_gn[...] = total

    @pl.loop(0, 18)
    def _(k):
        total = factors[0] * raw[0, k]
        for e in range(1, examples):
            total = total + factors[e] * raw[e, k]
        clipped[k] = total.astype(bf16)


def compute(x, cot, xt, ct, ktp, wl, sg):
    examples = x.shape[0]
    out = jax.ShapeDtypeStruct
    shapes = (
        out(x.shape, bf16),
        out(x.shape, bf16),
        out((18, C, C), bf16),
        out((18, C, C), bf16),
        out((C, LANES), f32),
        out((C, LANES), f32),
        out((examples, 18, C, C), f32),
        out((examples, C, LANES), f32),
        out((examples, 8, LANES), f32),
    )
    spec = pl.BlockSpec(memory_space=pltpu.VMEM)
    return pl.pallas_call(
        compute_kernel,
        out_shape=shapes,
        in_specs=[spec] * 7,
        out_specs=(spec,) * 9,
        scratch_shapes=WORK_SCRATCH + [pltpu.VMEM((18, C, C), f32), pltpu.VMEM((8, LANES), f32)],
        compiler_params=pltpu.CompilerParams(vmem_limit_bytes=58 << 20),
    )(x, cot, xt, ct, ktp, wl, sg)


def peer_copy(src, dst, send, recv, **where):
    return pltpu.make_async_remote_copy(
        src_ref=src, dst_ref=dst, send_sem=send, recv_sem=recv, device_id=where, device_id_type=MESH
    )


def greet(peers):
    barrier = pltpu.get_barrier_semaphore()
    for where in peers:
        pl.semaphore_signal(barrier, inc=1, device_id=where, device_id_type=MESH)
    pl.semaphore_wait(barrier, len(peers))


def near_of(z, c):
    return (z + 1 - 2 * (z % 2)) * 2 + c


def far_of(z, c):
    return lax.rem(z + 2, 4) * 2 + c


GRID = 2
A = 4
B = 8
D = 5
E = 6
F = 1
G = 8


class Exchange:
    def __init__(self, place, conv, gn, refs, sems):
        self.w, self.z, self.c, self.me = place
        self.conv, self.gn = conv, gn
        self.cb, self.cg, self.half, self.wb, self.quarter, self.nb, self.mid, self.fb = refs
        s_core, r_core, s_wide, r_wide, s_z, r_z = sems
        w, z, c = self.w, self.z, self.c
        sibling = self.me + 1 - 2 * c
        self.core = [
            peer_copy(conv.at[:, :, 1 - c], self.cb, s_core.at[0], r_core.at[0], narrow=sibling),
            peer_copy(gn.at[:, 1 - c], self.cg, s_core.at[1], r_core.at[1], narrow=sibling),
        ]
        self.wide = []
        for k in range(1, 4):
            to = lax.rem(w + k, 4)
            self.wide.append(
                peer_copy(self.half.at[to], self.wb.at[k - 1], s_wide.at[k - 1], r_wide.at[k - 1], wide=to)
            )
        self.p, self.h = z % 2, z // 2
        self.near = peer_copy(
            self.quarter.at[:, :, 1 - self.p], self.nb, s_z.at[0], r_z.at[0], narrow=near_of(z, c)
        )
        self.far = peer_copy(self.mid.at[:, 1 - self.h], self.fb, s_z.at[1], r_z.at[1], narrow=far_of(z, c))

    def clear(self):
        for q in range(1, 4):
            self.half[q, 9] = jnp.zeros_like(self.half[q, 9])

    def start_core(self):
        start_all(self.core)

    def start_wide(self):
        wait_all(self.core)
        half, c = self.half, self.c
        for k in range(2):

            @pl.loop(0, 9)
            def _(tap):
                total = self.conv[k * 9 + tap, :, c].astype(f32) + self.cb[k * 9 + tap].astype(f32)
                half[k * 2, tap] = total[:, :, :LANES].astype(bf16)
                half[k * 2 + 1, tap] = total[:, :, LANES:].astype(bf16)

        half[0, 9] = (self.gn[:, c].astype(f32) + self.cg[...].astype(f32)).astype(bf16)
        start_all(self.wide)

    def start_near(self):
        wait_all(self.wide)

        @pl.loop(0, 10)
        def _(tap):
            for zz in range(4):
                total = self.half[self.w, tap, zz].astype(f32)
                for k in range(3):
                    total = total + self.wb[k, tap, zz].astype(f32)
                self.quarter[tap, zz // 2, zz % 2] = total.astype(bf16)

        start_all([self.near])

    def start_far(self):
        wait_all([self.near])

        @pl.loop(0, 10)
        def _(tap):
            total = self.quarter[tap, :, self.p].astype(f32) + self.nb[tap].astype(f32)
            self.mid[tap] = total.astype(bf16)

        start_all([self.far])

    def finish(self, out):
        wait_all([self.far])

        @pl.loop(0, 10)
        def _(tap):
            out[tap] = (self.mid[tap, self.h].astype(f32) + self.fb[tap].astype(f32)).astype(bf16)


def start_all(copies):
    for copy in copies:
        copy.start()


def wait_all(copies):
    for copy in copies:
        copy.wait()


UNITS = 20


def own_kernels(weight, gain, shard, sent):
    chans = weight.shape[1]
    lane = lax.broadcasted_iota(jnp.int32, (chans, LANES), 1)
    eye = lax.broadcasted_iota(jnp.int32, (chans, chans), 0) == lax.broadcasted_iota(
        jnp.int32, (chans, chans), 1
    )
    values = [
        jnp.sum(jnp.where(eye, jnp.broadcast_to(gain[k : k + 1, :], (chans, chans)), 0.0), axis=1, keepdims=True)
        for k in range(4)
    ]
    means = []
    for conv in range(2):
        total = jnp.zeros((chans, C), f32)
        for tap in range(9):
            total = total + weight[conv * 9 + tap]
        mean = jnp.sum(total, axis=1, keepdims=True) * (1.0 / FAN)
        total = jnp.zeros((chans, C), f32)
        for tap in range(9):
            centre = weight[conv * 9 + tap] - mean
            total = total + centre * centre
        spread = jnp.sum(total, axis=1, keepdims=True) * (1.0 / FAN)
        means.append(mean)
        values.append(lax.rsqrt(FAN * spread + 1e-06))
    tail = jnp.zeros((chans, LANES), f32)
    for k, value in enumerate(values):
        high = value.astype(bf16).astype(f32)
        mid = (value - high).astype(bf16).astype(f32)
        low = value - high - mid
        tail = tail + jnp.where(lane == k, high, 0.0)
        tail = tail + jnp.where(lane == 8 + k, mid, 0.0)
        tail = tail + jnp.where(lane == 16 + k, low, 0.0)
    zero = jnp.zeros((chans, LANES), bf16)
    for conv in range(2):
        for tap in range(9):
            kernel = ((weight[conv * 9 + tap] - means[conv]) * values[4 + conv]).astype(bf16)
            shard[conv, 2 * tap] = kernel[:, :LANES]
            shard[conv, 2 * tap + 1] = kernel[:, LANES:]
        shard[conv, 18] = tail.astype(bf16) if conv == 0 else zero
        shard[conv, 19] = zero
        sent(conv)


def mega_kernel(
    images, cots, timg, tcot, weight, gain, pairs, alive, counts, ob, op, red_out, gn_out, norms, infl, *scratch
):
    n = 8
    me = lax.axis_index("narrow")
    w = lax.axis_index("wide")
    z, c = me // 2, me % 2
    sibling = me + 1 - 2 * c
    examples = images.shape[0] // n
    chans = images.shape[1]
    mine = pl.ds(pl.multiple_of(me * chans, chans), chans)
    work, rest = scratch[: len(WORK_SCRATCH)], scratch[len(WORK_SCRATCH) :]
    x, cot, xt, ct, shard, ktp, block, part, raw, raw_gn, length, tgrad, tgn, sq = rest[:14]
    s_conv, s_gn, t_conv, t_gn, dt, red, figures = rest[14:21]
    s_refs, t_refs = rest[21:29], rest[29:37]
    s_sems, t_sems = rest[37:43], rest[43:49]
    s_in, r_in, s_kz, r_kz, s_kw, r_kw, s_kc, r_kc, s_loc = rest[49:58]
    s_out, r_out, s_fin, r_fin, s_fig, r_fig = rest[58:64]
    greet(
        [{"narrow": lax.rem(me + k, n)} for k in range(1, n)]
        + [{"wide": lax.rem(w + k, 4)} for k in range(1, 4)]
    )

    def spread(a, src, dst, cut):
        copies = []
        for k in range(n):
            to = lax.rem(me + k, n)
            if k == 0:
                copies.append(pltpu.make_async_copy(cut(src, to), dst, s_loc.at[a]))
            else:
                copies.append(peer_copy(cut(src, to), dst, s_in.at[a, k - 1], r_in.at[a, k - 1], narrow=to))
        return copies

    def test_cut(src, to):
        return src.at[:, pl.ds(pl.multiple_of(to * LANES, LANES), LANES)]

    def example_cut(e):
        return lambda src, to: src.at[to * examples + e]

    def give_back(a, e, src, dst):
        copies = []
        for k in range(n):
            to = lax.rem(me + k, n)
            piece = src.at[e, pl.ds(pl.multiple_of(to * chans, chans), chans)]
            place = dst.at[me * examples + e]
            slot = a * examples + e
            if k == 0:
                copies.append(pltpu.make_async_copy(piece, place, s_loc.at[6 + slot]))
            else:
                copies.append(peer_copy(piece, place, s_out.at[slot, k - 1], r_out.at[slot, k - 1], narrow=to))
        return copies

    in_test = spread(0, timg, xt.at[mine], test_cut) + spread(1, tcot, ct.at[mine], test_cut)
    in_x = [spread(2 + 2 * e, images, x.at[e, mine], example_cut(e)) for e in range(examples)]
    in_cot = [spread(3 + 2 * e, cots, cot.at[e, mine], example_cut(e)) for e in range(examples)]
    out_block = [give_back(0, e, block, ob) for e in range(examples)]
    out_part = [give_back(1, e, part, op) for e in range(examples)]
    fifth = pl.ds(w * (UNITS // 4), UNITS // 4)
    h, p = z // 2, z % 2
    k_far, k_near, k_wide, k_core = [], [], [], []
    for conv in range(2):
        k_far.append(
            [
                peer_copy(
                    shard.at[conv, fifth],
                    ktp.at[conv, fifth, h, p, c],
                    s_kz.at[conv, 0],
                    r_kz.at[conv, 0],
                    narrow=far_of(z, c),
                )
            ]
        )
        held = ktp.at[conv, fifth, :, p, c]
        k_near.append([peer_copy(held, held, s_kz.at[conv, 1], r_kz.at[conv, 1], narrow=near_of(z, c))])
        held = ktp.at[conv, fifth, :, :, c]
        k_wide.append(
            [
                peer_copy(held, held, s_kw.at[conv, k - 1], r_kw.at[conv, k - 1], wide=lax.rem(w + k, 4))
                for k in range(1, 4)
            ]
        )
        held = ktp.at[conv, :, :, :, c]
        k_core.append([peer_copy(held, held, s_kc.at[conv], r_kc.at[conv], narrow=sibling)])

    own_kernels(weight, gain, shard, lambda conv: start_all(k_far[conv]))
    start_all(in_test)
    for conv in range(2):
        ktp[conv, fifth, h, p, c] = shard[conv, fifth]
    for conv in range(2):
        wait_all(k_far[conv])
        start_all(k_near[conv])
    for e in range(examples):
        start_all(in_x[e])
        start_all(in_cot[e])
    wk = make_work(work)
    fill_work(wk)
    place = (w, z, c, me)
    direction = Exchange(place, t_conv, t_gn, t_refs, t_sems)
    clipped = Exchange(place, s_conv, s_gn, s_refs, s_sems)
    direction.clear()
    clipped.clear()
    lane = lax.broadcasted_iota(jnp.int32, (1, LANES), 1)
    half = lane // PIX
    sign = jnp.zeros((1, LANES), f32)
    for p in range(pairs.shape[1]):
        sign = sign + jnp.where(lax.rem(pairs[0, p], AUG) == me * 2 + half, 1.0, 0.0)
        sign = sign - jnp.where(lax.rem(pairs[1, p], AUG) == me * 2 + half, 1.0, 0.0)

    def slot_weight(e):
        count = counts[me * examples + e]
        live = jnp.where(me * examples + e < alive[0], count, 0)
        each = 1.0 / jnp.full((1, LANES), count.astype(f32))
        return lambda t: jnp.where(t * 2 + half < live, each, 0.0)

    for conv in range(2):
        wait_all(k_near[conv])
        start_all(k_wide[conv])

    def kernel_arrived(conv):
        wait_all(k_wide[conv])
        start_all(k_core[conv])
        wait_all(k_core[conv])
        if conv == 0:
            unpack_params(wk, ktp[0, 18].reshape(C, LANES))
        for unit in range(18):
            wk.kf[conv, :, unit * LANES : (unit + 1) * LANES] = ktp[conv, unit].reshape(C, LANES)
        turn_kernel(wk, conv)

    kernel_arrived(0)
    wait_all(in_test)
    forward(wk, lambda t: xt[...].astype(f32), 1, None)
    kernel_arrived(1)
    backward_two(wk, lambda t: ct[...].astype(f32), lambda t: sign, 1, tgrad)
    backward_one(wk, 1, tgrad, tgn, None)
    raw_gradient(wk, tgrad, sq)

    @pl.loop(0, 18)
    def _(k):
        t_conv[k] = tgrad[k].astype(bf16).reshape(4, 2, chans, C)

    t_gn[...] = tgn[...].astype(bf16).reshape(4, 2, chans, LANES)
    direction.start_core()

    own = dt.at[c, w, z // 2, z % 2]
    both = dt.at[c, w, :, z % 2]
    far_ag = [peer_copy(own, own, s_fin.at[0, 0], r_fin.at[0, 0], narrow=far_of(z, c))]
    near_ag = [peer_copy(both, both, s_fin.at[0, 1], r_fin.at[0, 1], narrow=near_of(z, c))]
    wide_ag = []
    for k in range(1, 4):
        to = lax.rem(w + k, 4)
        wide_ag.append(
            peer_copy(dt.at[c, w], dt.at[c, w], s_fin.at[1, k - 1], r_fin.at[1, k - 1], wide=to)
        )
    core_ag = [peer_copy(dt.at[c], dt.at[c], s_fin.at[2, 0], r_fin.at[2, 0], narrow=sibling)]

    def early_forward(e):
        if e == 0:
            direction.start_wide()

    def between(e):
        if e == 1:
            direction.start_far()
            start_all(out_block[0][A:])

    def after_raw(e):
        if e == 0:
            direction.start_near()
            start_all(out_block[0][:A])
        else:
            direction.finish(own)
            start_all(far_ag)
            start_all(out_part[0][:D])

    for e in range(examples):
        wait_all(in_x[e])

        def block_store(t, value):
            block[e, :, lane_tile(t)] = value.astype(bf16)

        def part_store(t, value):
            part[e, :, lane_tile(t)] = value.astype(bf16)

        forward(
            wk,
            lambda t: x[e, :, lane_tile(t)].astype(f32),
            8,
            block_store,
            functools.partial(early_forward, e),
        )
        wait_all(in_cot[e])
        backward_two(wk, lambda t: cot[e, :, lane_tile(t)].astype(f32), slot_weight(e), 8, raw.at[e])
        between(e)
        backward_one(wk, 8, raw.at[e], raw_gn.at[e], part_store)
        sq[...] = jnp.zeros_like(sq)
        raw_gradient(wk, raw.at[e], sq)
        gn = raw_gn[e]
        square = whole_sum(sq[...]) + whole_sum(gn * gn)
        length[e] = jnp.broadcast_to(jnp.sqrt(square), (8, LANES))
        after_raw(e)

    factors = [CLIP / jnp.maximum(length[e][0:1, 0:1], CLIP) for e in range(examples)]
    total = factors[0] * raw_gn[0]
    for e in range(1, examples):
        total = total + factors[e] * raw_gn[e]
    s_gn[...] = total.astype(bf16).reshape(4, 2, chans, LANES)

    @pl.loop(0, 18)
    def _(k):
        total = factors[0] * raw[0, k]
        for e in range(1, examples):
            total = total + factors[e] * raw[e, k]
        s_conv[k] = total.astype(bf16).reshape(4, 2, chans, C)

    clipped.start_core()
    clipped.start_wide()
    wait_all(far_ag)
    start_all(near_ag)
    start_all(out_part[0][D:])
    start_all(out_block[1][:E])
    wait_all(near_ag)
    start_all(wide_ag)
    clipped.start_near()
    start_all(out_block[1][E:])
    start_all(out_part[1][:F])
    clipped.start_far()
    start_all(out_part[1][F:G])
    clipped.finish(red.at[w])
    finals = []
    for k in range(1, 4):
        to = lax.rem(w + k, 4)
        finals.append(peer_copy(red.at[w], red.at[w], s_fin.at[3, k - 1], r_fin.at[3, k - 1], wide=to))
    start_all(finals)
    wait_all(wide_ag)
    start_all(core_ag)
    wait_all(core_ag)
    inner_products(dt, raw, raw_gn, length, figures, me, chans)
    figs = []
    for k in range(1, n):
        to = lax.rem(me + k, n)
        figs.append(peer_copy(figures.at[me], figures.at[me], s_fig.at[k - 1], r_fig.at[k - 1], narrow=to))
    start_all(figs)
    start_all(out_part[1][G:])
    wait_all(figs)
    slot = lax.broadcasted_iota(jnp.int32, (8, LANES), 1)
    table = jnp.zeros((8, LANES), f32)
    for k in range(n):
        for e in range(examples):
            table = table + jnp.where(slot == k * examples + e, figures[k, e], 0.0)
    norms[...] = table[0:1, : n * examples]
    infl[...] = table[1:2, : n * examples]
    for e in range(examples):
        wait_all(out_block[e])
        wait_all(out_part[e])
    wait_all(finals)
    gn_out[...] = red[0, 9]
    for conv in range(2):
        for tap in range(9):
            red_out[conv * 9 + tap, :, :LANES] = red[conv * 2, tap]
            red_out[conv * 9 + tap, :, LANES:] = red[conv * 2 + 1, tap]


def inner_products(dt, raw, raw_gn, length, figures, me, chans):
    examples = raw.shape[0]
    zero = jnp.zeros((chans, LANES), f32)

    def visit(index, carry):
        q, rest = index // 8, index % 8
        at = pl.ds(pl.multiple_of(rest * chans, chans), chans)
        lanes = pl.ds(pl.multiple_of((q % 2) * LANES, LANES), LANES)
        square = carry[0]
        sums = list(carry[1:])
        for tap in range(9):
            d = dt[rest % 2, q, rest // 4, (rest // 2) % 2, tap].astype(f32)
            square = square + d * d
            for e in range(examples):
                sums[e] = sums[e] + d * raw[e, (q // 2) * 9 + tap, at, lanes]
        return (square, *sums)

    totals = lax.fori_loop(0, 32, visit, (zero,) * (examples + 1), unroll=4)

    def visit_gn(rest, carry):
        at = pl.ds(pl.multiple_of(rest * chans, chans), chans)
        d = dt[rest % 2, 0, rest // 4, (rest // 2) % 2, 9].astype(f32)
        return (carry[0] + d * d,) + tuple(carry[1 + e] + d * raw_gn[e, at, :] for e in range(examples))

    totals = lax.fori_loop(0, 8, visit_gn, totals)
    dir_sq = whole_sum(totals[0])
    params = 18 * C * C + 4 * C
    top = lax.broadcasted_iota(jnp.int32, (8, LANES), 0)
    for e in range(examples):
        size = length[e]
        factor = CLIP / jnp.maximum(size, CLIP)
        influence = factor * whole_sum(totals[1 + e]) * math.sqrt(params) / (CLIP * jnp.sqrt(dir_sq + 1e-06))
        figures[me, e] = jnp.where(top == 0, size, influence)


def mega(images, cots, timg, tcot, weight, gain, pairs, alive, counts):
    held, chans = images.shape[0], images.shape[1]
    examples = held // 8
    out = jax.ShapeDtypeStruct
    anyspace = pl.BlockSpec(memory_space=pl.ANY)
    vmem = pl.BlockSpec(memory_space=pltpu.VMEM)
    smem = pl.BlockSpec(memory_space=pltpu.SMEM)
    dma = pltpu.SemaphoreType.DMA
    exchange = [
        pltpu.VMEM((18, 4, chans, C), bf16),
        pltpu.VMEM((4, chans, LANES), bf16),
        pltpu.VMEM((4, 10, 4, chans, LANES), bf16),
        pltpu.VMEM((3, 10, 4, chans, LANES), bf16),
        pltpu.VMEM((10, 2, 2, chans, LANES), bf16),
        pltpu.VMEM((10, 2, chans, LANES), bf16),
        pltpu.VMEM((10, 2, chans, LANES), bf16),
        pltpu.VMEM((10, chans, LANES), bf16),
    ]
    sems = [dma((2,)), dma((2,)), dma((3,)), dma((3,)), dma((2,)), dma((2,))]
    scratch = [
        pltpu.VMEM((examples, C, AUG * PIX), bf16),
        pltpu.VMEM((examples, C, AUG * PIX), bf16),
        pltpu.VMEM((C, LANES), bf16),
        pltpu.VMEM((C, LANES), bf16),
        pltpu.VMEM((2, UNITS, chans, LANES), bf16),
        pltpu.VMEM((2, UNITS, 2, 2, 2, chans, LANES), bf16),
        pltpu.VMEM((examples, C, AUG * PIX), bf16),
        pltpu.VMEM((examples, C, AUG * PIX), bf16),
        pltpu.VMEM((examples, 18, C, C), f32),
        pltpu.VMEM((examples, C, LANES), f32),
        pltpu.VMEM((examples, 8, LANES), f32),
        pltpu.VMEM((18, C, C), f32),
        pltpu.VMEM((C, LANES), f32),
        pltpu.VMEM((8, LANES), f32),
        pltpu.VMEM((18, 4, 2, chans, C), bf16),
        pltpu.VMEM((4, 2, chans, LANES), bf16),
        pltpu.VMEM((18, 4, 2, chans, C), bf16),
        pltpu.VMEM((4, 2, chans, LANES), bf16),
        pltpu.VMEM((2, 4, 2, 2, 10, chans, LANES), bf16),
        pltpu.VMEM((4, 10, chans, LANES), bf16),
        pltpu.VMEM((8, examples, 8, LANES), f32),
    ]
    kinds = 2 + 2 * examples
    moves = [
        dma((kinds, 7)),
        dma((kinds, 7)),
        dma((2, 3)),
        dma((2, 3)),
        dma((2, 3)),
        dma((2, 3)),
        dma((2,)),
        dma((2,)),
        dma((11,)),
        dma((2 * examples, 7)),
        dma((2 * examples, 7)),
        dma((4, 3)),
        dma((4, 3)),
        dma((7,)),
        dma((7,)),
    ]
    return pl.pallas_call(
        mega_kernel,
        out_shape=(
            out((held, chans, AUG * PIX), bf16),
            out((held, chans, AUG * PIX), bf16),
            out((18, chans, C), bf16),
            out((chans, LANES), bf16),
            out((1, held), f32),
            out((1, held), f32),
        ),
        in_specs=[anyspace] * 4 + [vmem] * 2 + [smem] * 3,
        out_specs=(anyspace, anyspace) + (vmem,) * 4,
        scratch_shapes=WORK_SCRATCH + scratch + exchange + exchange + sems + sems + moves,
        compiler_params=pltpu.CompilerParams(collective_id=0, has_side_effects=True, vmem_limit_bytes=60 << 20),
    )(images, cots, timg, tcot, weight, gain, pairs, alive, counts)


def update(weight, first, second, grad, correction, rate, decay):
    first_new = 0.5 * first + 0.5 * grad
    second_new = 0.5 * second + 0.5 * grad * grad
    step = first_new / correction / (jnp.sqrt(second_new / correction) + 1e-08)
    return weight - rate * (step + decay * weight), first_new, second_new


def tail_kernel(
    total, alive, counts, steps, ob, op, cots, red, red_gn, weight, m1, m2, noise, gw, g1, g2, gnoise, norms, infl,
    block_out, grad_out, new, low, first, second, gnew, gfirst, gsecond, norms_out, infl_out
):
    step = pl.program_id(0)
    held = ob.shape[0]
    block_out[...] = ob[...]
    image = lax.broadcasted_iota(jnp.int32, (1, AUG * PIX), 1) // PIX
    for j in range(held):
        e = step * held + j
        count = counts[e]
        live = jnp.where(e < alive[0], count, 0)
        each = 1.0 / jnp.full((1, AUG * PIX), count.astype(f32))
        row = jnp.where(image < live, each, 0.0)
        grad_out[j] = cots[j].astype(f32) * row + op[j].astype(f32)
    correction = 1.0 - jnp.exp2(jnp.full((1, 1), -steps[0].astype(f32)))
    grad = (red[...].astype(f32) + math.sqrt(total) * noise[...]) * (1.0 / total)
    value, one, two = update(weight[...], m1[...], m2[...], grad, correction, 1.0 / math.sqrt(FAN), 0.1)
    new[...] = value
    low[...] = value.astype(bf16)
    first[...] = one
    second[...] = two

    @pl.when(step == 0)
    def _():
        chans = red_gn.shape[0]
        eye = lax.broadcasted_iota(jnp.int32, (chans, chans), 0) == lax.broadcasted_iota(
            jnp.int32, (chans, chans), 1
        )
        for k in range(4):
            column = red_gn[:, k : k + 1].astype(f32)
            row = jnp.sum(jnp.where(eye, jnp.broadcast_to(column, (chans, chans)), 0.0), axis=0, keepdims=True)
            at = slice(k, k + 1)
            grad = (row + math.sqrt(total) * gnoise[at, :]) * (1.0 / total)
            value, one, two = update(gw[at, :], g1[at, :], g2[at, :], grad, correction, 0.1, 0.0)
            gnew[at, :] = value
            gfirst[at, :] = one
            gsecond[at, :] = two
        norms_out[...] = norms[...]
        infl_out[...] = infl[...]


def finish(total, alive, counts, steps, ob, op, cots, red, red_gn, conv, gn, norms, infl):
    held, chans = ob.shape[0], ob.shape[1]
    grid = GRID
    rows = 18 * chans
    smem = pl.BlockSpec(memory_space=pltpu.SMEM)
    images = pl.BlockSpec((held // grid, chans, AUG * PIX), lambda i: (i, 0, 0))
    part = pl.BlockSpec((rows // grid, C), lambda i: (i, 0))

    def whole(v):
        return pl.BlockSpec(v.shape, lambda i: (0,) * len(v.shape))

    def out(v, kind=None):
        return jax.ShapeDtypeStruct(v.shape, kind or v.dtype)

    flat = [v.transpose(0, 1, 2, 4, 3).reshape(rows, C) for v in conv]
    outs = pl.pallas_call(
        functools.partial(tail_kernel, total),
        grid=(grid,),
        out_shape=[out(ob), out(ob, f32)]
        + [out(flat[0]), out(flat[0], bf16), out(flat[0]), out(flat[0])]
        + [out(gn[0])] * 3
        + [out(norms), out(infl)],
        in_specs=[smem] * 3
        + [images] * 3
        + [part, whole(red_gn)]
        + [part] * 4
        + [whole(gn[0])] * 4
        + [whole(norms), whole(infl)],
        out_specs=[images] * 2 + [part] * 4 + [whole(gn[0])] * 3 + [whole(norms), whole(infl)],
        compiler_params=pltpu.CompilerParams(vmem_limit_bytes=62 << 20),
    )(alive, counts, steps, ob, op, cots, red.reshape(rows, C), red_gn, *flat, *gn, norms, infl)

    def back(v):
        return v.reshape(2, 3, 3, chans, C).transpose(0, 1, 2, 4, 3)

    block_out, grad_out, new, low, first, second, gnew, gfirst, gsecond, norms, infl = outs
    return (
        block_out,
        grad_out,
        norms.reshape(held),
        infl.reshape(held),
        back(new),
        back(low),
        back(first),
        back(second),
        gnew,
        gfirst,
        gsecond,
    )


def pieces(v):
    high = lax.reduce_precision(v, 8, 7)
    rest = v - high
    mid = lax.reduce_precision(rest, 8, 7)
    low = rest - mid
    return high.astype(bf16), mid.astype(bf16), low.astype(bf16)


def kernel_rows(conv_weight, gn_params):
    chans = conv_weight.shape[4]
    centre = conv_weight - jnp.mean(conv_weight, axis=(1, 2, 3), keepdims=True)
    spread = jnp.mean(centre * centre, axis=(1, 2, 3), keepdims=True)
    scale = lax.rsqrt(FAN * spread + 1e-06)
    kernels = (centre * scale).astype(bf16).reshape(2, FAN, chans)
    rows = kernels.transpose(2, 0, 1).reshape(chans, KCOLS)
    small = jnp.concatenate([gn_params.T, scale.reshape(2, chans).T, jnp.zeros((chans, 2), f32)], 1)
    tail = jnp.concatenate(list(pieces(small)) + [jnp.zeros((chans, LANES - 24), bf16)], 1)
    return jnp.concatenate([rows, tail], 1)


def plain_gather(images, cots, timg, tcot, kshard, narrow):
    share = narrow // 8
    x = lax.all_to_all(images, "narrow", 0, 1, tiled=True)
    cot = lax.all_to_all(cots, "narrow", 0, 1, tiled=True)
    ktp = lax.all_gather(kshard, "narrow", axis=0, tiled=True)
    own = (lax.axis_index("narrow") // share) * LANES

    def pick(v):
        return lax.dynamic_slice_in_dim(lax.all_gather(v, "narrow", axis=0, tiled=True), own, LANES, 1)

    return x, cot, pick(timg), pick(tcot), ktp


def plain_reduce(block, part, clip_conv, test_conv, clip_gn, test_gn, raw, raw_gn, length, chans):
    examples = block.shape[0]
    ob = lax.all_to_all(block, "narrow", 1, 0, tiled=True)
    op = lax.all_to_all(part, "narrow", 1, 0, tiled=True)
    own = lax.axis_index("narrow") * chans
    rows = lax.psum(clip_conv, ("wide", "narrow"))
    rows = lax.dynamic_slice_in_dim(rows, own, chans, 1)
    gn_rows = lax.dynamic_slice_in_dim(lax.psum(clip_gn.astype(bf16), ("wide", "narrow")), own, chans, 0)
    d = lax.psum(test_conv, ("wide", "narrow")).astype(f32)
    d_gn = lax.psum(test_gn.astype(bf16), ("wide", "narrow")).astype(f32)
    dir_sq = jnp.sum(d * d) + jnp.sum(d_gn * d_gn)
    inner = jnp.sum(raw * d, axis=(1, 2, 3)) + jnp.sum(raw_gn * d_gn, axis=(1, 2))
    size = length[:, 0, 0]
    factor = CLIP / jnp.maximum(size, CLIP)
    influence = factor * inner * math.sqrt(18 * C * C + 4 * C) / (CLIP * jnp.sqrt(dir_sq + 1e-06))
    figures = lax.all_gather(jnp.stack([size, influence], 1), "narrow", axis=0)
    return ob, op, rows, gn_rows, figures[:, :, 0], figures[:, :, 1]


def local(
    images,
    cotangent,
    test_images,
    test_cotangent,
    pair_index,
    example_count,
    aug_count,
    conv_weight,
    gn_params,
    conv_moment1,
    conv_moment2,
    gn_moment1,
    gn_moment2,
    noise_conv,
    noise_gn,
    step_count,
):
    n_wide, narrow = lax.axis_size("wide"), lax.axis_size("narrow")
    held, chans = images.shape[0], images.shape[1]
    examples = held // narrow
    share = narrow // 8
    me = lax.axis_index("narrow")
    timg, tcot = test_images[0], test_cotangent[0]
    if n_wide == 4 and narrow == 8:
        weight = conv_weight.transpose(0, 1, 2, 4, 3).reshape(18, chans, C)
        outs = mega(
            images, cotangent, timg, tcot, weight, gn_params, pair_index.T, example_count, aug_count
        )
    else:
        slots = jnp.arange(AUG, dtype=jnp.int32)
        live = jnp.arange(held, dtype=jnp.int32) < example_count[0]
        weights = jnp.where(
            live[:, None] & (slots[None, :] < aug_count[:, None]),
            1.0 / aug_count.astype(f32)[:, None],
            f32(0.0),
        )
        pixels = jnp.repeat(weights, PIX, axis=1)
        pairs = pair_index % AUG
        signs = jnp.sum((pairs[:, 0:1] == slots[None, :]).astype(f32), 0) - jnp.sum(
            (pairs[:, 1:2] == slots[None, :]).astype(f32), 0
        )
        sign_pixels = jnp.repeat(signs, PIX).reshape(8, LANES) * (1.0 / share)
        kshard = kernel_rows(conv_weight, gn_params)
        wl = lax.dynamic_slice_in_dim(pixels, me * examples, examples, 0)[:, None, :]
        sg = lax.dynamic_slice_in_dim(sign_pixels, me // share, 1, 0)
        x, cot, xt, ct, ktp = plain_gather(images, cotangent, timg, tcot, kshard, narrow)
        parts = compute(x, cot, xt, ct, ktp, wl, sg)
        outs = plain_reduce(*parts, chans)
    block_out, op, red, red_gn, lengths, influence = outs
    return finish(
        held * n_wide,
        example_count,
        aug_count,
        step_count,
        block_out,
        op,
        cotangent,
        red,
        red_gn,
        (conv_weight, conv_moment1, conv_moment2, noise_conv),
        (gn_params, gn_moment1, gn_moment2, noise_gn),
        lengths.reshape(1, held),
        influence.reshape(1, held),
    )


def solution(mesh):
    in_specs = (
        P("wide", "narrow", None),
        P("wide", "narrow", None),
        P("wide", "narrow", None),
        P("wide", "narrow", None),
        P("wide", None),
        P("wide"),
        P("wide"),
        P(None, None, None, None, "narrow"),
        P(None, "narrow"),
        P(None, None, None, None, "narrow"),
        P(None, None, None, None, "narrow"),
        P(None, "narrow"),
        P(None, "narrow"),
        P(None, None, None, None, "narrow"),
        P(None, "narrow"),
        P(),
    )
    out_specs = (
        P("wide", "narrow", None),
        P("wide", "narrow", None),
        P("wide"),
        P("wide"),
        P(None, None, None, None, "narrow"),
        P(None, None, None, None, "narrow"),
        P(None, None, None, None, "narrow"),
        P(None, None, None, None, "narrow"),
        P(None, "narrow"),
        P(None, "narrow"),
        P(None, "narrow"),
    )
    return jax.shard_map(local, mesh=mesh, in_specs=in_specs, out_specs=out_specs, check_vma=False)
```

```python
import functools
import math

import jax
import jax.numpy as jnp
from jax import lax
from jax.experimental import pallas as pl
from jax.experimental.pallas import tpu as pltpu
from jax.sharding import PartitionSpec as P

C = 256
MAP = 8
GROUPS = 16
AUG = 16
PIX = MAP * MAP
FAN = 9 * C
LANES = 128
CLIP = 6.0 * C
MESH = pl.DeviceIdType.MESH
f32 = jnp.float32
bf16 = jnp.bfloat16
KCOLS = 2 * FAN


def lane_tile(index):
    return pl.ds(pl.multiple_of(index * LANES, LANES), LANES)


def group_sum(tile):
    return tile.reshape(GROUPS, C // GROUPS, LANES).sum(1)


def spread_group(rows):
    return jnp.broadcast_to(rows[:, None, :], (GROUPS, C // GROUPS, LANES)).reshape(C, LANES)


def image_sum(rows, ones):
    high = rows.astype(bf16)
    rest = rows - high.astype(f32)
    mid = rest.astype(bf16)
    low = (rest - mid.astype(f32)).astype(bf16)
    return product(jnp.concatenate([high, mid, low], axis=1), ones)


def sigmoid(z):
    return 0.5 * jnp.tanh(0.5 * z) + 0.5


def tap_masks():
    lane = lax.broadcasted_iota(jnp.int32, (1, LANES), 1)
    row = (lane // MAP) % MAP
    col = lane % MAP
    masks = []
    for r in (-1, 0, 1):
        for c in (-1, 0, 1):
            ok = (row + r >= 0) & (row + r < MAP) & (col + c >= 0) & (col + c < MAP)
            masks.append(jnp.where(ok, 1.0, 0.0).astype(f32).astype(bf16))
    return masks


def store_taps(value, col_ref, t, masks, flip):
    for tap in range(9):
        shift = (tap // 3 - 1) * MAP + (tap % 3 - 1)
        if shift == 0:
            moved = value
        else:
            moved = pltpu.roll(value, (-shift) % LANES, 1) * masks[tap]
        place = 8 - tap if flip else tap
        col_ref[place * C : (place + 1) * C, lane_tile(t)] = moved


def product(a, b):
    return jnp.dot(a, b, preferred_element_type=f32)


def product_nt(a, b):
    return lax.dot_general(a, b, (((1,), (1,)), ((), ())), preferred_element_type=f32)


class Work:
    pass


def norm_forward(wk, load, tiles, which, hat, rstd, hidden, col):
    stat = wk.stat

    @pl.loop(0, tiles, unroll=tiles)
    def _(t):
        stat[pl.ds(pl.multiple_of(t * GROUPS, GROUPS), GROUPS), :] = group_sum(load(t))

    rows = tiles * GROUPS
    stat[:rows, :] = image_sum(stat[:rows, :], wk.ones[...]) * (1.0 / (PIX * C // GROUPS))

    @pl.loop(0, tiles, unroll=tiles)
    def _(t):
        at = pl.ds(pl.multiple_of(t * GROUPS, GROUPS), GROUPS)
        centre = load(t) - spread_group(stat[at, :])
        hat[:, lane_tile(t)] = centre
        stat[at, :] = group_sum(centre * centre)

    spread = image_sum(stat[:rows, :], wk.ones[...]) * (1.0 / (PIX * C // GROUPS))
    rstd[:rows, :] = lax.rsqrt(spread + 1e-05)

    @pl.loop(0, tiles, unroll=tiles)
    def _(t):
        at = pl.ds(pl.multiple_of(t * GROUPS, GROUPS), GROUPS)
        normed = hat[:, lane_tile(t)] * spread_group(rstd[at, :])
        hat[:, lane_tile(t)] = normed
        scaled = normed * wk.gn[2 * which] + wk.gn[2 * which + 1]
        act = (scaled * sigmoid(scaled)).astype(bf16)
        hidden[:, lane_tile(t)] = act
        if col is not None:
            store_taps(act, col, t, wk.masks, False)


def norm_backward(wk, grad, tiles, which, hat, rstd, emit, acc):
    stat, stat2 = wk.stat, wk.stat2
    acc[0] = jnp.zeros((C, LANES), f32)
    acc[1] = jnp.zeros((C, LANES), f32)

    @pl.loop(0, tiles, unroll=tiles)
    def _(t):
        at = pl.ds(pl.multiple_of(t * GROUPS, GROUPS), GROUPS)
        normed = hat[:, lane_tile(t)]
        scaled = normed * wk.gn[2 * which] + wk.gn[2 * which + 1]
        gate = sigmoid(scaled)
        inner = grad[:, lane_tile(t)] * gate * (1.0 + scaled * (1.0 - gate))
        acc[0] += inner * normed
        acc[1] += inner
        inner = inner * wk.gn[2 * which]
        grad[:, lane_tile(t)] = inner
        stat[at, :] = group_sum(inner)
        stat2[at, :] = group_sum(inner * normed)

    if emit is not None:
        rows = tiles * GROUPS
        scale = 1.0 / (PIX * C // GROUPS)
        stat[:rows, :] = image_sum(stat[:rows, :], wk.ones[...]) * scale
        stat2[:rows, :] = image_sum(stat2[:rows, :], wk.ones[...]) * scale

        @pl.loop(0, tiles, unroll=tiles)
        def _(t):
            at = pl.ds(pl.multiple_of(t * GROUPS, GROUPS), GROUPS)
            value = grad[:, lane_tile(t)] - spread_group(stat[at, :])
            value = value - hat[:, lane_tile(t)] * spread_group(stat2[at, :])
            emit(t, value * spread_group(rstd[at, :]))


def matmul_cols(out, left, right, width):
    step = min(width, 256)
    for j in range(0, width, step):
        out[:, j : j + step] = product(left, right[:, j : j + step])


def fill_work(wk):
    half_a = (lax.broadcasted_iota(jnp.int32, (3 * LANES, LANES), 0) // PIX) % 2
    half_b = lax.broadcasted_iota(jnp.int32, (3 * LANES, LANES), 1) // PIX
    wk.ones[...] = jnp.where(half_a == half_b, 1.0, 0.0).astype(f32).astype(bf16)
    wk.masks = tap_masks()


def unpack_params(wk, tail):
    tail = tail.astype(f32)
    for k in range(6):
        value = tail[:, k : k + 1] + tail[:, 8 + k : 9 + k] + tail[:, 16 + k : 17 + k]
        value = jnp.broadcast_to(value, (C, LANES))
        if k < 4:
            wk.gn[k] = value
        else:
            wk.rs[k - 4] = value


def turn_kernel(wk, conv):
    for tap in range(9):
        wk.kb[conv, :, tap * C : (tap + 1) * C] = wk.kf[conv, :, tap * C : (tap + 1) * C].T


def cols(ref, width):
    return ref if width == ref.shape[1] else ref.at[:, :width]


def forward(wk, x_load, tiles, block_store, early=None):
    width = tiles * LANES
    norm_forward(wk, x_load, tiles, 0, wk.hat1, wk.rstd1, wk.hid1, wk.col)
    if early is not None:
        early()
    matmul_cols(wk.mid, wk.kf[0], cols(wk.col, width), width)
    norm_forward(
        wk,
        lambda t: wk.mid[:, lane_tile(t)],
        tiles,
        1,
        wk.hat2,
        wk.rstd2,
        wk.hid2,
        wk.col if block_store is not None else None,
    )
    if block_store is not None:
        matmul_cols(wk.mid, wk.kf[1], cols(wk.col, width), width)

        @pl.loop(0, tiles, unroll=tiles)
        def _(t):
            block_store(t, x_load(t) + wk.mid[:, lane_tile(t)])


def backward_two(wk, cot_load, weight_load, tiles, grads):
    width = tiles * LANES

    @pl.loop(0, tiles, unroll=tiles)
    def _(t):
        store_taps((cot_load(t) * weight_load(t)).astype(bf16), wk.col, t, wk.masks, True)

    matmul_cols(wk.mid, wk.kb[1], cols(wk.col, width), width)
    for tap in range(9):
        grads[9 + tap] = product_nt(wk.col[tap * C : (tap + 1) * C, :width], wk.hid2[:, :width])


def backward_one(wk, tiles, grads, gn_out, part_store):
    width = tiles * LANES

    def emit_middle(t, value):
        store_taps(value.astype(bf16), wk.col, t, wk.masks, True)

    norm_backward(wk, wk.mid, tiles, 1, wk.hat2, wk.rstd2, emit_middle, wk.acc.at[1])
    matmul_cols(wk.mid, wk.kb[0], cols(wk.col, width), width)
    for tap in range(9):
        grads[tap] = product_nt(wk.col[tap * C : (tap + 1) * C, :width], wk.hid1[:, :width])
    norm_backward(wk, wk.mid, tiles, 0, wk.hat1, wk.rstd1, part_store, wk.acc.at[0])

    lane = lax.broadcasted_iota(jnp.int32, (1, LANES), 1)
    total = jnp.zeros((C, LANES), f32)
    for k in range(4):
        one = jnp.sum(wk.acc[k // 2, k % 2], axis=1, keepdims=True)
        total = total + jnp.where(lane == k, one, 0.0)
    gn_out[...] = total


def raw_gradient(wk, grads, sq):
    rows = 32

    @pl.loop(0, C // rows, unroll=2)
    def _(j):
        at = pl.ds(pl.multiple_of(j * rows, rows), rows)
        for conv in range(2):
            first = jnp.zeros((rows, C), f32)
            second = jnp.zeros((rows, C), f32)
            for tap in range(9):
                g = grads[conv * 9 + tap, at, :]
                k = wk.kf[conv, at, tap * C : (tap + 1) * C].astype(f32)
                first = first + g
                second = second + g * k
            first = jnp.sum(first, axis=1, keepdims=True) * (1.0 / FAN)
            second = jnp.sum(second, axis=1, keepdims=True)
            rs = wk.rs[conv, at, 0:1]
            squares = jnp.zeros((rows, C), f32)
            for tap in range(9):
                g = grads[conv * 9 + tap, at, :]
                k = wk.kf[conv, at, tap * C : (tap + 1) * C].astype(f32)
                value = (g - first - k * second) * rs
                grads[conv * 9 + tap, at, :] = value
                squares = squares + value * value
            fold = squares[:, :LANES] + squares[:, LANES:]
            sq[...] += fold.reshape(rows // 8, 8, LANES).sum(0)


def whole_sum(tile):
    return jnp.sum(jnp.sum(tile, axis=1, keepdims=True), axis=0, keepdims=True)


WORK_SCRATCH = [
    pltpu.VMEM((2, C, FAN), bf16),
    pltpu.VMEM((2, C, FAN), bf16),
    pltpu.VMEM((FAN, AUG * PIX), bf16),
    pltpu.VMEM((C, AUG * PIX), f32),
    pltpu.VMEM((C, AUG * PIX), f32),
    pltpu.VMEM((C, AUG * PIX), f32),
    pltpu.VMEM((C, AUG * PIX), bf16),
    pltpu.VMEM((C, AUG * PIX), bf16),
    pltpu.VMEM((LANES, LANES), f32),
    pltpu.VMEM((LANES, LANES), f32),
    pltpu.VMEM((LANES, LANES), f32),
    pltpu.VMEM((LANES, LANES), f32),
    pltpu.VMEM((3 * LANES, LANES), bf16),
    pltpu.VMEM((4, C, LANES), f32),
    pltpu.VMEM((2, C, LANES), f32),
    pltpu.VMEM((2, 2, C, LANES), f32),
]
WORK_NAMES = (
    "kf",
    "kb",
    "col",
    "mid",
    "hat1",
    "hat2",
    "hid1",
    "hid2",
    "stat",
    "stat2",
    "rstd1",
    "rstd2",
    "ones",
    "gn",
    "rs",
    "acc",
)


def make_work(refs):
    wk = Work()
    for name, ref in zip(WORK_NAMES, refs):
        setattr(wk, name, ref)
    return wk


def compute_kernel(
    x, cot, xt, ct, ktp, wl, sg, block, part, clipped, test, clipped_gn, test_gn, raw, raw_gn, length, *scratch
):
    examples = x.shape[0]
    wk = make_work(scratch[:-2])
    tgrad, sq = scratch[-2:]
    fill_work(wk)
    unpack_params(wk, ktp[:, KCOLS : KCOLS + LANES])
    for conv in range(2):
        wk.kf[conv] = ktp[:, conv * FAN : (conv + 1) * FAN]
        turn_kernel(wk, conv)
    forward(wk, lambda t: xt[...].astype(f32), 1, None)
    backward_two(wk, lambda t: ct[...].astype(f32), lambda t: sg[...], 1, tgrad)
    backward_one(wk, 1, tgrad, test_gn, None)
    raw_gradient(wk, tgrad, sq)

    @pl.loop(0, 18)
    def _(k):
        test[k] = tgrad[k].astype(bf16)

    sq[...] = jnp.zeros_like(sq)

    @pl.loop(0, examples)
    def _(e):
        def block_store(t, value):
            block[e, :, lane_tile(t)] = value.astype(bf16)

        def part_store(t, value):
            part[e, :, lane_tile(t)] = value.astype(bf16)

        forward(wk, lambda t: x[e, :, lane_tile(t)].astype(f32), 8, block_store)
        backward_two(
            wk,
            lambda t: cot[e, :, lane_tile(t)].astype(f32),
            lambda t: wl[e, :, lane_tile(t)],
            8,
            raw.at[e],
        )
        backward_one(wk, 8, raw.at[e], raw_gn.at[e], part_store)
        sq[...] = jnp.zeros_like(sq)
        raw_gradient(wk, raw.at[e], sq)
        gn = raw_gn[e]
        square = whole_sum(sq[...]) + whole_sum(gn * gn)
        length[e] = jnp.broadcast_to(jnp.sqrt(square), (8, LANES))

    factors = [CLIP / jnp.maximum(length[e][0:1, 0:1], CLIP) for e in range(examples)]
    total = factors[0] * raw_gn[0]
    for e in range(1, examples):
        total = total + factors[e] * raw_gn[e]
    clipped_gn[...] = total

    @pl.loop(0, 18)
    def _(k):
        total = factors[0] * raw[0, k]
        for e in range(1, examples):
            total = total + factors[e] * raw[e, k]
        clipped[k] = total.astype(bf16)


def compute(x, cot, xt, ct, ktp, wl, sg):
    examples = x.shape[0]
    out = jax.ShapeDtypeStruct
    shapes = (
        out(x.shape, bf16),
        out(x.shape, bf16),
        out((18, C, C), bf16),
        out((18, C, C), bf16),
        out((C, LANES), f32),
        out((C, LANES), f32),
        out((examples, 18, C, C), f32),
        out((examples, C, LANES), f32),
        out((examples, 8, LANES), f32),
    )
    spec = pl.BlockSpec(memory_space=pltpu.VMEM)
    return pl.pallas_call(
        compute_kernel,
        out_shape=shapes,
        in_specs=[spec] * 7,
        out_specs=(spec,) * 9,
        scratch_shapes=WORK_SCRATCH + [pltpu.VMEM((18, C, C), f32), pltpu.VMEM((8, LANES), f32)],
        compiler_params=pltpu.CompilerParams(vmem_limit_bytes=58 << 20),
    )(x, cot, xt, ct, ktp, wl, sg)


def peer_copy(src, dst, send, recv, **where):
    return pltpu.make_async_remote_copy(
        src_ref=src, dst_ref=dst, send_sem=send, recv_sem=recv, device_id=where, device_id_type=MESH
    )


def greet(peers):
    barrier = pltpu.get_barrier_semaphore()
    for where in peers:
        pl.semaphore_signal(barrier, inc=1, device_id=where, device_id_type=MESH)
    pl.semaphore_wait(barrier, len(peers))


def near_of(z, c):
    return (z + 1 - 2 * (z % 2)) * 2 + c


def far_of(z, c):
    return lax.rem(z + 2, 4) * 2 + c


GRID = 2
A = 4
B = 8
D = 5
E = 6
F = 1
G = 8


class Exchange:
    def __init__(self, place, conv, gn, refs, sems):
        self.w, self.z, self.c, self.me = place
        self.conv, self.gn = conv, gn
        self.cb, self.cg, self.half, self.wb, self.quarter, self.nb, self.mid, self.fb = refs
        s_core, r_core, s_wide, r_wide, s_z, r_z = sems
        w, z, c = self.w, self.z, self.c
        sibling = self.me + 1 - 2 * c
        self.core = [
            peer_copy(conv.at[:, :, 1 - c], self.cb, s_core.at[0], r_core.at[0], narrow=sibling),
            peer_copy(gn.at[:, 1 - c], self.cg, s_core.at[1], r_core.at[1], narrow=sibling),
        ]
        self.wide = []
        for k in range(1, 4):
            to = lax.rem(w + k, 4)
            self.wide.append(
                peer_copy(self.half.at[to], self.wb.at[k - 1], s_wide.at[k - 1], r_wide.at[k - 1], wide=to)
            )
        self.p, self.h = z % 2, z // 2
        self.near = peer_copy(
            self.quarter.at[:, :, 1 - self.p], self.nb, s_z.at[0], r_z.at[0], narrow=near_of(z, c)
        )
        self.far = peer_copy(self.mid.at[:, 1 - self.h], self.fb, s_z.at[1], r_z.at[1], narrow=far_of(z, c))

    def clear(self):
        for q in range(1, 4):
            self.half[q, 9] = jnp.zeros_like(self.half[q, 9])

    def start_core(self):
        start_all(self.core)

    def start_wide(self):
        wait_all(self.core)
        half, c = self.half, self.c
        for k in range(2):

            @pl.loop(0, 9)
            def _(tap):
                total = self.conv[k * 9 + tap, :, c].astype(f32) + self.cb[k * 9 + tap].astype(f32)
                half[k * 2, tap] = total[:, :, :LANES].astype(bf16)
                half[k * 2 + 1, tap] = total[:, :, LANES:].astype(bf16)

        half[0, 9] = (self.gn[:, c].astype(f32) + self.cg[...].astype(f32)).astype(bf16)
        start_all(self.wide)

    def start_near(self):
        wait_all(self.wide)

        @pl.loop(0, 10)
        def _(tap):
            for zz in range(4):
                total = self.half[self.w, tap, zz].astype(f32)
                for k in range(3):
                    total = total + self.wb[k, tap, zz].astype(f32)
                self.quarter[tap, zz // 2, zz % 2] = total.astype(bf16)

        start_all([self.near])

    def start_far(self):
        wait_all([self.near])

        @pl.loop(0, 10)
        def _(tap):
            total = self.quarter[tap, :, self.p].astype(f32) + self.nb[tap].astype(f32)
            self.mid[tap] = total.astype(bf16)

        start_all([self.far])

    def finish(self, out):
        wait_all([self.far])

        @pl.loop(0, 10)
        def _(tap):
            out[tap] = (self.mid[tap, self.h].astype(f32) + self.fb[tap].astype(f32)).astype(bf16)


def start_all(copies):
    for copy in copies:
        copy.start()


def wait_all(copies):
    for copy in copies:
        copy.wait()


UNITS = 20


def own_kernels(weight, gain, shard, sent):
    chans = weight.shape[1]
    lane = lax.broadcasted_iota(jnp.int32, (chans, LANES), 1)
    eye = lax.broadcasted_iota(jnp.int32, (chans, chans), 0) == lax.broadcasted_iota(
        jnp.int32, (chans, chans), 1
    )
    values = [
        jnp.sum(jnp.where(eye, jnp.broadcast_to(gain[k : k + 1, :], (chans, chans)), 0.0), axis=1, keepdims=True)
        for k in range(4)
    ]
    means = []
    for conv in range(2):
        total = jnp.zeros((chans, C), f32)
        for tap in range(9):
            total = total + weight[conv * 9 + tap]
        mean = jnp.sum(total, axis=1, keepdims=True) * (1.0 / FAN)
        total = jnp.zeros((chans, C), f32)
        for tap in range(9):
            centre = weight[conv * 9 + tap] - mean
            total = total + centre * centre
        spread = jnp.sum(total, axis=1, keepdims=True) * (1.0 / FAN)
        means.append(mean)
        values.append(lax.rsqrt(FAN * spread + 1e-06))
    tail = jnp.zeros((chans, LANES), f32)
    for k, value in enumerate(values):
        high = value.astype(bf16).astype(f32)
        mid = (value - high).astype(bf16).astype(f32)
        low = value - high - mid
        tail = tail + jnp.where(lane == k, high, 0.0)
        tail = tail + jnp.where(lane == 8 + k, mid, 0.0)
        tail = tail + jnp.where(lane == 16 + k, low, 0.0)
    zero = jnp.zeros((chans, LANES), bf16)
    for conv in range(2):
        for tap in range(9):
            kernel = ((weight[conv * 9 + tap] - means[conv]) * values[4 + conv]).astype(bf16)
            shard[conv, 2 * tap] = kernel[:, :LANES]
            shard[conv, 2 * tap + 1] = kernel[:, LANES:]
        shard[conv, 18] = tail.astype(bf16) if conv == 0 else zero
        shard[conv, 19] = zero
        sent(conv)


def mega_kernel(
    images, cots, timg, tcot, weight, gain, pairs, alive, counts, ob, op, red_out, gn_out, norms, infl, *scratch
):
    n = 8
    me = lax.axis_index("narrow")
    w = lax.axis_index("wide")
    z, c = me // 2, me % 2
    sibling = me + 1 - 2 * c
    examples = images.shape[0] // n
    chans = images.shape[1]
    mine = pl.ds(pl.multiple_of(me * chans, chans), chans)
    work, rest = scratch[: len(WORK_SCRATCH)], scratch[len(WORK_SCRATCH) :]
    x, cot, xt, ct, shard, ktp, block, part, raw, raw_gn, length, tgrad, tgn, sq = rest[:14]
    s_conv, s_gn, t_conv, t_gn, dt, red, figures = rest[14:21]
    s_refs, t_refs = rest[21:29], rest[29:37]
    s_sems, t_sems = rest[37:43], rest[43:49]
    s_in, r_in, s_kz, r_kz, s_kw, r_kw, s_kc, r_kc, s_loc = rest[49:58]
    s_out, r_out, s_fin, r_fin, s_fig, r_fig = rest[58:64]
    greet(
        [{"narrow": lax.rem(me + k, n)} for k in range(1, n)]
        + [{"wide": lax.rem(w + k, 4)} for k in range(1, 4)]
    )

    def spread(a, src, dst, cut):
        copies = []
        for k in range(n):
            to = lax.rem(me + k, n)
            if k == 0:
                copies.append(pltpu.make_async_copy(cut(src, to), dst, s_loc.at[a]))
            else:
                copies.append(peer_copy(cut(src, to), dst, s_in.at[a, k - 1], r_in.at[a, k - 1], narrow=to))
        return copies

    def test_cut(src, to):
        return src.at[:, pl.ds(pl.multiple_of(to * LANES, LANES), LANES)]

    def example_cut(e):
        return lambda src, to: src.at[to * examples + e]

    def give_back(a, e, src, dst):
        copies = []
        for k in range(n):
            to = lax.rem(me + k, n)
            piece = src.at[e, pl.ds(pl.multiple_of(to * chans, chans), chans)]
            place = dst.at[me * examples + e]
            slot = a * examples + e
            if k == 0:
                copies.append(pltpu.make_async_copy(piece, place, s_loc.at[6 + slot]))
            else:
                copies.append(peer_copy(piece, place, s_out.at[slot, k - 1], r_out.at[slot, k - 1], narrow=to))
        return copies

    in_test = spread(0, timg, xt.at[mine], test_cut) + spread(1, tcot, ct.at[mine], test_cut)
    in_x = [spread(2 + 2 * e, images, x.at[e, mine], example_cut(e)) for e in range(examples)]
    in_cot = [spread(3 + 2 * e, cots, cot.at[e, mine], example_cut(e)) for e in range(examples)]
    out_block = [give_back(0, e, block, ob) for e in range(examples)]
    out_part = [give_back(1, e, part, op) for e in range(examples)]
    fifth = pl.ds(w * (UNITS // 4), UNITS // 4)
    h, p = z // 2, z % 2
    k_far, k_near, k_wide, k_core = [], [], [], []
    for conv in range(2):
        k_far.append(
            [
                peer_copy(
                    shard.at[conv, fifth],
                    ktp.at[conv, fifth, h, p, c],
                    s_kz.at[conv, 0],
                    r_kz.at[conv, 0],
                    narrow=far_of(z, c),
                )
            ]
        )
        held = ktp.at[conv, fifth, :, p, c]
        k_near.append([peer_copy(held, held, s_kz.at[conv, 1], r_kz.at[conv, 1], narrow=near_of(z, c))])
        held = ktp.at[conv, fifth, :, :, c]
        k_wide.append(
            [
                peer_copy(held, held, s_kw.at[conv, k - 1], r_kw.at[conv, k - 1], wide=lax.rem(w + k, 4))
                for k in range(1, 4)
            ]
        )
        held = ktp.at[conv, :, :, :, c]
        k_core.append([peer_copy(held, held, s_kc.at[conv], r_kc.at[conv], narrow=sibling)])

    own_kernels(weight, gain, shard, lambda conv: start_all(k_far[conv]))
    start_all(in_test)
    for conv in range(2):
        ktp[conv, fifth, h, p, c] = shard[conv, fifth]
    for conv in range(2):
        wait_all(k_far[conv])
        start_all(k_near[conv])
    for e in range(examples):
        start_all(in_x[e])
        start_all(in_cot[e])
    wk = make_work(work)
    fill_work(wk)
    place = (w, z, c, me)
    direction = Exchange(place, t_conv, t_gn, t_refs, t_sems)
    clipped = Exchange(place, s_conv, s_gn, s_refs, s_sems)
    direction.clear()
    clipped.clear()
    lane = lax.broadcasted_iota(jnp.int32, (1, LANES), 1)
    half = lane // PIX
    sign = jnp.zeros((1, LANES), f32)
    for p in range(pairs.shape[1]):
        sign = sign + jnp.where(lax.rem(pairs[0, p], AUG) == me * 2 + half, 1.0, 0.0)
        sign = sign - jnp.where(lax.rem(pairs[1, p], AUG) == me * 2 + half, 1.0, 0.0)

    def slot_weight(e):
        count = counts[me * examples + e]
        live = jnp.where(me * examples + e < alive[0], count, 0)
        each = 1.0 / jnp.full((1, LANES), count.astype(f32))
        return lambda t: jnp.where(t * 2 + half < live, each, 0.0)

    for conv in range(2):
        wait_all(k_near[conv])
        start_all(k_wide[conv])

    def kernel_arrived(conv):
        wait_all(k_wide[conv])
        start_all(k_core[conv])
        wait_all(k_core[conv])
        if conv == 0:
            unpack_params(wk, ktp[0, 18].reshape(C, LANES))
        for unit in range(18):
            wk.kf[conv, :, unit * LANES : (unit + 1) * LANES] = ktp[conv, unit].reshape(C, LANES)
        turn_kernel(wk, conv)

    kernel_arrived(0)
    wait_all(in_test)
    forward(wk, lambda t: xt[...].astype(f32), 1, None)
    kernel_arrived(1)
    backward_two(wk, lambda t: ct[...].astype(f32), lambda t: sign, 1, tgrad)
    backward_one(wk, 1, tgrad, tgn, None)
    raw_gradient(wk, tgrad, sq)

    @pl.loop(0, 18)
    def _(k):
        t_conv[k] = tgrad[k].astype(bf16).reshape(4, 2, chans, C)

    t_gn[...] = tgn[...].astype(bf16).reshape(4, 2, chans, LANES)
    direction.start_core()

    own = dt.at[c, w, z // 2, z % 2]
    both = dt.at[c, w, :, z % 2]
    far_ag = [peer_copy(own, own, s_fin.at[0, 0], r_fin.at[0, 0], narrow=far_of(z, c))]
    near_ag = [peer_copy(both, both, s_fin.at[0, 1], r_fin.at[0, 1], narrow=near_of(z, c))]
    wide_ag = []
    for k in range(1, 4):
        to = lax.rem(w + k, 4)
        wide_ag.append(
            peer_copy(dt.at[c, w], dt.at[c, w], s_fin.at[1, k - 1], r_fin.at[1, k - 1], wide=to)
        )
    core_ag = [peer_copy(dt.at[c], dt.at[c], s_fin.at[2, 0], r_fin.at[2, 0], narrow=sibling)]

    def early_forward(e):
        if e == 0:
            direction.start_wide()

    def between(e):
        if e == 1:
            direction.start_far()
            start_all(out_block[0][A:])

    def after_raw(e):
        if e == 0:
            direction.start_near()
            start_all(out_block[0][:A])
        else:
            direction.finish(own)
            start_all(far_ag)
            start_all(out_part[0][:D])

    for e in range(examples):
        wait_all(in_x[e])

        def block_store(t, value):
            block[e, :, lane_tile(t)] = value.astype(bf16)

        def part_store(t, value):
            part[e, :, lane_tile(t)] = value.astype(bf16)

        forward(
            wk,
            lambda t: x[e, :, lane_tile(t)].astype(f32),
            8,
            block_store,
            functools.partial(early_forward, e),
        )
        wait_all(in_cot[e])
        backward_two(wk, lambda t: cot[e, :, lane_tile(t)].astype(f32), slot_weight(e), 8, raw.at[e])
        between(e)
        backward_one(wk, 8, raw.at[e], raw_gn.at[e], part_store)
        sq[...] = jnp.zeros_like(sq)
        raw_gradient(wk, raw.at[e], sq)
        gn = raw_gn[e]
        square = whole_sum(sq[...]) + whole_sum(gn * gn)
        length[e] = jnp.broadcast_to(jnp.sqrt(square), (8, LANES))
        after_raw(e)

    factors = [CLIP / jnp.maximum(length[e][0:1, 0:1], CLIP) for e in range(examples)]
    total = factors[0] * raw_gn[0]
    for e in range(1, examples):
        total = total + factors[e] * raw_gn[e]
    s_gn[...] = total.astype(bf16).reshape(4, 2, chans, LANES)

    @pl.loop(0, 18)
    def _(k):
        total = factors[0] * raw[0, k]
        for e in range(1, examples):
            total = total + factors[e] * raw[e, k]
        s_conv[k] = total.astype(bf16).reshape(4, 2, chans, C)

    clipped.start_core()
    clipped.start_wide()
    wait_all(far_ag)
    start_all(near_ag)
    start_all(out_part[0][D:])
    start_all(out_block[1][:E])
    wait_all(near_ag)
    start_all(wide_ag)
    clipped.start_near()
    start_all(out_block[1][E:])
    start_all(out_part[1][:F])
    clipped.start_far()
    start_all(out_part[1][F:G])
    clipped.finish(red.at[w])
    finals = []
    for k in range(1, 4):
        to = lax.rem(w + k, 4)
        finals.append(peer_copy(red.at[w], red.at[w], s_fin.at[3, k - 1], r_fin.at[3, k - 1], wide=to))
    start_all(finals)
    wait_all(wide_ag)
    start_all(core_ag)
    wait_all(core_ag)
    inner_products(dt, raw, raw_gn, length, figures, me, chans)
    figs = []
    for k in range(1, n):
        to = lax.rem(me + k, n)
        figs.append(peer_copy(figures.at[me], figures.at[me], s_fig.at[k - 1], r_fig.at[k - 1], narrow=to))
    start_all(figs)
    start_all(out_part[1][G:])
    wait_all(figs)
    slot = lax.broadcasted_iota(jnp.int32, (8, LANES), 1)
    table = jnp.zeros((8, LANES), f32)
    for k in range(n):
        for e in range(examples):
            table = table + jnp.where(slot == k * examples + e, figures[k, e], 0.0)
    norms[...] = table[0:1, : n * examples]
    infl[...] = table[1:2, : n * examples]
    for e in range(examples):
        wait_all(out_block[e])
        wait_all(out_part[e])
    wait_all(finals)
    gn_out[...] = red[0, 9]
    for conv in range(2):
        for tap in range(9):
            red_out[conv * 9 + tap, :, :LANES] = red[conv * 2, tap]
            red_out[conv * 9 + tap, :, LANES:] = red[conv * 2 + 1, tap]


def inner_products(dt, raw, raw_gn, length, figures, me, chans):
    examples = raw.shape[0]
    zero = jnp.zeros((chans, LANES), f32)

    def visit(index, carry):
        q, rest = index // 8, index % 8
        at = pl.ds(pl.multiple_of(rest * chans, chans), chans)
        lanes = pl.ds(pl.multiple_of((q % 2) * LANES, LANES), LANES)
        square = carry[0]
        sums = list(carry[1:])
        for tap in range(9):
            d = dt[rest % 2, q, rest // 4, (rest // 2) % 2, tap].astype(f32)
            square = square + d * d
            for e in range(examples):
                sums[e] = sums[e] + d * raw[e, (q // 2) * 9 + tap, at, lanes]
        return (square, *sums)

    totals = lax.fori_loop(0, 32, visit, (zero,) * (examples + 1), unroll=4)

    def visit_gn(rest, carry):
        at = pl.ds(pl.multiple_of(rest * chans, chans), chans)
        d = dt[rest % 2, 0, rest // 4, (rest // 2) % 2, 9].astype(f32)
        return (carry[0] + d * d,) + tuple(carry[1 + e] + d * raw_gn[e, at, :] for e in range(examples))

    totals = lax.fori_loop(0, 8, visit_gn, totals)
    dir_sq = whole_sum(totals[0])
    params = 18 * C * C + 4 * C
    top = lax.broadcasted_iota(jnp.int32, (8, LANES), 0)
    for e in range(examples):
        size = length[e]
        factor = CLIP / jnp.maximum(size, CLIP)
        influence = factor * whole_sum(totals[1 + e]) * math.sqrt(params) / (CLIP * jnp.sqrt(dir_sq + 1e-06))
        figures[me, e] = jnp.where(top == 0, size, influence)


def mega(images, cots, timg, tcot, weight, gain, pairs, alive, counts):
    held, chans = images.shape[0], images.shape[1]
    examples = held // 8
    out = jax.ShapeDtypeStruct
    anyspace = pl.BlockSpec(memory_space=pl.ANY)
    vmem = pl.BlockSpec(memory_space=pltpu.VMEM)
    smem = pl.BlockSpec(memory_space=pltpu.SMEM)
    dma = pltpu.SemaphoreType.DMA
    exchange = [
        pltpu.VMEM((18, 4, chans, C), bf16),
        pltpu.VMEM((4, chans, LANES), bf16),
        pltpu.VMEM((4, 10, 4, chans, LANES), bf16),
        pltpu.VMEM((3, 10, 4, chans, LANES), bf16),
        pltpu.VMEM((10, 2, 2, chans, LANES), bf16),
        pltpu.VMEM((10, 2, chans, LANES), bf16),
        pltpu.VMEM((10, 2, chans, LANES), bf16),
        pltpu.VMEM((10, chans, LANES), bf16),
    ]
    sems = [dma((2,)), dma((2,)), dma((3,)), dma((3,)), dma((2,)), dma((2,))]
    scratch = [
        pltpu.VMEM((examples, C, AUG * PIX), bf16),
        pltpu.VMEM((examples, C, AUG * PIX), bf16),
        pltpu.VMEM((C, LANES), bf16),
        pltpu.VMEM((C, LANES), bf16),
        pltpu.VMEM((2, UNITS, chans, LANES), bf16),
        pltpu.VMEM((2, UNITS, 2, 2, 2, chans, LANES), bf16),
        pltpu.VMEM((examples, C, AUG * PIX), bf16),
        pltpu.VMEM((examples, C, AUG * PIX), bf16),
        pltpu.VMEM((examples, 18, C, C), f32),
        pltpu.VMEM((examples, C, LANES), f32),
        pltpu.VMEM((examples, 8, LANES), f32),
        pltpu.VMEM((18, C, C), f32),
        pltpu.VMEM((C, LANES), f32),
        pltpu.VMEM((8, LANES), f32),
        pltpu.VMEM((18, 4, 2, chans, C), bf16),
        pltpu.VMEM((4, 2, chans, LANES), bf16),
        pltpu.VMEM((18, 4, 2, chans, C), bf16),
        pltpu.VMEM((4, 2, chans, LANES), bf16),
        pltpu.VMEM((2, 4, 2, 2, 10, chans, LANES), bf16),
        pltpu.VMEM((4, 10, chans, LANES), bf16),
        pltpu.VMEM((8, examples, 8, LANES), f32),
    ]
    kinds = 2 + 2 * examples
    moves = [
        dma((kinds, 7)),
        dma((kinds, 7)),
        dma((2, 3)),
        dma((2, 3)),
        dma((2, 3)),
        dma((2, 3)),
        dma((2,)),
        dma((2,)),
        dma((11,)),
        dma((2 * examples, 7)),
        dma((2 * examples, 7)),
        dma((4, 3)),
        dma((4, 3)),
        dma((7,)),
        dma((7,)),
    ]
    return pl.pallas_call(
        mega_kernel,
        out_shape=(
            out((held, chans, AUG * PIX), bf16),
            out((held, chans, AUG * PIX), bf16),
            out((18, chans, C), bf16),
            out((chans, LANES), bf16),
            out((1, held), f32),
            out((1, held), f32),
        ),
        in_specs=[anyspace] * 4 + [vmem] * 2 + [smem] * 3,
        out_specs=(anyspace, anyspace) + (vmem,) * 4,
        scratch_shapes=WORK_SCRATCH + scratch + exchange + exchange + sems + sems + moves,
        compiler_params=pltpu.CompilerParams(collective_id=0, has_side_effects=True, vmem_limit_bytes=60 << 20),
    )(images, cots, timg, tcot, weight, gain, pairs, alive, counts)


def update(weight, first, second, grad, correction, rate, decay):
    first_new = 0.5 * first + 0.5 * grad
    second_new = 0.5 * second + 0.5 * grad * grad
    step = first_new / correction / (jnp.sqrt(second_new / correction) + 1e-08)
    return weight - rate * (step + decay * weight), first_new, second_new


def tail_kernel(
    total, alive, counts, steps, ob, op, cots, red, red_gn, weight, m1, m2, noise, gw, g1, g2, gnoise, norms, infl,
    block_out, grad_out, new, low, first, second, gnew, gfirst, gsecond, norms_out, infl_out
):
    step = pl.program_id(0)
    held = ob.shape[0]
    block_out[...] = ob[...]
    image = lax.broadcasted_iota(jnp.int32, (1, AUG * PIX), 1) // PIX
    for j in range(held):
        e = step * held + j
        count = counts[e]
        live = jnp.where(e < alive[0], count, 0)
        each = 1.0 / jnp.full((1, AUG * PIX), count.astype(f32))
        row = jnp.where(image < live, each, 0.0)
        grad_out[j] = cots[j].astype(f32) * row + op[j].astype(f32)
    correction = 1.0 - jnp.exp2(jnp.full((1, 1), -steps[0].astype(f32)))
    grad = (red[...].astype(f32) + math.sqrt(total) * noise[...]) * (1.0 / total)
    value, one, two = update(weight[...], m1[...], m2[...], grad, correction, 1.0 / math.sqrt(FAN), 0.1)
    new[...] = value
    low[...] = value.astype(bf16)
    first[...] = one
    second[...] = two

    @pl.when(step == 0)
    def _():
        chans = red_gn.shape[0]
        eye = lax.broadcasted_iota(jnp.int32, (chans, chans), 0) == lax.broadcasted_iota(
            jnp.int32, (chans, chans), 1
        )
        for k in range(4):
            column = red_gn[:, k : k + 1].astype(f32)
            row = jnp.sum(jnp.where(eye, jnp.broadcast_to(column, (chans, chans)), 0.0), axis=0, keepdims=True)
            at = slice(k, k + 1)
            grad = (row + math.sqrt(total) * gnoise[at, :]) * (1.0 / total)
            value, one, two = update(gw[at, :], g1[at, :], g2[at, :], grad, correction, 0.1, 0.0)
            gnew[at, :] = value
            gfirst[at, :] = one
            gsecond[at, :] = two
        norms_out[...] = norms[...]
        infl_out[...] = infl[...]


def finish(total, alive, counts, steps, ob, op, cots, red, red_gn, conv, gn, norms, infl):
    held, chans = ob.shape[0], ob.shape[1]
    grid = GRID
    rows = 18 * chans
    smem = pl.BlockSpec(memory_space=pltpu.SMEM)
    images = pl.BlockSpec((held // grid, chans, AUG * PIX), lambda i: (i, 0, 0))
    part = pl.BlockSpec((rows // grid, C), lambda i: (i, 0))

    def whole(v):
        return pl.BlockSpec(v.shape, lambda i: (0,) * len(v.shape))

    def out(v, kind=None):
        return jax.ShapeDtypeStruct(v.shape, kind or v.dtype)

    flat = [v.transpose(0, 1, 2, 4, 3).reshape(rows, C) for v in conv]
    outs = pl.pallas_call(
        functools.partial(tail_kernel, total),
        grid=(grid,),
        out_shape=[out(ob), out(ob, f32)]
        + [out(flat[0]), out(flat[0], bf16), out(flat[0]), out(flat[0])]
        + [out(gn[0])] * 3
        + [out(norms), out(infl)],
        in_specs=[smem] * 3
        + [images] * 3
        + [part, whole(red_gn)]
        + [part] * 4
        + [whole(gn[0])] * 4
        + [whole(norms), whole(infl)],
        out_specs=[images] * 2 + [part] * 4 + [whole(gn[0])] * 3 + [whole(norms), whole(infl)],
        compiler_params=pltpu.CompilerParams(vmem_limit_bytes=62 << 20),
    )(alive, counts, steps, ob, op, cots, red.reshape(rows, C), red_gn, *flat, *gn, norms, infl)

    def back(v):
        return v.reshape(2, 3, 3, chans, C).transpose(0, 1, 2, 4, 3)

    block_out, grad_out, new, low, first, second, gnew, gfirst, gsecond, norms, infl = outs
    return (
        block_out,
        grad_out,
        norms.reshape(held),
        infl.reshape(held),
        back(new),
        back(low),
        back(first),
        back(second),
        gnew,
        gfirst,
        gsecond,
    )


def pieces(v):
    high = lax.reduce_precision(v, 8, 7)
    rest = v - high
    mid = lax.reduce_precision(rest, 8, 7)
    low = rest - mid
    return high.astype(bf16), mid.astype(bf16), low.astype(bf16)


def kernel_rows(conv_weight, gn_params):
    chans = conv_weight.shape[4]
    centre = conv_weight - jnp.mean(conv_weight, axis=(1, 2, 3), keepdims=True)
    spread = jnp.mean(centre * centre, axis=(1, 2, 3), keepdims=True)
    scale = lax.rsqrt(FAN * spread + 1e-06)
    kernels = (centre * scale).astype(bf16).reshape(2, FAN, chans)
    rows = kernels.transpose(2, 0, 1).reshape(chans, KCOLS)
    small = jnp.concatenate([gn_params.T, scale.reshape(2, chans).T, jnp.zeros((chans, 2), f32)], 1)
    tail = jnp.concatenate(list(pieces(small)) + [jnp.zeros((chans, LANES - 24), bf16)], 1)
    return jnp.concatenate([rows, tail], 1)


def plain_gather(images, cots, timg, tcot, kshard, narrow):
    share = narrow // 8
    x = lax.all_to_all(images, "narrow", 0, 1, tiled=True)
    cot = lax.all_to_all(cots, "narrow", 0, 1, tiled=True)
    ktp = lax.all_gather(kshard, "narrow", axis=0, tiled=True)
    own = (lax.axis_index("narrow") // share) * LANES

    def pick(v):
        return lax.dynamic_slice_in_dim(lax.all_gather(v, "narrow", axis=0, tiled=True), own, LANES, 1)

    return x, cot, pick(timg), pick(tcot), ktp


def plain_reduce(block, part, clip_conv, test_conv, clip_gn, test_gn, raw, raw_gn, length, chans):
    examples = block.shape[0]
    ob = lax.all_to_all(block, "narrow", 1, 0, tiled=True)
    op = lax.all_to_all(part, "narrow", 1, 0, tiled=True)
    own = lax.axis_index("narrow") * chans
    rows = lax.psum(clip_conv, ("wide", "narrow"))
    rows = lax.dynamic_slice_in_dim(rows, own, chans, 1)
    gn_rows = lax.dynamic_slice_in_dim(lax.psum(clip_gn.astype(bf16), ("wide", "narrow")), own, chans, 0)
    d = lax.psum(test_conv, ("wide", "narrow")).astype(f32)
    d_gn = lax.psum(test_gn.astype(bf16), ("wide", "narrow")).astype(f32)
    dir_sq = jnp.sum(d * d) + jnp.sum(d_gn * d_gn)
    inner = jnp.sum(raw * d, axis=(1, 2, 3)) + jnp.sum(raw_gn * d_gn, axis=(1, 2))
    size = length[:, 0, 0]
    factor = CLIP / jnp.maximum(size, CLIP)
    influence = factor * inner * math.sqrt(18 * C * C + 4 * C) / (CLIP * jnp.sqrt(dir_sq + 1e-06))
    figures = lax.all_gather(jnp.stack([size, influence], 1), "narrow", axis=0)
    return ob, op, rows, gn_rows, figures[:, :, 0], figures[:, :, 1]


def local(
    images,
    cotangent,
    test_images,
    test_cotangent,
    pair_index,
    example_count,
    aug_count,
    conv_weight,
    gn_params,
    conv_moment1,
    conv_moment2,
    gn_moment1,
    gn_moment2,
    noise_conv,
    noise_gn,
    step_count,
):
    n_wide, narrow = lax.axis_size("wide"), lax.axis_size("narrow")
    held, chans = images.shape[0], images.shape[1]
    examples = held // narrow
    share = narrow // 8
    me = lax.axis_index("narrow")
    timg, tcot = test_images[0], test_cotangent[0]
    if n_wide == 4 and narrow == 8:
        weight = conv_weight.transpose(0, 1, 2, 4, 3).reshape(18, chans, C)
        outs = mega(
            images, cotangent, timg, tcot, weight, gn_params, pair_index.T, example_count, aug_count
        )
    else:
        slots = jnp.arange(AUG, dtype=jnp.int32)
        live = jnp.arange(held, dtype=jnp.int32) < example_count[0]
        weights = jnp.where(
            live[:, None] & (slots[None, :] < aug_count[:, None]),
            1.0 / aug_count.astype(f32)[:, None],
            f32(0.0),
        )
        pixels = jnp.repeat(weights, PIX, axis=1)
        pairs = pair_index % AUG
        signs = jnp.sum((pairs[:, 0:1] == slots[None, :]).astype(f32), 0) - jnp.sum(
            (pairs[:, 1:2] == slots[None, :]).astype(f32), 0
        )
        sign_pixels = jnp.repeat(signs, PIX).reshape(8, LANES) * (1.0 / share)
        kshard = kernel_rows(conv_weight, gn_params)
        wl = lax.dynamic_slice_in_dim(pixels, me * examples, examples, 0)[:, None, :]
        sg = lax.dynamic_slice_in_dim(sign_pixels, me // share, 1, 0)
        x, cot, xt, ct, ktp = plain_gather(images, cotangent, timg, tcot, kshard, narrow)
        parts = compute(x, cot, xt, ct, ktp, wl, sg)
        outs = plain_reduce(*parts, chans)
    block_out, op, red, red_gn, lengths, influence = outs
    return finish(
        held * n_wide,
        example_count,
        aug_count,
        step_count,
        block_out,
        op,
        cotangent,
        red,
        red_gn,
        (conv_weight, conv_moment1, conv_moment2, noise_conv),
        (gn_params, gn_moment1, gn_moment2, noise_gn),
        lengths.reshape(1, held),
        influence.reshape(1, held),
    )


def solution(mesh):
    in_specs = (
        P("wide", "narrow", None),
        P("wide", "narrow", None),
        P("wide", "narrow", None),
        P("wide", "narrow", None),
        P("wide", None),
        P("wide"),
        P("wide"),
        P(None, None, None, None, "narrow"),
        P(None, "narrow"),
        P(None, None, None, None, "narrow"),
        P(None, None, None, None, "narrow"),
        P(None, "narrow"),
        P(None, "narrow"),
        P(None, None, None, None, "narrow"),
        P(None, "narrow"),
        P(),
    )
    out_specs = (
        P("wide", "narrow", None),
        P("wide", "narrow", None),
        P("wide"),
        P("wide"),
        P(None, None, None, None, "narrow"),
        P(None, None, None, None, "narrow"),
        P(None, None, None, None, "narrow"),
        P(None, None, None, None, "narrow"),
        P(None, "narrow"),
        P(None, "narrow"),
        P(None, "narrow"),
    )
    return jax.shard_map(local, mesh=mesh, in_specs=in_specs, out_specs=out_specs, check_vma=False)
```
